32 devices in a mesh: slab: 2 (over y), pulse: 4 (over z), rx: 2 (over x), rng: 2 (over core).
Axes of the slice: x: 2, y: 2, z: 4, core: 2. Of those that a mesh axis runs over, the one named last changes fastest.
Arguments:
- echoes: bfloat16 [2, 64, 16, 4096], P(None, ('slab', 'pulse'), 'rx', 'rng'), parts along dimension 1, may hold values from -6 to 6
- beam_angle: int32 [64], replicated, may hold values from 0 to 1023
- interp_table: int32 [32, 2, 64], replicated, may hold values from 0 to 11
Outputs:
- focused: float32 [2, 128, 4096], P(None, 'slab', ('rng', 'rx', 'pulse')), parts along dimension 1
The draws below stay inside these ranges and needn't reach their ends.
There are 2 independent parts, one for each index of `slab`. The reference program is written for one: setup_inputs(seed, part) draws one part's arguments, and reference() takes and returns one part's arrays. A program takes and returns all parts, laid end to end along the dimension named above; an argument that names none is the same for every part. Nothing has to cross between parts.
All inputs are finite; a program needn't handle non-finite values.
Results may differ from the reference program's by a relative error of at most 0.0059.
Values may be sent and summed in bfloat16 or wider, within the bound.
A program may use at most 64 MiB of HBM per device.

```python
import math
import jax
import jax.numpy as jnp
from jax import lax

BEAMS = 64
RXS = 16
RTAPS = 64
CTAPS = 512
P_DEV = 8
R_DEV = 2048
PULSES = 32
R = 4096
N_RNG = 2


def place_ends(result, rng, low, top_value):
    longest = result.shape.index(max(result.shape))
    spots = []
    for shift in (0, 1):
        where = [jax.random.randint(jax.random.fold_in(rng, axis), (), 0, length) for axis, length in enumerate(result.shape)]
        where[longest] = (where[longest] + shift) % result.shape[longest]
        spots.append(tuple(where))
    return result.at[spots[0]].set(low).at[spots[1]].set(top_value)


def steps_of(own_key, dims, split, least, high):
    factor_of = 1.0
    for dim, parts in split:
        heights = jax.random.uniform(jax.random.fold_in(jax.random.fold_in(own_key, 6), dim), (parts,), jnp.float32, least / len(split), high / len(split))
        factor_of = factor_of * jnp.repeat(jnp.exp(heights), dims[dim] // parts).reshape((-1,) + (1,) * (len(dims) - 1 - dim))
    return factor_of


def noise(own_key, shape, deviation, reach, shards=(), kind=jnp.bfloat16):
    gain = steps_of(own_key, shape, shards, -0.22, 0.18) if shards else 1.0
    drawn = jax.random.normal(own_key, shape, jnp.float32) * deviation * gain
    return jnp.minimum(jnp.maximum(drawn, -reach), reach).astype(kind)


def setup_inputs(seed: int = 0, part: int = 0) -> dict:
    splits = jax.random.split(jax.random.key(seed), 4)
    own_keys = jax.random.split(jax.random.fold_in(splits[3], part), 4)
    return {
        "echoes": noise(own_keys[0], (2, PULSES, RXS, R), 1.0, 6.0, ((1, 4), (2, 2), (3, 2))),
        "beam_angle": place_ends(jax.random.randint(splits[1], (BEAMS,), 0, 1024), jax.random.fold_in(splits[1], 1), 0, 1023).astype(jnp.int32),
        "interp_table": place_ends(jax.random.randint(splits[2], (PULSES, 2, BEAMS), 0, 12), jax.random.fold_in(splits[2], 1), 0, 11).astype(jnp.int32),
    }


half_root = 0.7071067811865476
full_turn = 2.0 * math.pi

def receiver_taps(channel_ids, tap_count):
    tap_index = jnp.arange(tap_count, dtype=jnp.float32)
    window = 0.5 - 0.5 * jnp.cos(full_turn * (tap_index + 0.5) / tap_count)
    window = window / jnp.sqrt(jnp.sum(window * window))
    channel = channel_ids.astype(jnp.float32)[:, None] + 1.0
    angle = full_turn * channel * (tap_index - tap_count // 2) / (4 * tap_count)
    return ((window * jnp.cos(angle)).astype(jnp.bfloat16), (window * jnp.sin(angle)).astype(jnp.bfloat16))

def chirp_taps(tap_count):
    offset = jnp.arange(tap_count, dtype=jnp.int32) - tap_count // 2
    phase_step = jnp.mod(offset * offset, 2 * tap_count).astype(jnp.float32)
    angle = math.pi * phase_step / tap_count
    scale = 1.0 / math.sqrt(tap_count)
    return ((jnp.cos(angle) * scale).astype(jnp.bfloat16), (-jnp.sin(angle) * scale).astype(jnp.bfloat16))

def steering(beam_angle, receivers):
    channel = jnp.arange(receivers, dtype=jnp.int32)
    turns = jnp.mod(beam_angle[:, None] * channel[None, :], 1024).astype(jnp.float32)
    angle = full_turn * turns / 1024.0
    scale = 1.0 / math.sqrt(receivers)
    return ((jnp.cos(angle) * scale).astype(jnp.bfloat16), (-jnp.sin(angle) * scale).astype(jnp.bfloat16))

def interp_matrices(codes, beam_count):
    shifted = codes // 4 - 1
    fraction = jnp.mod(codes, 4).astype(jnp.float32) / 4.0
    weights = (-fraction * (fraction - 1.0) * (fraction - 2.0) / 6.0, (fraction + 1.0) * (fraction - 1.0) * (fraction - 2.0) / 2.0, -(fraction + 1.0) * fraction * (fraction - 2.0) / 2.0, (fraction + 1.0) * fraction * (fraction - 1.0) / 6.0)
    columns = jnp.arange(beam_count, dtype=jnp.int32)
    matrices = jnp.zeros(codes.shape + (beam_count,), jnp.float32)
    for tap_index in range(4):
        target = jnp.mod(columns + shifted + tap_index - 1, beam_count)
        matrices = matrices + weights[tap_index][..., None] * (target[..., None] == columns).astype(jnp.float32)
    return matrices

def phases(node_ids, positions, beam_angle, side):
    base = jnp.mod(beam_angle[:, None] * (positions[None, :] + 1), 1024)
    factor = 2 * node_ids + side + 1
    turns = jnp.mod(base[:, None, :] * factor[None, :, None], 1024).astype(jnp.float32)
    angle = full_turn * turns / 1024.0
    return (jnp.cos(angle), jnp.sin(angle))

def side_term(picture, matrices, cosine, sine):
    moved = jnp.einsum('gqa,cagr->cqgr', matrices, picture, precision=lax.Precision.HIGHEST)
    return (cosine * moved[0] - sine * moved[1], sine * moved[0] + cosine * moved[1])

def merge_pair(left_image, right_image, node_ids, positions, beam_angle, interp_table):
    matrices = interp_matrices(interp_table[node_ids], left_image.shape[1])
    left_cos, left_sin = phases(node_ids, positions, beam_angle, 0)
    right_cos, right_sin = phases(node_ids, positions, beam_angle, 1)
    left_re, left_im = side_term(left_image, matrices[:, 0], left_cos, left_sin)
    right_re, right_im = side_term(right_image, matrices[:, 1], right_cos, right_sin)
    return jnp.stack([(left_re + right_re) * half_root, (left_im + right_im) * half_root])

def correlate(signal_re, signal_im, taps_re, taps_im):
    tap_count = taps_re.shape[-1]
    length = signal_re.shape[-1]
    total = length + tap_count
    signal = signal_re + 1j * signal_im
    kernel = (taps_re + 1j * taps_im)[..., ::-1]
    product = jnp.fft.ifft(jnp.fft.fft(signal, total) * jnp.fft.fft(kernel, total))
    start = tap_count // 2 - 1
    window = product[..., start:start + length]
    return (jnp.real(window), jnp.imag(window))

def settle(values):
    return lax.optimization_barrier(values.astype(jnp.bfloat16)).astype(jnp.float32)

def reference(echoes, beam_angle, interp_table):
    group_count = PULSES // P_DEV
    length = R_DEV * N_RNG
    rx_re, rx_im = receiver_taps(jnp.arange(RXS, dtype=jnp.int32), RTAPS)
    rx_re = rx_re.astype(jnp.float32)
    rx_im = rx_im.astype(jnp.float32)
    chirp_re, chirp_im = chirp_taps(CTAPS)
    chirp_re = chirp_re.astype(jnp.float32)
    chirp_im = chirp_im.astype(jnp.float32)
    steering_real, steering_imaginary = steering(beam_angle, RXS)
    steering_real = steering_real.astype(jnp.float32)
    steering_imaginary = steering_imaginary.astype(jnp.float32)
    positions = jnp.arange(length, dtype=jnp.int32)
    grouped = jnp.moveaxis(echoes.reshape(2, group_count, P_DEV, RXS, length), 1, 0)
    local_levels = P_DEV.bit_length() - 1
    highest_precision = lax.Precision.HIGHEST

    def one_group(packed):
        block, group_index = packed
        filtered_re, filtered_im = correlate(block[0].astype(jnp.float32), block[1].astype(jnp.float32), rx_re, rx_im)
        filtered_re = settle(filtered_re)
        filtered_im = settle(filtered_im)
        compressed_real_part, compressed_imaginary_part = correlate(filtered_re, filtered_im, chirp_re, chirp_im)
        compressed_real_part = settle(compressed_real_part)
        compressed_imaginary_part = settle(compressed_imaginary_part)
        beam_output_real = jnp.einsum('lx,yxd->lyd', steering_real, compressed_real_part, precision=highest_precision) - jnp.einsum('lx,yxd->lyd', steering_imaginary, compressed_imaginary_part, precision=highest_precision)
        beam_output_imaginary = jnp.einsum('lx,yxd->lyd', steering_imaginary, compressed_real_part, precision=highest_precision) + jnp.einsum('lx,yxd->lyd', steering_real, compressed_imaginary_part, precision=highest_precision)
        picture = jnp.stack([beam_output_real, beam_output_imaginary])
        for level in range(local_levels):
            groups_now = P_DEV >> level + 1
            node_ids = (group_count + group_index) * groups_now + jnp.arange(groups_now, dtype=jnp.int32)
            paired = picture.reshape(2, BEAMS, groups_now, 2, length)
            picture = merge_pair(paired[:, :, :, 0], paired[:, :, :, 1], node_ids, positions, beam_angle, interp_table)
        return picture[:, :, 0]
    pictures = lax.map(one_group, (grouped, jnp.arange(group_count, dtype=jnp.int32)))
    picture = jnp.moveaxis(pictures, 0, 2)
    for level in range(group_count.bit_length() - 1):
        groups_now = group_count >> level + 1
        node_ids = groups_now + jnp.arange(groups_now, dtype=jnp.int32)
        paired = picture.reshape(2, BEAMS, groups_now, 2, length)
        picture = merge_pair(paired[:, :, :, 0], paired[:, :, :, 1], node_ids, positions, beam_angle, interp_table)
    return picture[:, :, 0]
```

```python
import functools
import math

import jax
import ml_dtypes
import jax.numpy as jnp
import numpy as np
from jax import lax
from jax.experimental import pallas as pl
from jax.experimental.pallas import tpu as pltpu
from jax.sharding import PartitionSpec as P

RTAPS = 64
CTAPS = 512


half_root = 0.7071067811865476
full_turn = 2.0 * math.pi
SPAN = 256
EDGE = 384
MESH = pl.DeviceIdType.MESH


def extended_2(block, sides, width):
    for axis, dim in sides:
        count = lax.axis_size(axis)
        forward = [(i, i + 1) for i in range(count - 1)]
        backward = [(target, source) for source, target in forward]
        low = lax.ppermute(
            lax.slice_in_dim(block, block.shape[dim] - width, None, axis=dim), axis, forward
        )
        high = lax.ppermute(lax.slice_in_dim(block, 0, width, axis=dim), axis, backward)
        block = jnp.concatenate([low, block, high], axis=dim)
    return block


def swapped(x, axis, distance):
    return lax.ppermute(x, axis, [(i, i ^ 1 << distance) for i in range(lax.axis_size(axis))])


def receiver_taps(channel_ids, tap_count):
    tap_index = jnp.arange(tap_count, dtype=jnp.float32)
    window = 0.5 - 0.5 * jnp.cos(full_turn * (tap_index + 0.5) / tap_count)
    window = window / jnp.sqrt(jnp.sum(window * window))
    channel = channel_ids.astype(jnp.float32)[:, None] + 1.0
    angle = full_turn * channel * (tap_index - tap_count // 2) / (4 * tap_count)
    return (
        (window * jnp.cos(angle)).astype(jnp.bfloat16),
        (window * jnp.sin(angle)).astype(jnp.bfloat16),
    )


def chirp_taps(tap_count):
    offset = jnp.arange(tap_count, dtype=jnp.int32) - tap_count // 2
    phase_step = jnp.mod(offset * offset, 2 * tap_count).astype(jnp.float32)
    angle = math.pi * phase_step / tap_count
    scale = 1.0 / math.sqrt(tap_count)
    return (
        (jnp.cos(angle) * scale).astype(jnp.bfloat16),
        (-jnp.sin(angle) * scale).astype(jnp.bfloat16),
    )


def steering(beam_angle, receivers):
    channel = jnp.arange(receivers, dtype=jnp.int32)
    turns = jnp.mod(beam_angle[:, None] * channel[None, :], 1024).astype(jnp.float32)
    angle = full_turn * turns / 1024.0
    scale = 1.0 / math.sqrt(receivers)
    return (
        (jnp.cos(angle) * scale).astype(jnp.bfloat16),
        (-jnp.sin(angle) * scale).astype(jnp.bfloat16),
    )


def interp_matrices(codes, beam_count):
    shifted = codes // 4 - 1
    fraction = jnp.mod(codes, 4).astype(jnp.float32) / 4.0
    weights = (
        -fraction * (fraction - 1.0) * (fraction - 2.0) / 6.0,
        (fraction + 1.0) * (fraction - 1.0) * (fraction - 2.0) / 2.0,
        -(fraction + 1.0) * fraction * (fraction - 2.0) / 2.0,
        (fraction + 1.0) * fraction * (fraction - 1.0) / 6.0,
    )
    columns = jnp.arange(beam_count, dtype=jnp.int32)
    matrices = jnp.zeros(codes.shape + (beam_count,), jnp.float32)
    for tap_index in range(4):
        target = jnp.mod(columns + shifted + tap_index - 1, beam_count)
        matrices = matrices + weights[tap_index][..., None] * (target[..., None] == columns).astype(
            jnp.float32
        )
    return matrices


def phases(node_ids, positions, beam_angle, side):
    base = jnp.mod(beam_angle[:, None] * (positions[None, :] + 1), 1024)
    factor = 2 * node_ids + side + 1
    turns = jnp.mod(base[:, None, :] * factor[None, :, None], 1024).astype(jnp.float32)
    angle = full_turn * turns / 1024.0
    return (jnp.cos(angle), jnp.sin(angle))


def side_term(picture, matrices, cosine, sine):
    moved = jnp.einsum("gqa,cagr->cqgr", matrices, picture, precision=lax.Precision.HIGHEST)
    return (cosine * moved[0] - sine * moved[1], sine * moved[0] + cosine * moved[1])


def merge_pair(left_image, right_image, node_ids, positions, beam_angle, interp_table):
    matrices = interp_matrices(
        lax.dynamic_slice_in_dim(interp_table, node_ids[0], node_ids.shape[0]), left_image.shape[1]
    )
    left_cos, left_sin = phases(node_ids, positions, beam_angle, 0)
    right_cos, right_sin = phases(node_ids, positions, beam_angle, 1)
    left_re, left_im = side_term(left_image, matrices[:, 0], left_cos, left_sin)
    right_re, right_im = side_term(right_image, matrices[:, 1], right_cos, right_sin)
    return jnp.stack([(left_re + right_re) * half_root, (left_im + right_im) * half_root])


def toeplitz_blocks(taps_re, taps_im):
    tap_count = taps_re.shape[-1]
    leading = taps_re.shape[:-1]

    def lay_out(taps):
        padded = jnp.concatenate([taps, jnp.zeros(leading + (tap_count + 1,), taps.dtype)], axis=-1)
        tiled = jnp.tile(padded, (1,) * len(leading) + (tap_count,))
        banded = tiled[..., : 2 * tap_count * tap_count].reshape(
            leading + (tap_count, 2 * tap_count)
        )
        return jnp.swapaxes(banded, -1, -2)

    real_band = lay_out(taps_re)
    imag_band = lay_out(taps_im)
    upper = jnp.concatenate([real_band, imag_band], axis=-1)
    lower = jnp.concatenate([-imag_band, real_band], axis=-1)
    return jnp.concatenate([upper, lower], axis=-2)


def block_filter(extended, matrices, tap_count, per_channel):
    pulses, channels, length = extended.shape[1:]
    blocks = length // tap_count - 1
    pieces = extended.reshape(2, pulses, channels, blocks + 1, tap_count)
    windows = jnp.concatenate([pieces[:, :, :, :-1], pieces[:, :, :, 1:]], axis=4)
    windows = jnp.transpose(windows, (1, 2, 3, 0, 4)).reshape(
        pulses, channels, blocks, 4 * tap_count
    )
    if per_channel:
        output = jnp.einsum("pcnw,cwo->pcno", windows, matrices, preferred_element_type=jnp.float32)
    else:
        output = jnp.einsum("pcnw,wo->pcno", windows, matrices, preferred_element_type=jnp.float32)
    output = output.reshape(pulses, channels, blocks, 2, tap_count)
    return jnp.transpose(output, (3, 0, 1, 2, 4)).reshape(2, pulses, channels, blocks * tap_count)


def local(echoes, beam_angle, interp_table):
    rx_count = lax.axis_size("rx")
    pulse_count = lax.axis_size("pulse")
    rng_place = lax.axis_index("rng")
    rx_place = lax.axis_index("rx")
    pulse_place = lax.axis_index("pulse")
    pulses, channels, length = echoes.shape[1:]
    beam_count = beam_angle.shape[0]
    receivers = channels * rx_count
    channel_ids = rx_place * channels + jnp.arange(channels, dtype=jnp.int32)
    rx_re, rx_im = receiver_taps(channel_ids, RTAPS)
    rx_bands = toeplitz_blocks(rx_re, rx_im)
    chirp_re, chirp_im = chirp_taps(CTAPS)
    chirp_band = toeplitz_blocks(chirp_re, chirp_im)
    extended = extended_2(echoes, (("rng", 3),), RTAPS // 2)
    filtered = block_filter(extended, rx_bands, RTAPS, True).astype(jnp.bfloat16)
    filtered = extended_2(filtered, (("rng", 3),), CTAPS // 2)
    compressed = block_filter(filtered, chirp_band, CTAPS, False).astype(jnp.bfloat16)
    steering_real, steering_imaginary = steering(beam_angle, receivers)
    steer_matrix = jnp.concatenate(
        [
            jnp.concatenate([steering_real, -steering_imaginary], axis=1),
            jnp.concatenate([steering_imaginary, steering_real], axis=1),
        ],
        axis=0,
    )
    arrived = lax.all_to_all(compressed, "rx", split_axis=3, concat_axis=2, tiled=True)
    item_count, recv_count, owned_cols = arrived.shape[1:]
    stacked = jnp.transpose(arrived, (0, 2, 1, 3)).reshape(2 * recv_count, item_count * owned_cols)
    formed = jnp.dot(steer_matrix, stacked, preferred_element_type=jnp.float32)
    picture = formed.reshape(2, beam_count, item_count, owned_cols)
    owned_width = length // rx_count
    positions = (
        rng_place * length + rx_place * owned_width + jnp.arange(owned_width, dtype=jnp.int32)
    )
    for level in range(pulses.bit_length() - 1):
        groups_now = pulses >> level + 1
        node_ids = (pulse_count + pulse_place) * groups_now + jnp.arange(
            groups_now, dtype=jnp.int32
        )
        paired = picture.reshape(2, beam_count, groups_now, 2, owned_width)
        picture = merge_pair(
            paired[:, :, :, 0], paired[:, :, :, 1], node_ids, positions, beam_angle, interp_table
        )
    picture = picture[:, :, 0]
    cross_levels = pulse_count.bit_length() - 1
    piece_width = owned_width // pulse_count
    pieces = picture.reshape(2, beam_count, pulse_count, piece_width)
    spots = positions.reshape(pulse_count, piece_width)
    for level in range(cross_levels):
        parity = jnp.right_shift(pulse_place, level) & 1
        count_now = pieces.shape[2]
        paired = pieces.reshape(2, beam_count, count_now // 2, 2, piece_width)
        kept_half = lax.dynamic_index_in_dim(paired, parity, 3, keepdims=False)
        sent_half = lax.dynamic_index_in_dim(paired, 1 - parity, 3, keepdims=False)
        partner = swapped(sent_half, "pulse", level)
        spot_pairs = spots.reshape(count_now // 2, 2, piece_width)
        spots = lax.dynamic_index_in_dim(spot_pairs, parity, 1, keepdims=False)
        own_part = kept_half.reshape(2, beam_count, -1)
        other_part = partner.reshape(2, beam_count, -1)
        left_image = jnp.where(parity == 0, own_part, other_part)
        right_image = jnp.where(parity == 0, other_part, own_part)
        combine_node_ids = jnp.reshape(
            (pulse_count >> level + 1) + jnp.right_shift(pulse_place, level + 1), (1,)
        )
        merged = merge_pair(
            left_image[:, :, None],
            right_image[:, :, None],
            combine_node_ids,
            spots.reshape(-1),
            beam_angle,
            interp_table,
        )
        flat = merged[:, :, 0]
        pieces = flat.reshape(2, beam_count, count_now // 2, piece_width)
    picture = pieces.reshape(2, beam_count, piece_width)
    return picture


def receiver_bands(receivers):
    t = np.arange(RTAPS, dtype=np.float64)
    window = 0.5 - 0.5 * np.cos(full_turn * (t + 0.5) / RTAPS)
    window = window / np.sqrt(np.sum(window * window))
    angle = full_turn * np.arange(1, receivers + 1)[:, None] * (t - RTAPS // 2) / (4 * RTAPS)
    lag = np.arange(3 * 128)[:, None] - np.arange(128)[None, :] - (128 - RTAPS // 2)
    return banded(window * np.cos(angle), window * np.sin(angle), lag, RTAPS, 3 * 128)


def chirp_bands():
    t = np.arange(CTAPS) - CTAPS // 2
    angle = math.pi * ((t * t) % (2 * CTAPS)) / CTAPS
    scale = 1.0 / math.sqrt(CTAPS)
    lag = np.arange(CTAPS + 128)[:, None] - np.arange(128)[None, :]
    return banded(np.cos(angle)[None] * scale, -np.sin(angle)[None] * scale, lag, CTAPS, 128)[0]


def banded(taps_re, taps_im, lag, count, group):
    inside = (lag >= 0) & (lag < count)
    spot = np.clip(lag, 0, count - 1)
    re = np.where(inside, taps_re[:, spot], 0.0)
    im = np.where(inside, taps_im[:, spot], 0.0)
    channels, rows, cols = re.shape
    upper = np.concatenate([re, im], axis=2).reshape(channels, rows // group, 1, group, 2 * cols)
    lower = np.concatenate([-im, re], axis=2).reshape(channels, rows // group, 1, group, 2 * cols)
    both = np.concatenate([upper, lower], axis=2)
    return both.reshape(channels, 2 * rows, 2 * cols).astype(np.float32).astype(ml_dtypes.bfloat16)


def turn(k, scale):
    shifted = k + 128
    quadrant = jnp.bitwise_and(jnp.right_shift(shifted, 8), 3)
    y = (jnp.bitwise_and(shifted, 255) - 128).astype(jnp.float32) * (full_turn / 1024.0)
    z = y * y
    sine = y * (1.0 + z * (-1 / 6 + z * (1 / 120 + z * (-1 / 5040 + z * (1 / 362880)))))
    cosine = 1.0 + z * (-0.5 + z * (1 / 24 + z * (-1 / 720 + z * (1 / 40320))))
    odd = jnp.bitwise_and(quadrant, 1) == 1
    c = jnp.where(odd, sine, cosine)
    s = jnp.where(odd, cosine, sine)
    c = jnp.where(jnp.bitwise_and(quadrant + 1, 2) == 2, -c, c)
    s = jnp.where(quadrant >= 2, -s, s)
    return c * scale, s * scale


def upright(row, size):
    across = lax.broadcasted_iota(jnp.int32, (size, size), 1)
    down = lax.broadcasted_iota(jnp.int32, (size, size), 0)
    spread = jnp.where(across == down, jnp.broadcast_to(row.astype(jnp.float32), (size, size)), 0.0)
    return jnp.sum(spread, axis=1, keepdims=True)


def interp_matrix(row, size):
    codes = upright(row, size).astype(jnp.int32)
    shift = jnp.right_shift(codes, 2) - 1
    f = jnp.bitwise_and(codes, 3).astype(jnp.float32) * 0.25
    weights = (
        -f * (f - 1.0) * (f - 2.0) * (1 / 6),
        (f + 1.0) * (f - 1.0) * (f - 2.0) * 0.5,
        -(f + 1.0) * f * (f - 2.0) * 0.5,
        (f + 1.0) * f * (f - 1.0) * (1 / 6),
    )
    across = lax.broadcasted_iota(jnp.int32, (size, size), 1)
    down = lax.broadcasted_iota(jnp.int32, (size, size), 0)
    gap = jnp.bitwise_and(across - down - shift + 1, size - 1)
    out = jnp.zeros((size, size), jnp.float32)
    for k in range(4):
        out = jnp.where(gap == k, weights[k], out)
    return out.astype(jnp.bfloat16)


def focus_kernel(
    pulse_count, ech, ang_hbm, tab_hbm, trx_hbm, chp_hbm, out,
    ang, tab, held, edge, turned, filt, trx, chp, phase, form, first, second, last,
    offered, both, sent, got,
    near_sem, halo_sem, offer_send, offer_recv, piece_send, piece_recv,
):
    rx, rng, me = lax.axis_index("rx"), lax.axis_index("rng"), lax.axis_index("pulse")
    beams = ang.shape[1]
    pulses, channels, length = ech.shape[1:]
    owned = length // 2
    barrier = pltpu.get_barrier_semaphore()
    pl.semaphore_signal(barrier, inc=1, device_id={"rx": 1 - rx}, device_id_type=MESH)
    pl.semaphore_signal(barrier, inc=1, device_id={"rng": 1 - rng}, device_id_type=MESH)
    for step in range(1, pulse_count):
        pl.semaphore_signal(
            barrier, inc=1, device_id={"pulse": lax.rem(me + step, pulse_count)}, device_id_type=MESH
        )

    tables = [
        pltpu.make_async_copy(ang_hbm, ang, near_sem.at[0]),
        pltpu.make_async_copy(tab_hbm, tab, near_sem.at[1]),
    ]
    near = [
        pltpu.make_async_copy(ech, held, near_sem.at[2]),
        pltpu.make_async_copy(
            trx_hbm.at[pl.ds(rx * channels, channels)], trx, near_sem.at[3]
        ),
        pltpu.make_async_copy(chp_hbm, chp, near_sem.at[4]),
    ]
    for copy in tables + near:
        copy.start()

    blocks = length // 128

    @pl.when(rng == 0)
    def _():
        turned[:, :, :, :EDGE] = jnp.zeros(turned.shape[:3] + (EDGE,), turned.dtype)
        filt[:, :512] = jnp.zeros((filt.shape[0], 512), filt.dtype)

    @pl.when(rng == 1)
    def _():
        turned[:, :, :, EDGE + length :] = jnp.zeros(turned.shape[:3] + (EDGE,), turned.dtype)
        filt[:, 512 + 2 * length :] = jnp.zeros((filt.shape[0], 512), filt.dtype)

    def filter_blocks(start, count):
        def pair(i, carry):
            results = []
            for odd in range(2):
                c = 2 * i + odd
                left = jnp.concatenate(
                    [
                        jnp.concatenate(
                            [
                                turned[part, c, :, pl.ds(pl.multiple_of(128 * (start + j), 128), 384)]
                                for part in range(2)
                            ],
                            axis=1,
                        )
                        for j in range(count)
                    ],
                    axis=0,
                ).astype(jnp.bfloat16)
                results.append(jnp.dot(left, trx[c], preferred_element_type=jnp.float32))
            row = pl.multiple_of(2 * i * pulses, 2 * pulses)
            for j in range(count):
                filt[pl.ds(row, 2 * pulses), pl.ds(pl.multiple_of(256 * (start + j), 256), 256)] = (
                    jnp.concatenate([r[8 * j : 8 * j + 8] for r in results], axis=0).astype(jnp.bfloat16)
                )
            return carry

        lax.fori_loop(0, channels // 2, pair, 0)

    for copy in tables:
        copy.wait()
    angle = upright(ang[...], beams).astype(jnp.int32)
    base = [pulse_count * (pulses >> k) + (pulses >> k) * me for k in range(3)]
    rows = [base[k] + i for k in range(3) for i in range(pulses >> k)]
    rows += [(pulse_count >> k) + jnp.right_shift(me, k) for k in range(2)]

    wide = (beams, 2 * 2 * channels * pulses)
    column = lax.broadcasted_iota(jnp.int32, wide, 1)
    local_channel = jnp.bitwise_and(jnp.right_shift(column, 3), channels - 1)
    receiver = local_channel + channels * jnp.right_shift(column, 7)
    cosine, sine = turn(jnp.bitwise_and(angle * receiver, 1023), 0.25)
    imag = jnp.bitwise_and(jnp.right_shift(column, 6), 1) == 1
    steer = [
        jnp.where(imag, sine, cosine).astype(jnp.bfloat16),
        jnp.where(imag, cosine, -sine).astype(jnp.bfloat16),
    ]
    lane_pulse = jnp.bitwise_and(column, pulses - 1)
    for p in range(pulses):
        matrix = interp_matrix(tab[pl.ds(rows[p], 1), :], beams)
        for part in range(2):
            mixed = jnp.dot(matrix, steer[part], preferred_element_type=jnp.float32)
            spot = (2 * p + part) * beams
            form[spot : spot + beams, :] = jnp.where(lane_pulse == p, mixed, 0.0).astype(jnp.bfloat16)
    empty = jnp.zeros((beams, beams), jnp.bfloat16)
    for i in range(4):
        row = [empty] * 4
        row[i] = interp_matrix(tab[pl.ds(rows[8 + i], 1), :], beams)
        first[i * beams : (i + 1) * beams, :] = jnp.concatenate(row, axis=1)
    for i in range(2):
        row = [empty] * 2
        row[i] = interp_matrix(tab[pl.ds(rows[12 + i], 1), :], beams)
        second[i * beams : (i + 1) * beams, :] = jnp.concatenate(row, axis=1)
        last[i] = interp_matrix(tab[pl.ds(rows[14 + i], 1), :], beams)

    near[0].wait()
    for part in range(2):
        for spot in range(0, length, SPAN):
            block = held[part, :, :, spot : spot + SPAN].astype(jnp.float32)
            turned[part, :, :, EDGE + spot : EDGE + spot + SPAN] = jnp.swapaxes(block, 0, 1)
    near[1].wait()
    near[2].wait()
    filter_blocks(2 + rng, blocks - 1)

    pl.semaphore_wait(barrier, 1 + pulse_count)
    halo = pltpu.make_async_remote_copy(
        src_ref=ech.at[:, :, :, pl.ds(pl.multiple_of((1 - rng) * (length - EDGE), 128), EDGE)],
        dst_ref=edge,
        send_sem=halo_sem.at[0],
        recv_sem=halo_sem.at[1],
        device_id={"rng": 1 - rng},
        device_id_type=MESH,
    )
    halo.start()

    def target_of(i):
        first_turn = lax.div(3 - i, 3)
        second_turn = lax.rem(lax.rem(i, 3), 2)
        third_turn = lax.div(lax.rem(i, 3), 2)
        fourth_turn = lax.div(i, 3)
        return (
            first_turn * lax.rem(me + 2, 4)
            + second_turn * (3 - me)
            + third_turn * (me + 1 - 2 * lax.rem(me, 2))
            + fourth_turn * me
        )

    def compress(half, target):
        left = jnp.concatenate(
            [
                filt[:, pl.ds(pl.multiple_of(2 * owned * half + 512 * target + 256 * b, 256), 1280)]
                for b in range(2)
            ],
            axis=0,
        )
        squeezed = jnp.dot(left, chp[...], preferred_element_type=jnp.float32)
        n = squeezed.shape[0] // 2
        return jnp.concatenate(
            [
                jnp.concatenate([squeezed[:n, :128], squeezed[n:, :128]], axis=1),
                jnp.concatenate([squeezed[:n, 128:], squeezed[n:, 128:]], axis=1),
            ],
            axis=0,
        ).astype(jnp.bfloat16)

    def offer(i):
        return pltpu.make_async_remote_copy(
            src_ref=offered.at[i],
            dst_ref=both.at[i, rx],
            send_sem=offer_send.at[i],
            recv_sem=offer_recv.at[i],
            device_id={"rx": 1 - rx},
            device_id_type=MESH,
        )

    def offers(late):
        def one(i, carry):
            target = target_of(i)
            needs = jnp.logical_and(rx == rng, lax.div(target, 2) == 1 - rng)

            @pl.when(needs if late else jnp.logical_not(needs))
            def _():
                offered[i] = compress(1 - rx, target)
                offer(i).start()

            return carry

        lax.fori_loop(0, pulse_count, one, 0)

    offers(False)

    halo.wait_recv()
    place = pl.multiple_of((1 - rng) * (length + EDGE), 128)
    for part in range(2):
        for spot in range(0, EDGE, 128):
            block = edge[part, :, :, spot : spot + 128].astype(jnp.float32)
            turned[part, :, :, pl.ds(pl.multiple_of(place + spot, 128), 128)] = jnp.swapaxes(block, 0, 1)
    filter_blocks((1 - rng) * (blocks + 1), 3)
    offers(True)

    start = (rng * length + rx * owned) + 1 + lax.broadcasted_iota(jnp.int32, (beams, SPAN), 1)
    for field in range(len(rows)):
        k = angle * (start * (rows[field] + 1))
        phase[0, field, 0], phase[0, field, 1] = turn(jnp.bitwise_and(k, 1023), half_root)


    def piece(i, target):
        return pltpu.make_async_remote_copy(
            src_ref=sent.at[i],
            dst_ref=got.at[i],
            send_sem=piece_send.at[i],
            recv_sem=piece_recv.at[i],
            device_id={"pulse": target},
            device_id_type=MESH,
        )

    def own(i, carry):
        both[i, rx] = compress(rx, target_of(i))
        return carry

    lax.fori_loop(0, pulse_count, own, 0)

    def chunk(i, carry):
        target = target_of(i)
        for field in range(len(rows)):
            quarter = jnp.bitwise_and(angle * ((rows[field] + 1) * target), 3)
            c = jnp.where(quarter == 0, 1.0, jnp.where(quarter == 2, -1.0, 0.0))
            s = jnp.where(quarter == 1, 1.0, jnp.where(quarter == 3, -1.0, 0.0))
            re, im = phase[0, field, 0], phase[0, field, 1]
            phase[1, field, 0] = c * re - s * im
            phase[1, field, 1] = s * re + c * im
        offer(i).wait_recv()
        right = jnp.concatenate([both[i, 0], both[i, 1]], axis=0)

        def spun(field, re, im):
            c, s = phase[1, field, 0], phase[1, field, 1]
            return c * re - s * im, s * re + c * im

        images = []
        for g in range(pulses // 2):
            parts = []
            for side in range(2):
                p = 2 * g + side
                x = jnp.dot(
                    form[2 * p * beams : 2 * (p + 1) * beams, :], right, preferred_element_type=jnp.float32
                )
                parts.append(spun(p, x[:beams], x[beams:]))
            images.append(
                jnp.concatenate([parts[0][k] + parts[1][k] for k in range(2)], axis=1).astype(jnp.bfloat16)
            )
        field = pulses
        for matrix in (first, second):
            x = jnp.dot(matrix[...], jnp.concatenate(images, axis=0), preferred_element_type=jnp.float32)
            merged = []
            for g in range(len(images) // 2):
                parts = []
                for side in range(2):
                    y = x[(2 * g + side) * beams : (2 * g + side + 1) * beams]
                    parts.append(spun(field, y[:, :SPAN], y[:, SPAN:]))
                    field += 1
                merged.append(
                    jnp.concatenate([parts[0][k] + parts[1][k] for k in range(2)], axis=1).astype(jnp.bfloat16)
                )
            images = merged
        picture = images[0]
        for k in range(2):
            y = jnp.dot(last[k], picture, preferred_element_type=jnp.float32)
            re, im = spun(field + k, y[:, :SPAN], y[:, SPAN:])
            if k == 0:
                picture = jnp.concatenate([re, im], axis=1).astype(jnp.bfloat16)

        @pl.when(i < pulse_count - 1)
        def _():
            sent[i, 0] = re.astype(jnp.bfloat16)
            sent[i, 1] = im.astype(jnp.bfloat16)
            piece(i, target).start()

        @pl.when(i == pulse_count - 1)
        def _():
            out[0] = re
            out[1] = im

        return carry

    lax.fori_loop(0, pulse_count, chunk, 0)
    halo.wait_send()
    for i in range(pulse_count):
        offer(i).wait_send()
    for i in range(pulse_count - 1):
        piece(i, target_of(i)).wait()
        out[...] += got[i].astype(jnp.float32)


def fused(echoes, beam_angle, interp_table, pulse_count):
    pulses, channels, length = echoes.shape[1:]
    beams = beam_angle.shape[0]
    receivers = 2 * channels
    owned = length // 2
    bands = jnp.asarray(receiver_bands(receivers))
    chirps = jnp.asarray(chirp_bands())
    table = interp_table.reshape(-1, beams)
    extent = length + 2 * EDGE
    bf16, f32 = jnp.bfloat16, jnp.float32
    whole = pl.BlockSpec(memory_space=pltpu.VMEM)
    away = pl.BlockSpec(memory_space=pltpu.HBM)
    return pl.pallas_call(
        functools.partial(focus_kernel, pulse_count),
        out_shape=pltpu.VMEM((2, beams, SPAN), f32),
        in_specs=[away] * 5,
        out_specs=whole,
        scratch_shapes=[
            pltpu.VMEM((1, beams), jnp.int32),
            pltpu.VMEM(table.shape, jnp.int32),
            pltpu.VMEM((2, pulses, channels, length), bf16),
            pltpu.VMEM((2, pulses, channels, EDGE), bf16),
            pltpu.VMEM((2, channels, pulses, extent), f32),
            pltpu.VMEM((channels * pulses, 2 * length + 1024), bf16),
            pltpu.VMEM((channels,) + bands.shape[1:], bf16),
            pltpu.VMEM(chirps.shape, bf16),
            pltpu.VMEM((2, 16, 2, beams, SPAN), f32),
            pltpu.VMEM((2 * pulses * beams, 2 * receivers * pulses), bf16),
            pltpu.VMEM((4 * beams, 4 * beams), bf16),
            pltpu.VMEM((2 * beams, 2 * beams), bf16),
            pltpu.VMEM((2, beams, beams), bf16),
            pltpu.VMEM((pulse_count, 2 * channels * pulses, SPAN), bf16),
            pltpu.VMEM((pulse_count, 2, 2 * channels * pulses, SPAN), bf16),
            pltpu.VMEM((pulse_count - 1, 2, beams, SPAN), bf16),
            pltpu.VMEM((pulse_count - 1, 2, beams, SPAN), bf16),
            pltpu.SemaphoreType.DMA((5,)),
            pltpu.SemaphoreType.DMA((2,)),
            pltpu.SemaphoreType.DMA((pulse_count,)),
            pltpu.SemaphoreType.DMA((pulse_count,)),
            pltpu.SemaphoreType.DMA((pulse_count - 1,)),
            pltpu.SemaphoreType.DMA((pulse_count - 1,)),
        ],
        compiler_params=pltpu.CompilerParams(
            collective_id=0, has_side_effects=True, vmem_limit_bytes=50 << 20
        ),
    )(*[
        pltpu.with_memory_space_constraint(x, pltpu.HBM)
        for x in (echoes, beam_angle.reshape(1, beams), table, bands, chirps)
    ])


def route(echoes, beam_angle, interp_table):
    pulse_count = lax.axis_size("pulse")
    pulses, channels, length = echoes.shape[1:]
    fits = (
        lax.axis_size("rx") == 2
        and lax.axis_size("rng") == 2
        and pulse_count == 4
        and (pulses, channels, length) == (8, 8, 2 * SPAN * pulse_count)
        and beam_angle.shape[0] == 64
    )
    if fits:
        return fused(echoes, beam_angle, interp_table, pulse_count)
    return local(echoes, beam_angle, interp_table)


def solution(mesh):
    placed = (P(None, ("slab", "pulse"), "rx", "rng"), P(), P())
    return jax.shard_map(
        route,
        mesh=mesh,
        in_specs=placed,
        out_specs=P(None, "slab", ("rng", "rx", "pulse")),
        check_vma=False,
    )
```

```python
import functools
import math

import jax
import ml_dtypes
import jax.numpy as jnp
import numpy as np
from jax import lax
from jax.experimental import pallas as pl
from jax.experimental.pallas import tpu as pltpu
from jax.sharding import PartitionSpec as P

RTAPS = 64
CTAPS = 512


half_root = 0.7071067811865476
full_turn = 2.0 * math.pi
SPAN = 256
EDGE = 384
MESH = pl.DeviceIdType.MESH


def extended_2(block, sides, width):
    for axis, dim in sides:
        count = lax.axis_size(axis)
        forward = [(i, i + 1) for i in range(count - 1)]
        backward = [(target, source) for source, target in forward]
        low = lax.ppermute(
            lax.slice_in_dim(block, block.shape[dim] - width, None, axis=dim), axis, forward
        )
        high = lax.ppermute(lax.slice_in_dim(block, 0, width, axis=dim), axis, backward)
        block = jnp.concatenate([low, block, high], axis=dim)
    return block


def swapped(x, axis, distance):
    return lax.ppermute(x, axis, [(i, i ^ 1 << distance) for i in range(lax.axis_size(axis))])


def receiver_taps(channel_ids, tap_count):
    tap_index = jnp.arange(tap_count, dtype=jnp.float32)
    window = 0.5 - 0.5 * jnp.cos(full_turn * (tap_index + 0.5) / tap_count)
    window = window / jnp.sqrt(jnp.sum(window * window))
    channel = channel_ids.astype(jnp.float32)[:, None] + 1.0
    angle = full_turn * channel * (tap_index - tap_count // 2) / (4 * tap_count)
    return (
        (window * jnp.cos(angle)).astype(jnp.bfloat16),
        (window * jnp.sin(angle)).astype(jnp.bfloat16),
    )


def chirp_taps(tap_count):
    offset = jnp.arange(tap_count, dtype=jnp.int32) - tap_count // 2
    phase_step = jnp.mod(offset * offset, 2 * tap_count).astype(jnp.float32)
    angle = math.pi * phase_step / tap_count
    scale = 1.0 / math.sqrt(tap_count)
    return (
        (jnp.cos(angle) * scale).astype(jnp.bfloat16),
        (-jnp.sin(angle) * scale).astype(jnp.bfloat16),
    )


def steering(beam_angle, receivers):
    channel = jnp.arange(receivers, dtype=jnp.int32)
    turns = jnp.mod(beam_angle[:, None] * channel[None, :], 1024).astype(jnp.float32)
    angle = full_turn * turns / 1024.0
    scale = 1.0 / math.sqrt(receivers)
    return (
        (jnp.cos(angle) * scale).astype(jnp.bfloat16),
        (-jnp.sin(angle) * scale).astype(jnp.bfloat16),
    )


def interp_matrices(codes, beam_count):
    shifted = codes // 4 - 1
    fraction = jnp.mod(codes, 4).astype(jnp.float32) / 4.0
    weights = (
        -fraction * (fraction - 1.0) * (fraction - 2.0) / 6.0,
        (fraction + 1.0) * (fraction - 1.0) * (fraction - 2.0) / 2.0,
        -(fraction + 1.0) * fraction * (fraction - 2.0) / 2.0,
        (fraction + 1.0) * fraction * (fraction - 1.0) / 6.0,
    )
    columns = jnp.arange(beam_count, dtype=jnp.int32)
    matrices = jnp.zeros(codes.shape + (beam_count,), jnp.float32)
    for tap_index in range(4):
        target = jnp.mod(columns + shifted + tap_index - 1, beam_count)
        matrices = matrices + weights[tap_index][..., None] * (target[..., None] == columns).astype(
            jnp.float32
        )
    return matrices


def phases(node_ids, positions, beam_angle, side):
    base = jnp.mod(beam_angle[:, None] * (positions[None, :] + 1), 1024)
    factor = 2 * node_ids + side + 1
    turns = jnp.mod(base[:, None, :] * factor[None, :, None], 1024).astype(jnp.float32)
    angle = full_turn * turns / 1024.0
    return (jnp.cos(angle), jnp.sin(angle))


def side_term(picture, matrices, cosine, sine):
    moved = jnp.einsum("gqa,cagr->cqgr", matrices, picture, precision=lax.Precision.HIGHEST)
    return (cosine * moved[0] - sine * moved[1], sine * moved[0] + cosine * moved[1])


def merge_pair(left_image, right_image, node_ids, positions, beam_angle, interp_table):
    matrices = interp_matrices(
        lax.dynamic_slice_in_dim(interp_table, node_ids[0], node_ids.shape[0]), left_image.shape[1]
    )
    left_cos, left_sin = phases(node_ids, positions, beam_angle, 0)
    right_cos, right_sin = phases(node_ids, positions, beam_angle, 1)
    left_re, left_im = side_term(left_image, matrices[:, 0], left_cos, left_sin)
    right_re, right_im = side_term(right_image, matrices[:, 1], right_cos, right_sin)
    return jnp.stack([(left_re + right_re) * half_root, (left_im + right_im) * half_root])


def toeplitz_blocks(taps_re, taps_im):
    tap_count = taps_re.shape[-1]
    leading = taps_re.shape[:-1]

    def lay_out(taps):
        padded = jnp.concatenate([taps, jnp.zeros(leading + (tap_count + 1,), taps.dtype)], axis=-1)
        tiled = jnp.tile(padded, (1,) * len(leading) + (tap_count,))
        banded = tiled[..., : 2 * tap_count * tap_count].reshape(
            leading + (tap_count, 2 * tap_count)
        )
        return jnp.swapaxes(banded, -1, -2)

    real_band = lay_out(taps_re)
    imag_band = lay_out(taps_im)
    upper = jnp.concatenate([real_band, imag_band], axis=-1)
    lower = jnp.concatenate([-imag_band, real_band], axis=-1)
    return jnp.concatenate([upper, lower], axis=-2)


def block_filter(extended, matrices, tap_count, per_channel):
    pulses, channels, length = extended.shape[1:]
    blocks = length // tap_count - 1
    pieces = extended.reshape(2, pulses, channels, blocks + 1, tap_count)
    windows = jnp.concatenate([pieces[:, :, :, :-1], pieces[:, :, :, 1:]], axis=4)
    windows = jnp.transpose(windows, (1, 2, 3, 0, 4)).reshape(
        pulses, channels, blocks, 4 * tap_count
    )
    if per_channel:
        output = jnp.einsum("pcnw,cwo->pcno", windows, matrices, preferred_element_type=jnp.float32)
    else:
        output = jnp.einsum("pcnw,wo->pcno", windows, matrices, preferred_element_type=jnp.float32)
    output = output.reshape(pulses, channels, blocks, 2, tap_count)
    return jnp.transpose(output, (3, 0, 1, 2, 4)).reshape(2, pulses, channels, blocks * tap_count)


def local(echoes, beam_angle, interp_table):
    rx_count = lax.axis_size("rx")
    pulse_count = lax.axis_size("pulse")
    rng_place = lax.axis_index("rng")
    rx_place = lax.axis_index("rx")
    pulse_place = lax.axis_index("pulse")
    pulses, channels, length = echoes.shape[1:]
    beam_count = beam_angle.shape[0]
    receivers = channels * rx_count
    channel_ids = rx_place * channels + jnp.arange(channels, dtype=jnp.int32)
    rx_re, rx_im = receiver_taps(channel_ids, RTAPS)
    rx_bands = toeplitz_blocks(rx_re, rx_im)
    chirp_re, chirp_im = chirp_taps(CTAPS)
    chirp_band = toeplitz_blocks(chirp_re, chirp_im)
    extended = extended_2(echoes, (("rng", 3),), RTAPS // 2)
    filtered = block_filter(extended, rx_bands, RTAPS, True).astype(jnp.bfloat16)
    filtered = extended_2(filtered, (("rng", 3),), CTAPS // 2)
    compressed = block_filter(filtered, chirp_band, CTAPS, False).astype(jnp.bfloat16)
    steering_real, steering_imaginary = steering(beam_angle, receivers)
    steer_matrix = jnp.concatenate(
        [
            jnp.concatenate([steering_real, -steering_imaginary], axis=1),
            jnp.concatenate([steering_imaginary, steering_real], axis=1),
        ],
        axis=0,
    )
    arrived = lax.all_to_all(compressed, "rx", split_axis=3, concat_axis=2, tiled=True)
    item_count, recv_count, owned_cols = arrived.shape[1:]
    stacked = jnp.transpose(arrived, (0, 2, 1, 3)).reshape(2 * recv_count, item_count * owned_cols)
    formed = jnp.dot(steer_matrix, stacked, preferred_element_type=jnp.float32)
    picture = formed.reshape(2, beam_count, item_count, owned_cols)
    owned_width = length // rx_count
    positions = (
        rng_place * length + rx_place * owned_width + jnp.arange(owned_width, dtype=jnp.int32)
    )
    for level in range(pulses.bit_length() - 1):
        groups_now = pulses >> level + 1
        node_ids = (pulse_count + pulse_place) * groups_now + jnp.arange(
            groups_now, dtype=jnp.int32
        )
        paired = picture.reshape(2, beam_count, groups_now, 2, owned_width)
        picture = merge_pair(
            paired[:, :, :, 0], paired[:, :, :, 1], node_ids, positions, beam_angle, interp_table
        )
    picture = picture[:, :, 0]
    cross_levels = pulse_count.bit_length() - 1
    piece_width = owned_width // pulse_count
    pieces = picture.reshape(2, beam_count, pulse_count, piece_width)
    spots = positions.reshape(pulse_count, piece_width)
    for level in range(cross_levels):
        parity = jnp.right_shift(pulse_place, level) & 1
        count_now = pieces.shape[2]
        paired = pieces.reshape(2, beam_count, count_now // 2, 2, piece_width)
        kept_half = lax.dynamic_index_in_dim(paired, parity, 3, keepdims=False)
        sent_half = lax.dynamic_index_in_dim(paired, 1 - parity, 3, keepdims=False)
        partner = swapped(sent_half, "pulse", level)
        spot_pairs = spots.reshape(count_now // 2, 2, piece_width)
        spots = lax.dynamic_index_in_dim(spot_pairs, parity, 1, keepdims=False)
        own_part = kept_half.reshape(2, beam_count, -1)
        other_part = partner.reshape(2, beam_count, -1)
        left_image = jnp.where(parity == 0, own_part, other_part)
        right_image = jnp.where(parity == 0, other_part, own_part)
        combine_node_ids = jnp.reshape(
            (pulse_count >> level + 1) + jnp.right_shift(pulse_place, level + 1), (1,)
        )
        merged = merge_pair(
            left_image[:, :, None],
            right_image[:, :, None],
            combine_node_ids,
            spots.reshape(-1),
            beam_angle,
            interp_table,
        )
        flat = merged[:, :, 0]
        pieces = flat.reshape(2, beam_count, count_now // 2, piece_width)
    picture = pieces.reshape(2, beam_count, piece_width)
    return picture


def receiver_bands(receivers):
    t = np.arange(RTAPS, dtype=np.float64)
    window = 0.5 - 0.5 * np.cos(full_turn * (t + 0.5) / RTAPS)
    window = window / np.sqrt(np.sum(window * window))
    angle = full_turn * np.arange(1, receivers + 1)[:, None] * (t - RTAPS // 2) / (4 * RTAPS)
    lane = np.arange(128)
    row = np.concatenate([128 + lane, np.where(lane < 64, 256 + lane, lane)])
    lag = row[:, None] - np.arange(128)[None, :] - (128 - RTAPS // 2)
    return banded(window * np.cos(angle), window * np.sin(angle), lag, RTAPS, 128)


def chirp_bands():
    t = np.arange(CTAPS) - CTAPS // 2
    angle = math.pi * ((t * t) % (2 * CTAPS)) / CTAPS
    scale = 1.0 / math.sqrt(CTAPS)
    lag = np.arange(CTAPS + 128)[:, None] - np.arange(128)[None, :]
    return banded(np.cos(angle)[None] * scale, -np.sin(angle)[None] * scale, lag, CTAPS, 128)[0]


def banded(taps_re, taps_im, lag, count, group):
    inside = (lag >= 0) & (lag < count)
    spot = np.clip(lag, 0, count - 1)
    re = np.where(inside, taps_re[:, spot], 0.0)
    im = np.where(inside, taps_im[:, spot], 0.0)
    channels, rows, cols = re.shape
    upper = np.concatenate([re, im], axis=2).reshape(channels, rows // group, 1, group, 2 * cols)
    lower = np.concatenate([-im, re], axis=2).reshape(channels, rows // group, 1, group, 2 * cols)
    both = np.concatenate([upper, lower], axis=2)
    return both.reshape(channels, 2 * rows, 2 * cols).astype(np.float32).astype(ml_dtypes.bfloat16)


def turn(k, scale):
    shifted = k + 128
    quadrant = jnp.bitwise_and(jnp.right_shift(shifted, 8), 3)
    y = (jnp.bitwise_and(shifted, 255) - 128).astype(jnp.float32) * (full_turn / 1024.0)
    z = y * y
    sine = y * (1.0 + z * (-1 / 6 + z * (1 / 120 + z * (-1 / 5040 + z * (1 / 362880)))))
    cosine = 1.0 + z * (-0.5 + z * (1 / 24 + z * (-1 / 720 + z * (1 / 40320))))
    odd = jnp.bitwise_and(quadrant, 1) == 1
    c = jnp.where(odd, sine, cosine)
    s = jnp.where(odd, cosine, sine)
    c = jnp.where(jnp.bitwise_and(quadrant + 1, 2) == 2, -c, c)
    s = jnp.where(quadrant >= 2, -s, s)
    return c * scale, s * scale


def upright(row, size):
    across = lax.broadcasted_iota(jnp.int32, (size, size), 1)
    down = lax.broadcasted_iota(jnp.int32, (size, size), 0)
    spread = jnp.where(across == down, jnp.broadcast_to(row.astype(jnp.float32), (size, size)), 0.0)
    return jnp.sum(spread, axis=1, keepdims=True)


def interp_pair(codes, size):
    shift = jnp.right_shift(codes, 2) - 1
    f = jnp.bitwise_and(codes, 3).astype(jnp.float32) * 0.25
    weights = (
        -f * (f - 1.0) * (f - 2.0) * (1 / 6),
        (f + 1.0) * (f - 1.0) * (f - 2.0) * 0.5,
        -(f + 1.0) * f * (f - 2.0) * 0.5,
        (f + 1.0) * f * (f - 1.0) * (1 / 6),
    )
    wide = (size, 2 * size)
    first = lax.broadcasted_iota(jnp.int32, codes.shape, 1) + shift - 1
    gap = lax.broadcasted_iota(jnp.int32, wide, 0) - jnp.broadcast_to(first, wide)
    gap = jnp.bitwise_and(gap, size - 1)
    out = jnp.zeros(wide, jnp.float32)
    for k in range(4):
        out = jnp.where(gap == k, jnp.broadcast_to(weights[k], wide), out)
    return jnp.transpose(out).astype(jnp.bfloat16)


def times(a, b):
    return a[0] * b[0] - a[1] * b[1], a[0] * b[1] + a[1] * b[0]


def times_conj(a, b):
    return a[0] * b[0] + a[1] * b[1], a[1] * b[0] - a[0] * b[1]


def square(a):
    return (a[0] - a[1]) * (a[0] + a[1]), 2.0 * a[0] * a[1]


def choose(flag, a, b):
    return jnp.where(flag, a[0], b[0]), jnp.where(flag, a[1], b[1])


def powers(one, me):
    two = square(one)
    three = times(two, one)
    four = square(two)
    outer = choose(me < 2, three, four)
    more = choose(me < 2, choose(me == 0, one, two), choose(me == 2, three, four))
    inner = times(four, more)
    second = times_conj(square(inner), one)
    first = [times_conj(square(second), one)]
    first.append(times(first[0], two))
    leaf = [times_conj(square(first[0]), one)]
    for _ in range(3):
        leaf.append(times(leaf[-1], two))
    return [one] + leaf + first + [second, inner, outer]


def focus_kernel(
    pulse_count, ech, ang_hbm, tab_hbm, trx_hbm, chp_hbm, out,
    ang, tab, held, edge, wide, filt, trx, chp, phase, form, mats,
    offered, both, sent, got,
    near_sem, halo_sem, offer_send, offer_recv, piece_send, piece_recv,
):
    rx, rng, me = lax.axis_index("rx"), lax.axis_index("rng"), lax.axis_index("pulse")
    beams = ang.shape[1]
    rows, length = ech.shape[1:]
    channels = trx.shape[0]
    pulses = rows // channels
    owned = length // 2
    barrier = pltpu.get_barrier_semaphore()
    pl.semaphore_signal(barrier, inc=1, device_id={"rng": 1 - rng}, device_id_type=MESH)
    pl.semaphore_signal(barrier, inc=1, device_id={"rx": 1 - rx}, device_id_type=MESH)
    for step in range(1, pulse_count):
        pl.semaphore_signal(
            barrier, inc=1, device_id={"pulse": lax.rem(me + step, pulse_count)}, device_id_type=MESH
        )

    tables = [
        pltpu.make_async_copy(ang_hbm, ang, near_sem.at[0]),
        pltpu.make_async_copy(tab_hbm, tab, near_sem.at[1]),
    ]
    echo_in = pltpu.make_async_copy(ech, held, near_sem.at[2])
    chirp_in = pltpu.make_async_copy(chp_hbm, chp, near_sem.at[3])
    bands_in = [
        pltpu.make_async_copy(
            trx_hbm.at[pl.ds(rx * channels + 2 * i, 2)], trx.at[pl.ds(2 * i, 2)], near_sem.at[4 + i]
        )
        for i in range(channels // 2)
    ]
    for copy in tables + [echo_in] + bands_in + [chirp_in]:
        copy.start()

    @pl.when(rng == 0)
    def _():
        wide[:, 2] = jnp.zeros((2, rows, 128), wide.dtype)
        filt[:, :512] = jnp.zeros((rows, 512), filt.dtype)

    @pl.when(rng == 1)
    def _():
        wide[:, 3 + length // 128] = jnp.zeros((2, rows, 128), wide.dtype)
        filt[:, 512 + 2 * length :] = jnp.zeros((rows, 512), filt.dtype)

    for copy in tables:
        copy.wait()
    angle = upright(ang[...], beams).astype(jnp.int32)

    echo_in.wait()
    for part in range(2):
        for spot in range(length // 128):
            wide[part, 3 + spot] = held[part, :, 128 * spot : 128 * spot + 128].astype(jnp.float32)

    low = lax.broadcasted_iota(jnp.int32, (pulses, 128), 1) < 64

    def filter_pair(pair, start, blocks):
        results = []
        for c in (2 * pair, 2 * pair + 1):
            cells = [
                [
                    wide[part, start + j, pl.ds(c, pulses, stride=channels), :]
                    for j in range(blocks + 2)
                ]
                for part in range(2)
            ]
            left = jnp.concatenate(
                [
                    jnp.concatenate(
                        [
                            cells[0][j + 1],
                            cells[1][j + 1],
                            jnp.where(low, cells[0][j + 2], cells[0][j]),
                            jnp.where(low, cells[1][j + 2], cells[1][j]),
                        ],
                        axis=1,
                    )
                    for j in range(blocks)
                ],
                axis=0,
            ).astype(jnp.bfloat16)
            results.append(jnp.dot(left, trx[c], preferred_element_type=jnp.float32))
        for j in range(blocks):
            filt[2 * pair * pulses : 2 * (pair + 1) * pulses, pl.ds(pl.multiple_of(256 * (start + j), 256), 256)] = (
                jnp.concatenate([r[8 * j : 8 * j + 8] for r in results], axis=0).astype(jnp.bfloat16)
            )

    for pair in range(channels // 2):
        bands_in[pair].wait()
        filter_pair(pair, 2 + rng, length // 128 - 1)

    def relation(i, late):
        swap = late * (1 - jnp.abs(lax.div(me, 2) - rng))
        return jnp.where(i == 3, 3, lax.rem(i + 2 * swap, 3))

    def related(k):
        return jnp.where(
            k == 0,
            lax.rem(me + 2, 4),
            jnp.where(k == 1, 3 - me, jnp.where(k == 2, me + 1 - 2 * lax.rem(me, 2), me)),
        )

    def target_of(i, late):
        return related(relation(i, late))

    out_late = 1 - jnp.abs(rx - rng)
    in_late = jnp.abs(rx - rng)

    def compress(half, target):
        left = jnp.concatenate(
            [
                filt[:, pl.ds(pl.multiple_of(2 * owned * half + 512 * target + 256 * b, 256), 1280)]
                for b in range(2)
            ],
            axis=0,
        )
        squeezed = jnp.dot(left, chp[...], preferred_element_type=jnp.float32)
        n = squeezed.shape[0] // 2
        return jnp.concatenate(
            [
                jnp.concatenate([squeezed[:n, :128], squeezed[n:, :128]], axis=1),
                jnp.concatenate([squeezed[:n, 128:], squeezed[n:, 128:]], axis=1),
            ],
            axis=0,
        ).astype(jnp.bfloat16)

    def offer(i):
        return pltpu.make_async_remote_copy(
            src_ref=offered.at[i],
            dst_ref=both.at[i, rx],
            send_sem=offer_send.at[i],
            recv_sem=offer_recv.at[i],
            device_id={"rx": 1 - rx},
            device_id_type=MESH,
        )

    chirp_in.wait()
    offered[0] = compress(1 - rx, target_of(0, out_late))
    pl.semaphore_wait(barrier, 1 + pulse_count)
    offer(0).start()
    halo = pltpu.make_async_remote_copy(
        src_ref=ech.at[:, :, pl.ds(pl.multiple_of((1 - rng) * (length - EDGE), 128), EDGE)],
        dst_ref=edge,
        send_sem=halo_sem.at[0],
        recv_sem=halo_sem.at[1],
        device_id={"rng": 1 - rng},
        device_id_type=MESH,
    )
    halo.start()

    def needs(i):
        return out_late * (1 - jnp.abs(lax.div(target_of(i, out_late), 2) - (1 - rng)))

    for i in range(1, pulse_count):

        @pl.when(needs(i) == 0)
        def _():
            offered[i] = compress(1 - rx, target_of(i, out_late))
            offer(i).start()

    halo.wait_recv()
    place = (1 - rng) * (length // 128 + 3)
    for part in range(2):
        for spot in range(3):
            wide[part, place + spot] = edge[part, :, 128 * spot : 128 * spot + 128].astype(jnp.float32)
    for pair in range(channels // 2):
        filter_pair(pair, (1 - rng) * (length // 128 + 1), 3)

    for i in range(1, pulse_count):

        @pl.when(needs(i) == 1)
        def _():
            offered[i] = compress(1 - rx, target_of(i, out_late))
            offer(i).start()

    node = [(pulse_count + me) * (pulses >> k + 1) for k in range(3)]
    nodes = [node[k] + i for k in range(3) for i in range(pulses >> k + 1)]
    codes = [tab[pl.ds(2 * n + side, 1), :] for n in nodes for side in range(2)]
    codes += [tab[pl.ds((pulse_count >> k) + jnp.right_shift(me, k), 1), :] for k in range(2)]
    mixers = [
        interp_pair(jnp.concatenate(codes[2 * i : 2 * i + 2], axis=1), beams) for i in range(8)
    ]
    for i in range(4):
        mats[2 * i * beams : 2 * (i + 1) * beams, :] = mixers[4 + i]
    size = (beams, 2 * 2 * channels * pulses)
    column = lax.broadcasted_iota(jnp.int32, size, 1)
    local_channel = jnp.bitwise_and(jnp.right_shift(column, 3), channels - 1)
    receiver = local_channel + channels * jnp.right_shift(column, 7)
    cosine, sine = turn(jnp.bitwise_and(angle * receiver, 1023), 0.25)
    imag = jnp.bitwise_and(jnp.right_shift(column, 6), 1) == 1
    steer = [
        jnp.where(imag, sine, cosine).astype(jnp.bfloat16),
        jnp.where(imag, cosine, -sine).astype(jnp.bfloat16),
    ]
    lane_pulse = jnp.bitwise_and(column, pulses - 1)
    for i in range(pulses // 2):
        for part in range(2):
            mixed = jnp.dot(mixers[i], steer[part], preferred_element_type=jnp.float32)
            for side in range(2):
                p = 2 * i + side
                spot = (2 * p + part) * beams
                form[spot : spot + beams, :] = jnp.where(
                    lane_pulse == p, mixed[side * beams : (side + 1) * beams], 0.0
                ).astype(jnp.bfloat16)


    for i in range(pulse_count):
        both[i, rx] = compress(rx, target_of(i, in_late))

    along = (rng * length + rx * owned) + 1 + lax.broadcasted_iota(jnp.int32, (beams, 128), 1)
    fields = powers(turn(jnp.bitwise_and(angle * along, 1023), 1.0), me)
    steps = powers(
        turn(jnp.bitwise_and(jnp.broadcast_to(angle, (beams, 128)) * 128, 1023), 1.0), me
    )
    for k in range(len(fields)):
        field = fields[k] if k == 0 else (fields[k][0] * half_root, fields[k][1] * half_root)
        for spot in range(2 * pulse_count):
            if spot:
                field = times(field, steps[k])
            lanes = slice(128 * (spot % 2), 128 * (spot % 2) + 128)
            phase[spot // 2, k, 0, :, lanes], phase[spot // 2, k, 1, :, lanes] = field

    def piece(k):
        return pltpu.make_async_remote_copy(
            src_ref=sent.at[k],
            dst_ref=got.at[k],
            send_sem=piece_send.at[k],
            recv_sem=piece_recv.at[k],
            device_id={"pulse": related(k)},
            device_id_type=MESH,
        )

    def chunk(i, carry):
        k = relation(i, in_late)
        target = related(k)
        offer(i).wait_recv()
        right = jnp.concatenate([both[i, 0], both[i, 1]], axis=0)

        def spun(field, x):
            return times((phase[target, field, 0], phase[target, field, 1]), x)

        def joined(field, left_x, right_x):
            moved = spun(0, right_x)
            return spun(field, (left_x[0] + moved[0], left_x[1] + moved[1]))

        def image(x):
            return jnp.concatenate([x[0], x[1]], axis=1).astype(jnp.bfloat16)

        def interpolated(k, x):
            y = jnp.dot(
                mats[pl.ds(k * beams, beams), :], image(x), preferred_element_type=jnp.float32
            )
            return y[:, :SPAN], y[:, SPAN:]

        images = []
        for p in range(pulses):
            x = jnp.dot(
                form[2 * p * beams : 2 * (p + 1) * beams, :], right, preferred_element_type=jnp.float32
            )
            images.append((x[:beams], x[beams:]))
        field, node = 1, 0
        while True:
            merged = []
            for g in range(len(images) // 2):
                merged.append(joined(field, images[2 * g], images[2 * g + 1]))
                field += 1
            images = []
            for x in merged:
                images.append(interpolated(node, x))
                node += 1
            if len(images) == 1:
                break
        picture = spun(field, images[0])
        re, im = spun(field + 1, interpolated(node, picture))

        @pl.when(i < pulse_count - 1)
        def _():
            sent[k, 0] = re.astype(jnp.bfloat16)
            sent[k, 1] = im.astype(jnp.bfloat16)
            piece(k).start()

        @pl.when(i == pulse_count - 1)
        def _():
            out[0] = re
            out[1] = im

        return carry

    lax.fori_loop(0, pulse_count, chunk, 0)
    halo.wait_send()
    for i in range(pulse_count):
        offer(i).wait_send()
    for i in range(pulse_count - 1):
        piece(i).wait()
        out[...] += got[i].astype(jnp.float32)


def fused(echoes, beam_angle, interp_table, pulse_count):
    pulses, channels, length = echoes.shape[1:]
    beams = beam_angle.shape[0]
    receivers = 2 * channels
    rows = pulses * channels
    bands = jnp.asarray(receiver_bands(receivers))
    chirps = jnp.asarray(chirp_bands())
    table = interp_table.reshape(-1, beams)
    bf16, f32 = jnp.bfloat16, jnp.float32
    away = pl.BlockSpec(memory_space=pltpu.HBM)
    operands = (echoes.reshape(2, rows, length), beam_angle.reshape(1, beams), table, bands, chirps)
    return pl.pallas_call(
        functools.partial(focus_kernel, pulse_count),
        out_shape=pltpu.VMEM((2, beams, SPAN), f32),
        in_specs=[away] * 5,
        out_specs=pl.BlockSpec(memory_space=pltpu.VMEM),
        scratch_shapes=[
            pltpu.VMEM((1, beams), jnp.int32),
            pltpu.VMEM(table.shape, jnp.int32),
            pltpu.VMEM((2, rows, length), bf16),
            pltpu.VMEM((2, rows, EDGE), bf16),
            pltpu.VMEM((2, length // 128 + 6, rows, 128), f32),
            pltpu.VMEM((rows, 2 * length + 1024), bf16),
            pltpu.VMEM((channels,) + bands.shape[1:], bf16),
            pltpu.VMEM(chirps.shape, bf16),
            pltpu.VMEM((pulse_count, 10, 2, beams, SPAN), f32),
            pltpu.VMEM((2 * pulses * beams, 2 * receivers * pulses), bf16),
            pltpu.VMEM((8 * beams, beams), bf16),
            pltpu.VMEM((pulse_count, 2 * rows, SPAN), bf16),
            pltpu.VMEM((pulse_count, 2, 2 * rows, SPAN), bf16),
            pltpu.VMEM((pulse_count - 1, 2, beams, SPAN), bf16),
            pltpu.VMEM((pulse_count - 1, 2, beams, SPAN), bf16),
            pltpu.SemaphoreType.DMA((8,)),
            pltpu.SemaphoreType.DMA((2,)),
            pltpu.SemaphoreType.DMA((pulse_count,)),
            pltpu.SemaphoreType.DMA((pulse_count,)),
            pltpu.SemaphoreType.DMA((pulse_count - 1,)),
            pltpu.SemaphoreType.DMA((pulse_count - 1,)),
        ],
        compiler_params=pltpu.CompilerParams(
            collective_id=0, has_side_effects=True, vmem_limit_bytes=50 << 20
        ),
    )(*[pltpu.with_memory_space_constraint(x, pltpu.HBM) for x in operands])


def route(echoes, beam_angle, interp_table):
    pulse_count = lax.axis_size("pulse")
    pulses, channels, length = echoes.shape[1:]
    fits = (
        lax.axis_size("rx") == 2
        and lax.axis_size("rng") == 2
        and pulse_count == 4
        and (pulses, channels, length) == (8, 8, 2 * SPAN * pulse_count)
        and beam_angle.shape[0] == 64
    )
    if fits:
        return fused(echoes, beam_angle, interp_table, pulse_count)
    return local(echoes, beam_angle, interp_table)


def solution(mesh):
    placed = (P(None, ("slab", "pulse"), "rx", "rng"), P(), P())
    return jax.shard_map(
        route,
        mesh=mesh,
        in_specs=placed,
        out_specs=P(None, "slab", ("rng", "rx", "pulse")),
        check_vma=False,
    )
```

```python
import functools
import math

import jax
import ml_dtypes
import jax.numpy as jnp
import numpy as np
from jax import lax
from jax.experimental import pallas as pl
from jax.experimental.pallas import tpu as pltpu
from jax.sharding import PartitionSpec as P

RTAPS = 64
CTAPS = 512


half_root = 0.7071067811865476
full_turn = 2.0 * math.pi
SPAN = 256
EDGE = 384
MESH = pl.DeviceIdType.MESH


def extended_2(block, sides, width):
    for axis, dim in sides:
        count = lax.axis_size(axis)
        forward = [(i, i + 1) for i in range(count - 1)]
        backward = [(target, source) for source, target in forward]
        low = lax.ppermute(
            lax.slice_in_dim(block, block.shape[dim] - width, None, axis=dim), axis, forward
        )
        high = lax.ppermute(lax.slice_in_dim(block, 0, width, axis=dim), axis, backward)
        block = jnp.concatenate([low, block, high], axis=dim)
    return block


def swapped(x, axis, distance):
    return lax.ppermute(x, axis, [(i, i ^ 1 << distance) for i in range(lax.axis_size(axis))])


def receiver_taps(channel_ids, tap_count):
    tap_index = jnp.arange(tap_count, dtype=jnp.float32)
    window = 0.5 - 0.5 * jnp.cos(full_turn * (tap_index + 0.5) / tap_count)
    window = window / jnp.sqrt(jnp.sum(window * window))
    channel = channel_ids.astype(jnp.float32)[:, None] + 1.0
    angle = full_turn * channel * (tap_index - tap_count // 2) / (4 * tap_count)
    return (
        (window * jnp.cos(angle)).astype(jnp.bfloat16),
        (window * jnp.sin(angle)).astype(jnp.bfloat16),
    )


def chirp_taps(tap_count):
    offset = jnp.arange(tap_count, dtype=jnp.int32) - tap_count // 2
    phase_step = jnp.mod(offset * offset, 2 * tap_count).astype(jnp.float32)
    angle = math.pi * phase_step / tap_count
    scale = 1.0 / math.sqrt(tap_count)
    return (
        (jnp.cos(angle) * scale).astype(jnp.bfloat16),
        (-jnp.sin(angle) * scale).astype(jnp.bfloat16),
    )


def steering(beam_angle, receivers):
    channel = jnp.arange(receivers, dtype=jnp.int32)
    turns = jnp.mod(beam_angle[:, None] * channel[None, :], 1024).astype(jnp.float32)
    angle = full_turn * turns / 1024.0
    scale = 1.0 / math.sqrt(receivers)
    return (
        (jnp.cos(angle) * scale).astype(jnp.bfloat16),
        (-jnp.sin(angle) * scale).astype(jnp.bfloat16),
    )


def interp_matrices(codes, beam_count):
    shifted = codes // 4 - 1
    fraction = jnp.mod(codes, 4).astype(jnp.float32) / 4.0
    weights = (
        -fraction * (fraction - 1.0) * (fraction - 2.0) / 6.0,
        (fraction + 1.0) * (fraction - 1.0) * (fraction - 2.0) / 2.0,
        -(fraction + 1.0) * fraction * (fraction - 2.0) / 2.0,
        (fraction + 1.0) * fraction * (fraction - 1.0) / 6.0,
    )
    columns = jnp.arange(beam_count, dtype=jnp.int32)
    matrices = jnp.zeros(codes.shape + (beam_count,), jnp.float32)
    for tap_index in range(4):
        target = jnp.mod(columns + shifted + tap_index - 1, beam_count)
        matrices = matrices + weights[tap_index][..., None] * (target[..., None] == columns).astype(
            jnp.float32
        )
    return matrices


def phases(node_ids, positions, beam_angle, side):
    base = jnp.mod(beam_angle[:, None] * (positions[None, :] + 1), 1024)
    factor = 2 * node_ids + side + 1
    turns = jnp.mod(base[:, None, :] * factor[None, :, None], 1024).astype(jnp.float32)
    angle = full_turn * turns / 1024.0
    return (jnp.cos(angle), jnp.sin(angle))


def side_term(picture, matrices, cosine, sine):
    moved = jnp.einsum("gqa,cagr->cqgr", matrices, picture, precision=lax.Precision.HIGHEST)
    return (cosine * moved[0] - sine * moved[1], sine * moved[0] + cosine * moved[1])


def merge_pair(left_image, right_image, node_ids, positions, beam_angle, interp_table):
    matrices = interp_matrices(
        lax.dynamic_slice_in_dim(interp_table, node_ids[0], node_ids.shape[0]), left_image.shape[1]
    )
    left_cos, left_sin = phases(node_ids, positions, beam_angle, 0)
    right_cos, right_sin = phases(node_ids, positions, beam_angle, 1)
    left_re, left_im = side_term(left_image, matrices[:, 0], left_cos, left_sin)
    right_re, right_im = side_term(right_image, matrices[:, 1], right_cos, right_sin)
    return jnp.stack([(left_re + right_re) * half_root, (left_im + right_im) * half_root])


def toeplitz_blocks(taps_re, taps_im):
    tap_count = taps_re.shape[-1]
    leading = taps_re.shape[:-1]

    def lay_out(taps):
        padded = jnp.concatenate([taps, jnp.zeros(leading + (tap_count + 1,), taps.dtype)], axis=-1)
        tiled = jnp.tile(padded, (1,) * len(leading) + (tap_count,))
        banded = tiled[..., : 2 * tap_count * tap_count].reshape(
            leading + (tap_count, 2 * tap_count)
        )
        return jnp.swapaxes(banded, -1, -2)

    real_band = lay_out(taps_re)
    imag_band = lay_out(taps_im)
    upper = jnp.concatenate([real_band, imag_band], axis=-1)
    lower = jnp.concatenate([-imag_band, real_band], axis=-1)
    return jnp.concatenate([upper, lower], axis=-2)


def block_filter(extended, matrices, tap_count, per_channel):
    pulses, channels, length = extended.shape[1:]
    blocks = length // tap_count - 1
    pieces = extended.reshape(2, pulses, channels, blocks + 1, tap_count)
    windows = jnp.concatenate([pieces[:, :, :, :-1], pieces[:, :, :, 1:]], axis=4)
    windows = jnp.transpose(windows, (1, 2, 3, 0, 4)).reshape(
        pulses, channels, blocks, 4 * tap_count
    )
    if per_channel:
        output = jnp.einsum("pcnw,cwo->pcno", windows, matrices, preferred_element_type=jnp.float32)
    else:
        output = jnp.einsum("pcnw,wo->pcno", windows, matrices, preferred_element_type=jnp.float32)
    output = output.reshape(pulses, channels, blocks, 2, tap_count)
    return jnp.transpose(output, (3, 0, 1, 2, 4)).reshape(2, pulses, channels, blocks * tap_count)


def local(echoes, beam_angle, interp_table):
    rx_count = lax.axis_size("rx")
    pulse_count = lax.axis_size("pulse")
    rng_place = lax.axis_index("rng")
    rx_place = lax.axis_index("rx")
    pulse_place = lax.axis_index("pulse")
    pulses, channels, length = echoes.shape[1:]
    beam_count = beam_angle.shape[0]
    receivers = channels * rx_count
    channel_ids = rx_place * channels + jnp.arange(channels, dtype=jnp.int32)
    rx_re, rx_im = receiver_taps(channel_ids, RTAPS)
    rx_bands = toeplitz_blocks(rx_re, rx_im)
    chirp_re, chirp_im = chirp_taps(CTAPS)
    chirp_band = toeplitz_blocks(chirp_re, chirp_im)
    extended = extended_2(echoes, (("rng", 3),), RTAPS // 2)
    filtered = block_filter(extended, rx_bands, RTAPS, True).astype(jnp.bfloat16)
    filtered = extended_2(filtered, (("rng", 3),), CTAPS // 2)
    compressed = block_filter(filtered, chirp_band, CTAPS, False).astype(jnp.bfloat16)
    steering_real, steering_imaginary = steering(beam_angle, receivers)
    steer_matrix = jnp.concatenate(
        [
            jnp.concatenate([steering_real, -steering_imaginary], axis=1),
            jnp.concatenate([steering_imaginary, steering_real], axis=1),
        ],
        axis=0,
    )
    arrived = lax.all_to_all(compressed, "rx", split_axis=3, concat_axis=2, tiled=True)
    item_count, recv_count, owned_cols = arrived.shape[1:]
    stacked = jnp.transpose(arrived, (0, 2, 1, 3)).reshape(2 * recv_count, item_count * owned_cols)
    formed = jnp.dot(steer_matrix, stacked, preferred_element_type=jnp.float32)
    picture = formed.reshape(2, beam_count, item_count, owned_cols)
    owned_width = length // rx_count
    positions = (
        rng_place * length + rx_place * owned_width + jnp.arange(owned_width, dtype=jnp.int32)
    )
    for level in range(pulses.bit_length() - 1):
        groups_now = pulses >> level + 1
        node_ids = (pulse_count + pulse_place) * groups_now + jnp.arange(
            groups_now, dtype=jnp.int32
        )
        paired = picture.reshape(2, beam_count, groups_now, 2, owned_width)
        picture = merge_pair(
            paired[:, :, :, 0], paired[:, :, :, 1], node_ids, positions, beam_angle, interp_table
        )
    picture = picture[:, :, 0]
    cross_levels = pulse_count.bit_length() - 1
    piece_width = owned_width // pulse_count
    pieces = picture.reshape(2, beam_count, pulse_count, piece_width)
    spots = positions.reshape(pulse_count, piece_width)
    for level in range(cross_levels):
        parity = jnp.right_shift(pulse_place, level) & 1
        count_now = pieces.shape[2]
        paired = pieces.reshape(2, beam_count, count_now // 2, 2, piece_width)
        kept_half = lax.dynamic_index_in_dim(paired, parity, 3, keepdims=False)
        sent_half = lax.dynamic_index_in_dim(paired, 1 - parity, 3, keepdims=False)
        partner = swapped(sent_half, "pulse", level)
        spot_pairs = spots.reshape(count_now // 2, 2, piece_width)
        spots = lax.dynamic_index_in_dim(spot_pairs, parity, 1, keepdims=False)
        own_part = kept_half.reshape(2, beam_count, -1)
        other_part = partner.reshape(2, beam_count, -1)
        left_image = jnp.where(parity == 0, own_part, other_part)
        right_image = jnp.where(parity == 0, other_part, own_part)
        combine_node_ids = jnp.reshape(
            (pulse_count >> level + 1) + jnp.right_shift(pulse_place, level + 1), (1,)
        )
        merged = merge_pair(
            left_image[:, :, None],
            right_image[:, :, None],
            combine_node_ids,
            spots.reshape(-1),
            beam_angle,
            interp_table,
        )
        flat = merged[:, :, 0]
        pieces = flat.reshape(2, beam_count, count_now // 2, piece_width)
    picture = pieces.reshape(2, beam_count, piece_width)
    return picture


def receiver_bands(receivers):
    t = np.arange(RTAPS, dtype=np.float64)
    window = 0.5 - 0.5 * np.cos(full_turn * (t + 0.5) / RTAPS)
    window = window / np.sqrt(np.sum(window * window))
    angle = full_turn * np.arange(1, receivers + 1)[:, None] * (t - RTAPS // 2) / (4 * RTAPS)
    lane = np.arange(128)
    row = np.concatenate([128 + lane, np.where(lane < 64, 256 + lane, lane)])
    lag = row[:, None] - np.arange(128)[None, :] - (128 - RTAPS // 2)
    return banded(window * np.cos(angle), window * np.sin(angle), lag, RTAPS, 128)


def chirp_bands():
    t = np.arange(CTAPS) - CTAPS // 2
    angle = math.pi * ((t * t) % (2 * CTAPS)) / CTAPS
    scale = 1.0 / math.sqrt(CTAPS)
    lag = np.arange(CTAPS + 128)[:, None] - np.arange(128)[None, :]
    return banded(np.cos(angle)[None] * scale, -np.sin(angle)[None] * scale, lag, CTAPS, 128)[0]


def banded(taps_re, taps_im, lag, count, group):
    inside = (lag >= 0) & (lag < count)
    spot = np.clip(lag, 0, count - 1)
    re = np.where(inside, taps_re[:, spot], 0.0)
    im = np.where(inside, taps_im[:, spot], 0.0)
    channels, rows, cols = re.shape
    upper = np.concatenate([re, im], axis=2).reshape(channels, rows // group, 1, group, 2 * cols)
    lower = np.concatenate([-im, re], axis=2).reshape(channels, rows // group, 1, group, 2 * cols)
    both = np.concatenate([upper, lower], axis=2)
    return both.reshape(channels, 2 * rows, 2 * cols).astype(np.float32).astype(ml_dtypes.bfloat16)


def turn(k, scale):
    shifted = k + 128
    quadrant = jnp.bitwise_and(jnp.right_shift(shifted, 8), 3)
    y = (jnp.bitwise_and(shifted, 255) - 128).astype(jnp.float32) * (full_turn / 1024.0)
    z = y * y
    sine = y * (1.0 + z * (-1 / 6 + z * (1 / 120 + z * (-1 / 5040 + z * (1 / 362880)))))
    cosine = 1.0 + z * (-0.5 + z * (1 / 24 + z * (-1 / 720 + z * (1 / 40320))))
    odd = jnp.bitwise_and(quadrant, 1) == 1
    c = jnp.where(odd, sine, cosine)
    s = jnp.where(odd, cosine, sine)
    c = jnp.where(jnp.bitwise_and(quadrant + 1, 2) == 2, -c, c)
    s = jnp.where(quadrant >= 2, -s, s)
    return c * scale, s * scale


def upright(row, size, folded):
    across = lax.broadcasted_iota(jnp.int32, (size, size), 1)
    down = lax.broadcasted_iota(jnp.int32, (size, size), 0)
    if folded:
        down = 8 * jnp.bitwise_and(down, 7) + jnp.right_shift(down, 3)
    spread = jnp.where(across == down, jnp.broadcast_to(row.astype(jnp.float32), (size, size)), 0.0)
    return jnp.sum(spread, axis=1, keepdims=True)


def refold(x):
    return jnp.swapaxes(x.reshape(8, 8, x.shape[1]), 0, 1).reshape(x.shape)


def shift_and_weights(codes):
    shift = jnp.right_shift(codes, 2) - 1
    f = jnp.bitwise_and(codes, 3).astype(jnp.float32) * 0.25
    weights = (
        -f * (f - 1.0) * (f - 2.0) * (1 / 6),
        (f + 1.0) * (f - 1.0) * (f - 2.0) * 0.5,
        -(f + 1.0) * f * (f - 2.0) * 0.5,
        (f + 1.0) * f * (f - 1.0) * (1 / 6),
    )
    return shift, weights


def tap_rows(codes):
    shift, weights = shift_and_weights(codes)
    spread = []
    for d in range(-2, 4):
        row = jnp.zeros(codes.shape, jnp.float32)
        for k in range(4):
            row = jnp.where(shift == d - k + 1, weights[k], row)
        spread.append(row)
    return spread


def interp_pair(codes, size):
    shift, weights = shift_and_weights(codes)
    wide = (size, 2 * size)
    first = lax.broadcasted_iota(jnp.int32, codes.shape, 1) + shift - 1
    gap = lax.broadcasted_iota(jnp.int32, wide, 0) - jnp.broadcast_to(first, wide)
    gap = jnp.bitwise_and(gap, size - 1)
    out = jnp.zeros(wide, jnp.float32)
    for k in range(4):
        out = jnp.where(gap == k, jnp.broadcast_to(weights[k], wide), out)
    turned = jnp.transpose(out)
    halves = [refold(turned[:size]), refold(turned[size:])]
    return jnp.concatenate(halves, axis=0).astype(jnp.bfloat16)


def times(a, b):
    return a[0] * b[0] - a[1] * b[1], a[0] * b[1] + a[1] * b[0]


def times_conj(a, b):
    return a[0] * b[0] + a[1] * b[1], a[1] * b[0] - a[0] * b[1]


def square(a):
    return (a[0] - a[1]) * (a[0] + a[1]), 2.0 * a[0] * a[1]


def choose(flag, a, b):
    return jnp.where(flag, a[0], b[0]), jnp.where(flag, a[1], b[1])


def powers(one, me):
    two = square(one)
    three = times(two, one)
    four = square(two)
    outer = choose(me < 2, three, four)
    more = choose(me < 2, choose(me == 0, one, two), choose(me == 2, three, four))
    inner = times(four, more)
    second = times_conj(square(inner), one)
    first = [times_conj(square(second), one)]
    first.append(times(first[0], two))
    leaf = [times_conj(square(first[0]), one)]
    for _ in range(3):
        leaf.append(times(leaf[-1], two))
    return [one] + leaf + first + [second, inner, outer]


def focus_kernel(
    pulse_count, ech, ang_hbm, tab_hbm, trx_hbm, chp_hbm, out,
    ang, tab, held, edge, wide, filt, trx, chp, phase, form, coef,
    offered, both, sent, got, final,
    near_sem, halo_sem, offer_send, offer_recv, piece_send, piece_recv,
):
    rx, rng, me = lax.axis_index("rx"), lax.axis_index("rng"), lax.axis_index("pulse")
    beams = ang.shape[1]
    rows, length = ech.shape[1:]
    channels = trx.shape[0]
    pulses = rows // channels
    owned = length // 2
    barrier = pltpu.get_barrier_semaphore()
    pl.semaphore_signal(barrier, inc=1, device_id={"rng": 1 - rng}, device_id_type=MESH)
    pl.semaphore_signal(barrier, inc=1, device_id={"rx": 1 - rx}, device_id_type=MESH)
    for step in range(1, pulse_count):
        pl.semaphore_signal(
            barrier, inc=1, device_id={"pulse": lax.rem(me + step, pulse_count)}, device_id_type=MESH
        )

    tables = [
        pltpu.make_async_copy(ang_hbm, ang, near_sem.at[0]),
        pltpu.make_async_copy(tab_hbm, tab, near_sem.at[1]),
    ]
    echo_in = pltpu.make_async_copy(ech, held, near_sem.at[2])
    chirp_in = pltpu.make_async_copy(chp_hbm, chp, near_sem.at[3])
    bands_in = [
        pltpu.make_async_copy(
            trx_hbm.at[pl.ds(rx * channels + 2 * i, 2)], trx.at[pl.ds(2 * i, 2)], near_sem.at[4 + i]
        )
        for i in range(channels // 2)
    ]
    for copy in tables + [echo_in] + bands_in + [chirp_in]:
        copy.start()

    @pl.when(rng == 0)
    def _():
        wide[:, 2] = jnp.zeros((2, rows, 128), wide.dtype)
        filt[:, :512] = jnp.zeros((rows, 512), filt.dtype)

    @pl.when(rng == 1)
    def _():
        wide[:, 3 + length // 128] = jnp.zeros((2, rows, 128), wide.dtype)
        filt[:, 512 + 2 * length :] = jnp.zeros((rows, 512), filt.dtype)

    for copy in tables:
        copy.wait()
    angle = upright(ang[...], beams, False).astype(jnp.int32)
    folded = upright(ang[...], beams, True).astype(jnp.int32)

    echo_in.wait()
    for part in range(2):
        for spot in range(length // 128):
            wide[part, 3 + spot] = held[part, :, 128 * spot : 128 * spot + 128].astype(jnp.float32)

    low = lax.broadcasted_iota(jnp.int32, (pulses, 128), 1) < 64

    def filter_pair(pair, start, blocks):
        results = []
        for c in (2 * pair, 2 * pair + 1):
            cells = [
                [
                    wide[part, start + j, pl.ds(c, pulses, stride=channels), :]
                    for j in range(blocks + 2)
                ]
                for part in range(2)
            ]
            left = jnp.concatenate(
                [
                    jnp.concatenate(
                        [
                            cells[0][j + 1],
                            cells[1][j + 1],
                            jnp.where(low, cells[0][j + 2], cells[0][j]),
                            jnp.where(low, cells[1][j + 2], cells[1][j]),
                        ],
                        axis=1,
                    )
                    for j in range(blocks)
                ],
                axis=0,
            ).astype(jnp.bfloat16)
            results.append(jnp.dot(left, trx[c], preferred_element_type=jnp.float32))
        for j in range(blocks):
            filt[2 * pair * pulses : 2 * (pair + 1) * pulses, pl.ds(pl.multiple_of(256 * (start + j), 256), 256)] = (
                jnp.concatenate([r[8 * j : 8 * j + 8] for r in results], axis=0).astype(jnp.bfloat16)
            )

    for pair in range(channels // 2):
        bands_in[pair].wait()
        filter_pair(pair, 2 + rng, length // 128 - 1)

    def relation(i, late):
        swap = late * (1 - jnp.abs(lax.div(me, 2) - rng))
        return jnp.where(i == 3, 3, lax.rem(i + 2 * swap, 3))

    def related(k):
        return jnp.where(
            k == 0,
            lax.rem(me + 2, 4),
            jnp.where(k == 1, 3 - me, jnp.where(k == 2, me + 1 - 2 * lax.rem(me, 2), me)),
        )

    def target_of(i, late):
        return related(relation(i, late))

    out_late = 1 - jnp.abs(rx - rng)
    in_late = jnp.abs(rx - rng)

    def compress(half, targets):
        left = jnp.concatenate(
            [
                filt[:, pl.ds(pl.multiple_of(2 * owned * half + 512 * target + 256 * b, 256), 1280)]
                for target in targets
                for b in range(2)
            ],
            axis=0,
        )
        squeezed = jnp.dot(left, chp[...], preferred_element_type=jnp.float32)
        units = [squeezed[rows * u : rows * (u + 1)] for u in range(2 * len(targets))]
        return [
            jnp.concatenate([x[:, :128], x[:, 128:]], axis=0).astype(jnp.bfloat16) for x in units
        ]

    def offer(u):
        return pltpu.make_async_remote_copy(
            src_ref=offered.at[u],
            dst_ref=both.at[u, rx],
            send_sem=offer_send.at[u],
            recv_sem=offer_recv.at[u],
            device_id={"rx": 1 - rx},
            device_id_type=MESH,
        )

    chirp_in.wait()
    def give(spots):
        made = compress(1 - rx, [target_of(i, out_late) for i in spots])
        units = [2 * i + h for i in spots for h in range(2)]
        for u, block in zip(units, made):
            offered[u] = block
        return units

    give([0])
    pl.semaphore_wait(barrier, 1 + pulse_count)
    offer(0).start()
    offer(1).start()
    halo = pltpu.make_async_remote_copy(
        src_ref=ech.at[:, :, pl.ds(pl.multiple_of((1 - rng) * (length - EDGE), 128), EDGE)],
        dst_ref=edge,
        send_sem=halo_sem.at[0],
        recv_sem=halo_sem.at[1],
        device_id={"rng": 1 - rng},
        device_id_type=MESH,
    )
    halo.start()

    swap = 1 - jnp.abs(lax.div(me, 2) - rng)
    for u in give([1 + 2 * out_late * swap]):
        offer(u).start()

    @pl.when(out_late == 0)
    def _():
        for u in give([2, 3]):
            offer(u).start()

    node = [(pulse_count + me) * (pulses >> k + 1) for k in range(3)]
    nodes = [node[k] + i for k in range(3) for i in range(pulses >> k + 1)]
    codes = [tab[pl.ds(2 * n + side, 1), :] for n in nodes for side in range(2)]
    codes += [tab[pl.ds((pulse_count >> k) + jnp.right_shift(me, k), 1), :] for k in range(2)]
    mixers = [
        interp_pair(jnp.concatenate(codes[2 * i : 2 * i + 2], axis=1), beams) for i in range(4)
    ]
    spread = tap_rows(jnp.concatenate(codes[8:], axis=0))
    for m in range(8):
        for d in range(6):
            coef[6 * m + d] = jnp.broadcast_to(
                upright(spread[d][m : m + 1], beams, True), (beams, 128)
            )
    size = (beams, 2 * 2 * channels * pulses)
    column = lax.broadcasted_iota(jnp.int32, size, 1)
    local_channel = jnp.bitwise_and(jnp.right_shift(column, 3), channels - 1)
    receiver = local_channel + channels * jnp.right_shift(column, 7)
    cosine, sine = turn(jnp.bitwise_and(angle * receiver, 1023), 0.25)
    imag = jnp.bitwise_and(jnp.right_shift(column, 6), 1) == 1
    steer = [
        jnp.where(imag, sine, cosine).astype(jnp.bfloat16),
        jnp.where(imag, cosine, -sine).astype(jnp.bfloat16),
    ]
    lane_pulse = jnp.bitwise_and(column, pulses - 1)
    for i in range(pulses // 2):
        for part in range(2):
            mixed = jnp.dot(mixers[i], steer[part], preferred_element_type=jnp.float32)
            for side in range(2):
                p = 2 * i + side
                spot = (2 * p + part) * beams
                form[spot : spot + beams, :] = jnp.where(
                    lane_pulse == p, mixed[side * beams : (side + 1) * beams], 0.0
                ).astype(jnp.bfloat16)


    halo.wait_recv()
    place = (1 - rng) * (length // 128 + 3)
    for part in range(2):
        for spot in range(3):
            wide[part, place + spot] = edge[part, :, 128 * spot : 128 * spot + 128].astype(jnp.float32)
    for pair in range(channels // 2):
        filter_pair(pair, (1 - rng) * (length // 128 + 1), 3)

    @pl.when(out_late == 1)
    def _():
        for u in give([2 - swap, 3 - swap]):
            offer(u).start()

    made = compress(rx, [target_of(i, in_late) for i in range(pulse_count)])
    for u in range(2 * pulse_count):
        both[u, rx] = made[u]

    along = (rng * length + rx * owned) + 1 + lax.broadcasted_iota(jnp.int32, (beams, 128), 1)
    fields = powers(turn(jnp.bitwise_and(folded * along, 1023), 1.0), me)
    steps = powers(
        turn(jnp.bitwise_and(jnp.broadcast_to(folded, (beams, 128)) * 128, 1023), 1.0), me
    )
    for k in range(len(fields)):
        field = fields[k] if k == 0 else (fields[k][0] * half_root, fields[k][1] * half_root)
        for spot in range(2 * pulse_count):
            if spot:
                field = times(field, steps[k])
            phase[spot, k, 0], phase[spot, k, 1] = field

    def piece(k, h):
        return pltpu.make_async_remote_copy(
            src_ref=sent.at[k, h],
            dst_ref=got.at[k, h],
            send_sem=piece_send.at[2 * k + h],
            recv_sem=piece_recv.at[2 * k + h],
            device_id={"pulse": related(k)},
            device_id_type=MESH,
        )

    def unit(u, carry):
        h = lax.rem(u, 2)
        k = relation(lax.div(u, 2), in_late)
        spot = 2 * related(k) + h
        offer(u).wait_recv()
        right = jnp.concatenate([both[u, 0], both[u, 1]], axis=0)

        def spun(field, x):
            return times((phase[spot, field, 0], phase[spot, field, 1]), x)

        def joined(field, left_x, right_x):
            moved = spun(0, right_x)
            return spun(field, (left_x[0] + moved[0], left_x[1] + moved[1]))

        def blended(m, x):
            results = []
            for part in range(2):
                rows_of = [x[part][8 * v : 8 * v + 8] for v in range(beams // 8)]
                lined = [pltpu.roll(v, 1, 0) for v in rows_of[-2:]] + rows_of
                lined += [pltpu.roll(v, 7, 0) for v in rows_of[:3]]
                sums = []
                for v in range(beams // 8):
                    terms = [coef[6 * m + d, 8 * v : 8 * v + 8] * lined[v + d] for d in range(6)]
                    sums.append(((terms[0] + terms[1]) + (terms[2] + terms[3])) + (terms[4] + terms[5]))
                results.append(jnp.concatenate(sums, axis=0))
            return results

        images = []
        for g in range(pulses // 2):
            x = jnp.dot(
                form[4 * g * beams : 4 * (g + 1) * beams, :], right, preferred_element_type=jnp.float32
            )
            x = [x[beams * n : beams * (n + 1)] for n in range(4)]
            images.append(blended(g, joined(1 + g, (x[0], x[1]), (x[2], x[3]))))
        images = [joined(5 + g, images[2 * g], images[2 * g + 1]) for g in range(2)]
        picture = joined(7, blended(4, images[0]), blended(5, images[1]))
        picture = spun(8, blended(6, picture))
        re, im = spun(9, blended(7, picture))

        @pl.when(k < pulse_count - 1)
        def _():
            sent[k, h, 0] = re.astype(jnp.bfloat16)
            sent[k, h, 1] = im.astype(jnp.bfloat16)
            piece(k, h).start()

        @pl.when(k == pulse_count - 1)
        def _():
            final[h, 0] = re
            final[h, 1] = im

        return carry

    lax.fori_loop(0, 2 * pulse_count, unit, 0)
    halo.wait_send()
    for u in range(2 * pulse_count):
        offer(u).wait_send()
    total = [[final[h, part] for part in range(2)] for h in range(2)]
    for k in (2, 0, 1):
        for h in range(2):
            piece(k, h).wait()
            for part in range(2):
                total[h][part] = total[h][part] + got[k, h, part].astype(jnp.float32)
    for part in range(2):
        out[part] = jnp.concatenate([refold(total[0][part]), refold(total[1][part])], axis=1)


def fused(echoes, beam_angle, interp_table, pulse_count):
    pulses, channels, length = echoes.shape[1:]
    beams = beam_angle.shape[0]
    receivers = 2 * channels
    rows = pulses * channels
    bands = jnp.asarray(receiver_bands(receivers))
    chirps = jnp.asarray(chirp_bands())
    table = interp_table.reshape(-1, beams)
    bf16, f32 = jnp.bfloat16, jnp.float32
    away = pl.BlockSpec(memory_space=pltpu.HBM)
    operands = (echoes.reshape(2, rows, length), beam_angle.reshape(1, beams), table, bands, chirps)
    return pl.pallas_call(
        functools.partial(focus_kernel, pulse_count),
        out_shape=pltpu.VMEM((2, beams, SPAN), f32),
        in_specs=[away] * 5,
        out_specs=pl.BlockSpec(memory_space=pltpu.VMEM),
        scratch_shapes=[
            pltpu.VMEM((1, beams), jnp.int32),
            pltpu.VMEM(table.shape, jnp.int32),
            pltpu.VMEM((2, rows, length), bf16),
            pltpu.VMEM((2, rows, EDGE), bf16),
            pltpu.VMEM((2, length // 128 + 6, rows, 128), f32),
            pltpu.VMEM((rows, 2 * length + 1024), bf16),
            pltpu.VMEM((channels,) + bands.shape[1:], bf16),
            pltpu.VMEM(chirps.shape, bf16),
            pltpu.VMEM((2 * pulse_count, 10, 2, beams, 128), f32),
            pltpu.VMEM((2 * pulses * beams, 2 * receivers * pulses), bf16),
            pltpu.VMEM((48, beams, 128), f32),
            pltpu.VMEM((2 * pulse_count, 2 * rows, 128), bf16),
            pltpu.VMEM((2 * pulse_count, 2, 2 * rows, 128), bf16),
            pltpu.VMEM((pulse_count - 1, 2, 2, beams, 128), bf16),
            pltpu.VMEM((pulse_count - 1, 2, 2, beams, 128), bf16),
            pltpu.VMEM((2, 2, beams, 128), f32),
            pltpu.SemaphoreType.DMA((8,)),
            pltpu.SemaphoreType.DMA((2,)),
            pltpu.SemaphoreType.DMA((2 * pulse_count,)),
            pltpu.SemaphoreType.DMA((2 * pulse_count,)),
            pltpu.SemaphoreType.DMA((2 * pulse_count - 2,)),
            pltpu.SemaphoreType.DMA((2 * pulse_count - 2,)),
        ],
        compiler_params=pltpu.CompilerParams(
            collective_id=0, has_side_effects=True, vmem_limit_bytes=50 << 20
        ),
    )(*[pltpu.with_memory_space_constraint(x, pltpu.HBM) for x in operands])


def route(echoes, beam_angle, interp_table):
    pulse_count = lax.axis_size("pulse")
    pulses, channels, length = echoes.shape[1:]
    fits = (
        lax.axis_size("rx") == 2
        and lax.axis_size("rng") == 2
        and pulse_count == 4
        and (pulses, channels, length) == (8, 8, 2 * SPAN * pulse_count)
        and beam_angle.shape[0] == 64
    )
    if fits:
        return fused(echoes, beam_angle, interp_table, pulse_count)
    return local(echoes, beam_angle, interp_table)


def solution(mesh):
    placed = (P(None, ("slab", "pulse"), "rx", "rng"), P(), P())
    return jax.shard_map(
        route,
        mesh=mesh,
        in_specs=placed,
        out_specs=P(None, "slab", ("rng", "rx", "pulse")),
        check_vma=False,
    )
```

```python
import functools
import math

import jax
import ml_dtypes
import jax.numpy as jnp
import numpy as np
from jax import lax
from jax.experimental import pallas as pl
from jax.experimental.pallas import tpu as pltpu
from jax.sharding import PartitionSpec as P

RTAPS = 64
CTAPS = 512


half_root = 0.7071067811865476
full_turn = 2.0 * math.pi
SPAN = 256
EDGE = 384
MESH = pl.DeviceIdType.MESH


def extended_2(block, sides, width):
    for axis, dim in sides:
        count = lax.axis_size(axis)
        forward = [(i, i + 1) for i in range(count - 1)]
        backward = [(target, source) for source, target in forward]
        low = lax.ppermute(
            lax.slice_in_dim(block, block.shape[dim] - width, None, axis=dim), axis, forward
        )
        high = lax.ppermute(lax.slice_in_dim(block, 0, width, axis=dim), axis, backward)
        block = jnp.concatenate([low, block, high], axis=dim)
    return block


def swapped(x, axis, distance):
    return lax.ppermute(x, axis, [(i, i ^ 1 << distance) for i in range(lax.axis_size(axis))])


def receiver_taps(channel_ids, tap_count):
    tap_index = jnp.arange(tap_count, dtype=jnp.float32)
    window = 0.5 - 0.5 * jnp.cos(full_turn * (tap_index + 0.5) / tap_count)
    window = window / jnp.sqrt(jnp.sum(window * window))
    channel = channel_ids.astype(jnp.float32)[:, None] + 1.0
    angle = full_turn * channel * (tap_index - tap_count // 2) / (4 * tap_count)
    return (
        (window * jnp.cos(angle)).astype(jnp.bfloat16),
        (window * jnp.sin(angle)).astype(jnp.bfloat16),
    )


def chirp_taps(tap_count):
    offset = jnp.arange(tap_count, dtype=jnp.int32) - tap_count // 2
    phase_step = jnp.mod(offset * offset, 2 * tap_count).astype(jnp.float32)
    angle = math.pi * phase_step / tap_count
    scale = 1.0 / math.sqrt(tap_count)
    return (
        (jnp.cos(angle) * scale).astype(jnp.bfloat16),
        (-jnp.sin(angle) * scale).astype(jnp.bfloat16),
    )


def steering(beam_angle, receivers):
    channel = jnp.arange(receivers, dtype=jnp.int32)
    turns = jnp.mod(beam_angle[:, None] * channel[None, :], 1024).astype(jnp.float32)
    angle = full_turn * turns / 1024.0
    scale = 1.0 / math.sqrt(receivers)
    return (
        (jnp.cos(angle) * scale).astype(jnp.bfloat16),
        (-jnp.sin(angle) * scale).astype(jnp.bfloat16),
    )


def interp_matrices(codes, beam_count):
    shifted = codes // 4 - 1
    fraction = jnp.mod(codes, 4).astype(jnp.float32) / 4.0
    weights = (
        -fraction * (fraction - 1.0) * (fraction - 2.0) / 6.0,
        (fraction + 1.0) * (fraction - 1.0) * (fraction - 2.0) / 2.0,
        -(fraction + 1.0) * fraction * (fraction - 2.0) / 2.0,
        (fraction + 1.0) * fraction * (fraction - 1.0) / 6.0,
    )
    columns = jnp.arange(beam_count, dtype=jnp.int32)
    matrices = jnp.zeros(codes.shape + (beam_count,), jnp.float32)
    for tap_index in range(4):
        target = jnp.mod(columns + shifted + tap_index - 1, beam_count)
        matrices = matrices + weights[tap_index][..., None] * (target[..., None] == columns).astype(
            jnp.float32
        )
    return matrices


def phases(node_ids, positions, beam_angle, side):
    base = jnp.mod(beam_angle[:, None] * (positions[None, :] + 1), 1024)
    factor = 2 * node_ids + side + 1
    turns = jnp.mod(base[:, None, :] * factor[None, :, None], 1024).astype(jnp.float32)
    angle = full_turn * turns / 1024.0
    return (jnp.cos(angle), jnp.sin(angle))


def side_term(picture, matrices, cosine, sine):
    moved = jnp.einsum("gqa,cagr->cqgr", matrices, picture, precision=lax.Precision.HIGHEST)
    return (cosine * moved[0] - sine * moved[1], sine * moved[0] + cosine * moved[1])


def merge_pair(left_image, right_image, node_ids, positions, beam_angle, interp_table):
    matrices = interp_matrices(
        lax.dynamic_slice_in_dim(interp_table, node_ids[0], node_ids.shape[0]), left_image.shape[1]
    )
    left_cos, left_sin = phases(node_ids, positions, beam_angle, 0)
    right_cos, right_sin = phases(node_ids, positions, beam_angle, 1)
    left_re, left_im = side_term(left_image, matrices[:, 0], left_cos, left_sin)
    right_re, right_im = side_term(right_image, matrices[:, 1], right_cos, right_sin)
    return jnp.stack([(left_re + right_re) * half_root, (left_im + right_im) * half_root])


def toeplitz_blocks(taps_re, taps_im):
    tap_count = taps_re.shape[-1]
    leading = taps_re.shape[:-1]

    def lay_out(taps):
        padded = jnp.concatenate([taps, jnp.zeros(leading + (tap_count + 1,), taps.dtype)], axis=-1)
        tiled = jnp.tile(padded, (1,) * len(leading) + (tap_count,))
        banded = tiled[..., : 2 * tap_count * tap_count].reshape(
            leading + (tap_count, 2 * tap_count)
        )
        return jnp.swapaxes(banded, -1, -2)

    real_band = lay_out(taps_re)
    imag_band = lay_out(taps_im)
    upper = jnp.concatenate([real_band, imag_band], axis=-1)
    lower = jnp.concatenate([-imag_band, real_band], axis=-1)
    return jnp.concatenate([upper, lower], axis=-2)


def block_filter(extended, matrices, tap_count, per_channel):
    pulses, channels, length = extended.shape[1:]
    blocks = length // tap_count - 1
    pieces = extended.reshape(2, pulses, channels, blocks + 1, tap_count)
    windows = jnp.concatenate([pieces[:, :, :, :-1], pieces[:, :, :, 1:]], axis=4)
    windows = jnp.transpose(windows, (1, 2, 3, 0, 4)).reshape(
        pulses, channels, blocks, 4 * tap_count
    )
    if per_channel:
        output = jnp.einsum("pcnw,cwo->pcno", windows, matrices, preferred_element_type=jnp.float32)
    else:
        output = jnp.einsum("pcnw,wo->pcno", windows, matrices, preferred_element_type=jnp.float32)
    output = output.reshape(pulses, channels, blocks, 2, tap_count)
    return jnp.transpose(output, (3, 0, 1, 2, 4)).reshape(2, pulses, channels, blocks * tap_count)


def local(echoes, beam_angle, interp_table):
    rx_count = lax.axis_size("rx")
    pulse_count = lax.axis_size("pulse")
    rng_place = lax.axis_index("rng")
    rx_place = lax.axis_index("rx")
    pulse_place = lax.axis_index("pulse")
    pulses, channels, length = echoes.shape[1:]
    beam_count = beam_angle.shape[0]
    receivers = channels * rx_count
    channel_ids = rx_place * channels + jnp.arange(channels, dtype=jnp.int32)
    rx_re, rx_im = receiver_taps(channel_ids, RTAPS)
    rx_bands = toeplitz_blocks(rx_re, rx_im)
    chirp_re, chirp_im = chirp_taps(CTAPS)
    chirp_band = toeplitz_blocks(chirp_re, chirp_im)
    extended = extended_2(echoes, (("rng", 3),), RTAPS // 2)
    filtered = block_filter(extended, rx_bands, RTAPS, True).astype(jnp.bfloat16)
    filtered = extended_2(filtered, (("rng", 3),), CTAPS // 2)
    compressed = block_filter(filtered, chirp_band, CTAPS, False).astype(jnp.bfloat16)
    steering_real, steering_imaginary = steering(beam_angle, receivers)
    steer_matrix = jnp.concatenate(
        [
            jnp.concatenate([steering_real, -steering_imaginary], axis=1),
            jnp.concatenate([steering_imaginary, steering_real], axis=1),
        ],
        axis=0,
    )
    arrived = lax.all_to_all(compressed, "rx", split_axis=3, concat_axis=2, tiled=True)
    item_count, recv_count, owned_cols = arrived.shape[1:]
    stacked = jnp.transpose(arrived, (0, 2, 1, 3)).reshape(2 * recv_count, item_count * owned_cols)
    formed = jnp.dot(steer_matrix, stacked, preferred_element_type=jnp.float32)
    picture = formed.reshape(2, beam_count, item_count, owned_cols)
    owned_width = length // rx_count
    positions = (
        rng_place * length + rx_place * owned_width + jnp.arange(owned_width, dtype=jnp.int32)
    )
    for level in range(pulses.bit_length() - 1):
        groups_now = pulses >> level + 1
        node_ids = (pulse_count + pulse_place) * groups_now + jnp.arange(
            groups_now, dtype=jnp.int32
        )
        paired = picture.reshape(2, beam_count, groups_now, 2, owned_width)
        picture = merge_pair(
            paired[:, :, :, 0], paired[:, :, :, 1], node_ids, positions, beam_angle, interp_table
        )
    picture = picture[:, :, 0]
    cross_levels = pulse_count.bit_length() - 1
    piece_width = owned_width // pulse_count
    pieces = picture.reshape(2, beam_count, pulse_count, piece_width)
    spots = positions.reshape(pulse_count, piece_width)
    for level in range(cross_levels):
        parity = jnp.right_shift(pulse_place, level) & 1
        count_now = pieces.shape[2]
        paired = pieces.reshape(2, beam_count, count_now // 2, 2, piece_width)
        kept_half = lax.dynamic_index_in_dim(paired, parity, 3, keepdims=False)
        sent_half = lax.dynamic_index_in_dim(paired, 1 - parity, 3, keepdims=False)
        partner = swapped(sent_half, "pulse", level)
        spot_pairs = spots.reshape(count_now // 2, 2, piece_width)
        spots = lax.dynamic_index_in_dim(spot_pairs, parity, 1, keepdims=False)
        own_part = kept_half.reshape(2, beam_count, -1)
        other_part = partner.reshape(2, beam_count, -1)
        left_image = jnp.where(parity == 0, own_part, other_part)
        right_image = jnp.where(parity == 0, other_part, own_part)
        combine_node_ids = jnp.reshape(
            (pulse_count >> level + 1) + jnp.right_shift(pulse_place, level + 1), (1,)
        )
        merged = merge_pair(
            left_image[:, :, None],
            right_image[:, :, None],
            combine_node_ids,
            spots.reshape(-1),
            beam_angle,
            interp_table,
        )
        flat = merged[:, :, 0]
        pieces = flat.reshape(2, beam_count, count_now // 2, piece_width)
    picture = pieces.reshape(2, beam_count, piece_width)
    return picture


def receiver_bands(receivers):
    t = np.arange(RTAPS, dtype=np.float64)
    window = 0.5 - 0.5 * np.cos(full_turn * (t + 0.5) / RTAPS)
    window = window / np.sqrt(np.sum(window * window))
    angle = full_turn * np.arange(1, receivers + 1)[:, None] * (t - RTAPS // 2) / (4 * RTAPS)
    lane = np.arange(128)
    near = np.where(lane < 64, np.where(lane < 32, 256 + lane, 64 + lane), np.where(lane < 96, 192 + lane, lane))
    row = np.concatenate([128 + lane, near])
    lag = row[:, None] - np.arange(128)[None, :] - (128 - RTAPS // 2)
    pairs = banded(window * np.cos(angle), window * np.sin(angle), lag, RTAPS, 128)
    middle = ((lane >= 32) & (lane < 96))[None, :, None]
    edges = np.where(middle, pairs[:, 384:], pairs[:, 256:384])
    return np.concatenate([pairs[:, :256], edges], axis=1)


def chirp_bands():
    t = np.arange(CTAPS) - CTAPS // 2
    angle = math.pi * ((t * t) % (2 * CTAPS)) / CTAPS
    scale = 1.0 / math.sqrt(CTAPS)
    lag = np.arange(CTAPS + 128)[:, None] - np.arange(128)[None, :]
    return banded(np.cos(angle)[None] * scale, -np.sin(angle)[None] * scale, lag, CTAPS, 128)[0]


def banded(taps_re, taps_im, lag, count, group):
    inside = (lag >= 0) & (lag < count)
    spot = np.clip(lag, 0, count - 1)
    re = np.where(inside, taps_re[:, spot], 0.0)
    im = np.where(inside, taps_im[:, spot], 0.0)
    channels, rows, cols = re.shape
    upper = np.concatenate([re, im], axis=2).reshape(channels, rows // group, 1, group, 2 * cols)
    lower = np.concatenate([-im, re], axis=2).reshape(channels, rows // group, 1, group, 2 * cols)
    both = np.concatenate([upper, lower], axis=2)
    return both.reshape(channels, 2 * rows, 2 * cols).astype(np.float32).astype(ml_dtypes.bfloat16)


def turn(k, scale):
    shifted = k + 128
    quadrant = jnp.bitwise_and(jnp.right_shift(shifted, 8), 3)
    y = (jnp.bitwise_and(shifted, 255) - 128).astype(jnp.float32) * (full_turn / 1024.0)
    z = y * y
    sine = y * (1.0 + z * (-1 / 6 + z * (1 / 120 + z * (-1 / 5040 + z * (1 / 362880)))))
    cosine = 1.0 + z * (-0.5 + z * (1 / 24 + z * (-1 / 720 + z * (1 / 40320))))
    odd = jnp.bitwise_and(quadrant, 1) == 1
    c = jnp.where(odd, sine, cosine)
    s = jnp.where(odd, cosine, sine)
    c = jnp.where(jnp.bitwise_and(quadrant + 1, 2) == 2, -c, c)
    s = jnp.where(quadrant >= 2, -s, s)
    return c * scale, s * scale


def upright(row, size, folded):
    across = lax.broadcasted_iota(jnp.int32, (size, size), 1)
    down = lax.broadcasted_iota(jnp.int32, (size, size), 0)
    if folded:
        down = 8 * jnp.bitwise_and(down, 7) + jnp.right_shift(down, 3)
    spread = jnp.where(across == down, jnp.broadcast_to(row.astype(jnp.float32), (size, size)), 0.0)
    return jnp.sum(spread, axis=1, keepdims=True)


def refold(x):
    return jnp.swapaxes(x.reshape(8, 8, x.shape[1]), 0, 1).reshape(x.shape)


def shift_and_weights(codes):
    shift = jnp.right_shift(codes, 2) - 1
    f = jnp.bitwise_and(codes, 3).astype(jnp.float32) * 0.25
    weights = (
        -f * (f - 1.0) * (f - 2.0) * (1 / 6),
        (f + 1.0) * (f - 1.0) * (f - 2.0) * 0.5,
        -(f + 1.0) * f * (f - 2.0) * 0.5,
        (f + 1.0) * f * (f - 1.0) * (1 / 6),
    )
    return shift, weights


def tap_rows(codes):
    shift, weights = shift_and_weights(codes)
    spread = []
    for d in range(-2, 4):
        row = jnp.zeros(codes.shape, jnp.float32)
        for k in range(4):
            row = jnp.where(shift == d - k + 1, weights[k], row)
        spread.append(row)
    return spread


def interp_pair(codes, size):
    shift, weights = shift_and_weights(codes)
    wide = (size, 2 * size)
    first = lax.broadcasted_iota(jnp.int32, codes.shape, 1) + shift - 1
    gap = lax.broadcasted_iota(jnp.int32, wide, 0) - jnp.broadcast_to(first, wide)
    gap = jnp.bitwise_and(gap, size - 1)
    out = jnp.zeros(wide, jnp.float32)
    for k in range(4):
        out = jnp.where(gap == k, jnp.broadcast_to(weights[k], wide), out)
    turned = jnp.transpose(out)
    halves = [refold(turned[:size]), refold(turned[size:])]
    return jnp.concatenate(halves, axis=0).astype(jnp.bfloat16)


def times(a, b):
    return a[0] * b[0] - a[1] * b[1], a[0] * b[1] + a[1] * b[0]


def times_conj(a, b):
    return a[0] * b[0] + a[1] * b[1], a[1] * b[0] - a[0] * b[1]


def square(a):
    return (a[0] - a[1]) * (a[0] + a[1]), 2.0 * a[0] * a[1]


def choose(flag, a, b):
    return jnp.where(flag, a[0], b[0]), jnp.where(flag, a[1], b[1])


def powers(one, me):
    two = square(one)
    three = times(two, one)
    four = square(two)
    outer = choose(me < 2, three, four)
    more = choose(me < 2, choose(me == 0, one, two), choose(me == 2, three, four))
    inner = times(four, more)
    second = times_conj(square(inner), one)
    first = [times_conj(square(second), one)]
    first.append(times(first[0], two))
    leaf = [times_conj(square(first[0]), one)]
    for _ in range(3):
        leaf.append(times(leaf[-1], two))
    return [one] + leaf + first + [second, inner, outer]


def focus_kernel(
    pulse_count, ech, ang_hbm, tab_hbm, trx_hbm, chp_hbm, out,
    ang, tab, held, edge, wide, filt, trx, chp, phase, form, coef,
    offered, both, sent, got, final,
    near_ok, far_ok, near_sem, halo_sem, offer_send, offer_recv, piece_send, piece_recv,
):
    rx, rng, me = lax.axis_index("rx"), lax.axis_index("rng"), lax.axis_index("pulse")
    beams = ang.shape[1]
    rows, length = ech.shape[1:]
    channels = trx.shape[0]
    pulses = rows // channels
    owned = length // 2
    barrier = pltpu.get_barrier_semaphore()
    for step in range(1, pulse_count):
        far = {"pulse": lax.rem(me + step, pulse_count), "rng": 0}
        pl.semaphore_signal(barrier, inc=1, device_id=far, device_id_type=MESH)
    pl.semaphore_signal(barrier, inc=1, device_id={"rx": 1 - rx, "rng": 1}, device_id_type=MESH)

    @pl.when(rng == 0)
    def _():
        pl.semaphore_signal(barrier, inc=1, device_id={"rng": 1}, device_id_type=MESH)

    tables = [
        pltpu.make_async_copy(ang_hbm, ang, near_sem.at[0]),
        pltpu.make_async_copy(tab_hbm, tab, near_sem.at[1]),
    ]
    echo_in = pltpu.make_async_copy(ech, held, near_sem.at[2])
    chirp_in = pltpu.make_async_copy(chp_hbm, chp, near_sem.at[3])
    bands_in = [
        pltpu.make_async_copy(
            trx_hbm.at[pl.ds(rx * channels + 2 * i, 2)], trx.at[pl.ds(2 * i, 2)], near_sem.at[4 + i]
        )
        for i in range(channels // 2)
    ]
    for copy in tables + [echo_in] + bands_in + [chirp_in]:
        copy.start()

    @pl.when(rng == 0)
    def _():
        wide[:, 2] = jnp.zeros((2, rows, 128), wide.dtype)
        filt[:, :512] = jnp.zeros((rows, 512), filt.dtype)

    @pl.when(rng == 1)
    def _():
        wide[:, 3 + length // 128] = jnp.zeros((2, rows, 128), wide.dtype)
        filt[:, 512 + 2 * length :] = jnp.zeros((rows, 512), filt.dtype)

    for copy in tables:
        copy.wait()
    angle = upright(ang[...], beams, False).astype(jnp.int32)
    folded = upright(ang[...], beams, True).astype(jnp.int32)

    echo_in.wait()
    for part in range(2):
        for spot in range(length // 128):
            wide[part, 3 + spot] = held[part, :, 128 * spot : 128 * spot + 128].astype(jnp.float32)

    lane = lax.broadcasted_iota(jnp.int32, (pulses, 128), 1)
    low = lane < 64
    middle = jnp.logical_and(lane >= 32, lane < 96)

    def filter_pair(pair, start, blocks):
        results = []
        for c in (2 * pair, 2 * pair + 1):
            cells = [
                [
                    wide[part, start + j, pl.ds(c, pulses, stride=channels), :]
                    for j in range(blocks + 2)
                ]
                for part in range(2)
            ]
            left = jnp.concatenate(
                [
                    jnp.concatenate(
                        [
                            cells[0][j + 1],
                            cells[1][j + 1],
                            jnp.where(
                                middle,
                                pltpu.roll(jnp.where(low, cells[1][j + 2], cells[1][j]), 64, 1),
                                jnp.where(low, cells[0][j + 2], cells[0][j]),
                            ),
                        ],
                        axis=1,
                    )
                    for j in range(blocks)
                ],
                axis=0,
            ).astype(jnp.bfloat16)
            results.append(jnp.dot(left, trx[c], preferred_element_type=jnp.float32))
        for j in range(blocks):
            filt[2 * pair * pulses : 2 * (pair + 1) * pulses, pl.ds(pl.multiple_of(256 * (start + j), 256), 256)] = (
                jnp.concatenate([r[8 * j : 8 * j + 8] for r in results], axis=0).astype(jnp.bfloat16)
            )


    @pl.when(rng == 1)
    def _():
        pl.semaphore_wait(barrier, 3)
        pl.semaphore_signal(near_ok, inc=1, device_id={"rng": 0}, device_id_type=MESH)

    @pl.when(rng == 0)
    def _():
        pl.semaphore_wait(near_ok, 1)

    halo = pltpu.make_async_remote_copy(
        src_ref=ech.at[:, :, pl.ds(pl.multiple_of((1 - rng) * (length - EDGE), 128), EDGE)],
        dst_ref=edge,
        send_sem=halo_sem.at[0],
        recv_sem=halo_sem.at[1],
        device_id={"rng": 1 - rng},
        device_id_type=MESH,
    )
    halo.start()
    for pair in range(channels // 2):
        bands_in[pair].wait()
        filter_pair(pair, 2 + rng, length // 128 - 1)

    def turn_of(u):
        k = jnp.where(u < 2, 1, jnp.where(u > 5, 3, jnp.where((u - 3) * (u - 4) == 0, 2, 0)))
        h = jnp.where(u * (u - 4) * (u - 5) * (u - 7) == 0, 1, 0)
        return k, h

    def related(k):
        return jnp.where(
            k == 0,
            lax.rem(me + 2, 4),
            jnp.where(k == 1, 3 - me, jnp.where(k == 2, me + 1 - 2 * lax.rem(me, 2), me)),
        )

    def spot_of(u):
        k, h = turn_of(u)
        return 2 * related(k) + h

    late = (1 - jnp.abs(rx - rng)) * (1 - jnp.abs(lax.div(me, 2) - rng))

    def compress(half, units):
        left = jnp.concatenate(
            [
                filt[:, pl.ds(pl.multiple_of(2 * owned * half + 256 * spot_of(u), 256), 1280)]
                for u in units
            ],
            axis=0,
        )
        made = jnp.dot(left, chp[...], preferred_element_type=jnp.float32)
        made = [made[rows * n : rows * (n + 1)] for n in range(len(units))]
        return [
            jnp.concatenate([x[:, :128], x[:, 128:]], axis=0).astype(jnp.bfloat16) for x in made
        ]

    def offer(u):
        return pltpu.make_async_remote_copy(
            src_ref=offered.at[u],
            dst_ref=both.at[u, rx],
            send_sem=offer_send.at[u],
            recv_sem=offer_recv.at[u],
            device_id={"rx": 1 - rx},
            device_id_type=MESH,
        )

    def give(units):
        for u, block in zip(units, compress(1 - rx, units)):
            offered[u] = block
        for u in units:
            offer(u).start()

    chirp_in.wait()

    @pl.when(late == 0)
    def _():
        give([0, 1])


    halo.wait_recv()
    place = (1 - rng) * (length // 128 + 3)
    for part in range(2):
        for spot in range(3):
            wide[part, place + spot] = edge[part, :, 128 * spot : 128 * spot + 128].astype(jnp.float32)
    for pair in range(channels // 2):
        filter_pair(pair, (1 - rng) * (length // 128 + 1), 3)

    @pl.when(late == 1)
    def _():
        give([0, 1])

    give([2, 3])
    give([4, 5, 6, 7])

    node = [(pulse_count + me) * (pulses >> k + 1) for k in range(3)]
    nodes = [node[k] + i for k in range(3) for i in range(pulses >> k + 1)]
    codes = [tab[pl.ds(2 * n + side, 1), :] for n in nodes for side in range(2)]
    codes += [tab[pl.ds((pulse_count >> k) + jnp.right_shift(me, k), 1), :] for k in range(2)]
    mixers = [
        interp_pair(jnp.concatenate(codes[2 * i : 2 * i + 2], axis=1), beams) for i in range(4)
    ]
    spread = tap_rows(jnp.concatenate(codes[8:], axis=0))
    for m in range(8):
        for d in range(6):
            coef[6 * m + d] = jnp.broadcast_to(
                upright(spread[d][m : m + 1], beams, True), (beams, 128)
            )
    size = (beams, 2 * 2 * channels * pulses)
    column = lax.broadcasted_iota(jnp.int32, size, 1)
    local_channel = jnp.bitwise_and(jnp.right_shift(column, 3), channels - 1)
    receiver = local_channel + channels * jnp.right_shift(column, 7)
    cosine, sine = turn(jnp.bitwise_and(angle * receiver, 1023), 0.25)
    imag = jnp.bitwise_and(jnp.right_shift(column, 6), 1) == 1
    steer = [
        jnp.where(imag, sine, cosine).astype(jnp.bfloat16),
        jnp.where(imag, cosine, -sine).astype(jnp.bfloat16),
    ]
    lane_pulse = jnp.bitwise_and(column, pulses - 1)
    for i in range(pulses // 2):
        for part in range(2):
            mixed = jnp.dot(mixers[i], steer[part], preferred_element_type=jnp.float32)
            for side in range(2):
                p = 2 * i + side
                spot = (2 * p + part) * beams
                form[spot : spot + beams, :] = jnp.where(
                    lane_pulse == p, mixed[side * beams : (side + 1) * beams], 0.0
                ).astype(jnp.bfloat16)


    made = compress(rx, list(range(2 * pulse_count)))
    for u in range(2 * pulse_count):
        both[u, rx] = made[u]

    along = (rng * length + rx * owned) + 1 + lax.broadcasted_iota(jnp.int32, (beams, 128), 1)
    fields = powers(turn(jnp.bitwise_and(folded * along, 1023), 1.0), me)
    steps = powers(
        turn(jnp.bitwise_and(jnp.broadcast_to(folded, (beams, 128)) * 128, 1023), 1.0), me
    )
    for k in range(len(fields)):
        field = fields[k] if k == 0 else (fields[k][0] * half_root, fields[k][1] * half_root)
        for spot in range(2 * pulse_count):
            if spot:
                field = times(field, steps[k])
            phase[spot, k, 0], phase[spot, k, 1] = field

    def piece(u):
        k = 2 if u == 0 else turn_of(u)[0]
        return pltpu.make_async_remote_copy(
            src_ref=sent.at[u],
            dst_ref=got.at[u],
            send_sem=piece_send.at[u],
            recv_sem=piece_recv.at[u],
            device_id={"pulse": related(k)},
            device_id_type=MESH,
        )

    def unit(u, carry):
        spot = spot_of(u)
        offer(u).wait_recv()
        right = jnp.concatenate([both[u, 0], both[u, 1]], axis=0)

        def spun(field, x):
            return times((phase[spot, field, 0], phase[spot, field, 1]), x)

        def joined(field, left_x, right_x):
            moved = spun(0, right_x)
            return spun(field, (left_x[0] + moved[0], left_x[1] + moved[1]))

        def blended(m, x):
            results = []
            for part in range(2):
                rows_of = [x[part][8 * v : 8 * v + 8] for v in range(beams // 8)]
                lined = [pltpu.roll(v, 1, 0) for v in rows_of[-2:]] + rows_of
                lined += [pltpu.roll(v, 7, 0) for v in rows_of[:3]]
                sums = []
                for v in range(beams // 8):
                    terms = [coef[6 * m + d, 8 * v : 8 * v + 8] * lined[v + d] for d in range(6)]
                    sums.append(((terms[0] + terms[1]) + (terms[2] + terms[3])) + (terms[4] + terms[5]))
                results.append(jnp.concatenate(sums, axis=0))
            return results

        images = []
        for g in range(pulses // 2):
            x = jnp.dot(
                form[4 * g * beams : 4 * (g + 1) * beams, :], right, preferred_element_type=jnp.float32
            )
            x = [x[beams * n : beams * (n + 1)] for n in range(4)]
            images.append(blended(g, joined(1 + g, (x[0], x[1]), (x[2], x[3]))))
        images = [joined(5 + g, images[2 * g], images[2 * g + 1]) for g in range(2)]
        picture = joined(7, blended(4, images[0]), blended(5, images[1]))
        picture = spun(8, blended(6, picture))
        re, im = spun(9, blended(7, picture))

        for n in range(6):

            @pl.when(u == n)
            def _():
                x = (re, im)
                if n == 5:
                    piece(0).wait_recv()
                    x = [x[part] + got[0, part].astype(jnp.float32) for part in range(2)]
                sent[n, 0] = x[0].astype(jnp.bfloat16)
                sent[n, 1] = x[1].astype(jnp.bfloat16)
                piece(n).start()

        @pl.when(u > 5)
        def _():
            final[u - 6, 0] = re
            final[u - 6, 1] = im

        return carry


    @pl.when(rng == 0)
    def _():
        pl.semaphore_wait(barrier, 2 * (pulse_count - 1))
        pl.semaphore_signal(far_ok, inc=1, device_id={"rng": 1}, device_id_type=MESH)

    @pl.when(rng == 1)
    def _():
        pl.semaphore_wait(far_ok, 1)

    lax.fori_loop(0, 2 * pulse_count, unit, 0)
    halo.wait_send()
    for u in range(2 * pulse_count):
        offer(u).wait_send()
    total = [[final[h, part] for part in range(2)] for h in range(2)]
    for u in (1, 3, 4, 2, 5):
        h = 1 if u > 3 else 0
        piece(u).wait_recv()
        for part in range(2):
            total[h][part] = total[h][part] + got[u, part].astype(jnp.float32)
    for part in range(2):
        out[part] = jnp.concatenate([refold(total[0][part]), refold(total[1][part])], axis=1)
    for u in range(6):
        piece(u).wait_send()


def fused(echoes, beam_angle, interp_table, pulse_count):
    pulses, channels, length = echoes.shape[1:]
    beams = beam_angle.shape[0]
    receivers = 2 * channels
    rows = pulses * channels
    bands = jnp.asarray(receiver_bands(receivers))
    chirps = jnp.asarray(chirp_bands())
    table = interp_table.reshape(-1, beams)
    bf16, f32 = jnp.bfloat16, jnp.float32
    away = pl.BlockSpec(memory_space=pltpu.HBM)
    operands = (echoes.reshape(2, rows, length), beam_angle.reshape(1, beams), table, bands, chirps)
    return pl.pallas_call(
        functools.partial(focus_kernel, pulse_count),
        out_shape=pltpu.VMEM((2, beams, SPAN), f32),
        in_specs=[away] * 5,
        out_specs=pl.BlockSpec(memory_space=pltpu.VMEM),
        scratch_shapes=[
            pltpu.VMEM((1, beams), jnp.int32),
            pltpu.VMEM(table.shape, jnp.int32),
            pltpu.VMEM((2, rows, length), bf16),
            pltpu.VMEM((2, rows, EDGE), bf16),
            pltpu.VMEM((2, length // 128 + 6, rows, 128), f32),
            pltpu.VMEM((rows, 2 * length + 1024), bf16),
            pltpu.VMEM((channels,) + bands.shape[1:], bf16),
            pltpu.VMEM(chirps.shape, bf16),
            pltpu.VMEM((2 * pulse_count, 10, 2, beams, 128), f32),
            pltpu.VMEM((2 * pulses * beams, 2 * receivers * pulses), bf16),
            pltpu.VMEM((48, beams, 128), f32),
            pltpu.VMEM((2 * pulse_count, 2 * rows, 128), bf16),
            pltpu.VMEM((2 * pulse_count, 2, 2 * rows, 128), bf16),
            pltpu.VMEM((6, 2, beams, 128), bf16),
            pltpu.VMEM((6, 2, beams, 128), bf16),
            pltpu.VMEM((2, 2, beams, 128), f32),
            pltpu.SemaphoreType.REGULAR,
            pltpu.SemaphoreType.REGULAR,
            pltpu.SemaphoreType.DMA((8,)),
            pltpu.SemaphoreType.DMA((2,)),
            pltpu.SemaphoreType.DMA((2 * pulse_count,)),
            pltpu.SemaphoreType.DMA((2 * pulse_count,)),
            pltpu.SemaphoreType.DMA((2 * pulse_count - 2,)),
            pltpu.SemaphoreType.DMA((2 * pulse_count - 2,)),
        ],
        compiler_params=pltpu.CompilerParams(
            collective_id=0, has_side_effects=True, vmem_limit_bytes=50 << 20
        ),
    )(*[pltpu.with_memory_space_constraint(x, pltpu.HBM) for x in operands])


def route(echoes, beam_angle, interp_table):
    pulse_count = lax.axis_size("pulse")
    pulses, channels, length = echoes.shape[1:]
    fits = (
        lax.axis_size("rx") == 2
        and lax.axis_size("rng") == 2
        and pulse_count == 4
        and (pulses, channels, length) == (8, 8, 2 * SPAN * pulse_count)
        and beam_angle.shape[0] == 64
    )
    if fits:
        return fused(echoes, beam_angle, interp_table, pulse_count)
    return local(echoes, beam_angle, interp_table)


def solution(mesh):
    placed = (P(None, ("slab", "pulse"), "rx", "rng"), P(), P())
    return jax.shard_map(
        route,
        mesh=mesh,
        in_specs=placed,
        out_specs=P(None, "slab", ("rng", "rx", "pulse")),
        check_vma=False,
    )
```

```python
import functools
import math

import jax
import ml_dtypes
import jax.numpy as jnp
import numpy as np
from jax import lax
from jax.experimental import pallas as pl
from jax.experimental.pallas import tpu as pltpu
from jax.sharding import PartitionSpec as P

RTAPS = 64
CTAPS = 512


half_root = 0.7071067811865476
full_turn = 2.0 * math.pi
SPAN = 256
EDGE = 384
MESH = pl.DeviceIdType.MESH


def extended_2(block, sides, width):
    for axis, dim in sides:
        count = lax.axis_size(axis)
        forward = [(i, i + 1) for i in range(count - 1)]
        backward = [(target, source) for source, target in forward]
        low = lax.ppermute(
            lax.slice_in_dim(block, block.shape[dim] - width, None, axis=dim), axis, forward
        )
        high = lax.ppermute(lax.slice_in_dim(block, 0, width, axis=dim), axis, backward)
        block = jnp.concatenate([low, block, high], axis=dim)
    return block


def swapped(x, axis, distance):
    return lax.ppermute(x, axis, [(i, i ^ 1 << distance) for i in range(lax.axis_size(axis))])


def receiver_taps(channel_ids, tap_count):
    tap_index = jnp.arange(tap_count, dtype=jnp.float32)
    window = 0.5 - 0.5 * jnp.cos(full_turn * (tap_index + 0.5) / tap_count)
    window = window / jnp.sqrt(jnp.sum(window * window))
    channel = channel_ids.astype(jnp.float32)[:, None] + 1.0
    angle = full_turn * channel * (tap_index - tap_count // 2) / (4 * tap_count)
    return (
        (window * jnp.cos(angle)).astype(jnp.bfloat16),
        (window * jnp.sin(angle)).astype(jnp.bfloat16),
    )


def chirp_taps(tap_count):
    offset = jnp.arange(tap_count, dtype=jnp.int32) - tap_count // 2
    phase_step = jnp.mod(offset * offset, 2 * tap_count).astype(jnp.float32)
    angle = math.pi * phase_step / tap_count
    scale = 1.0 / math.sqrt(tap_count)
    return (
        (jnp.cos(angle) * scale).astype(jnp.bfloat16),
        (-jnp.sin(angle) * scale).astype(jnp.bfloat16),
    )


def steering(beam_angle, receivers):
    channel = jnp.arange(receivers, dtype=jnp.int32)
    turns = jnp.mod(beam_angle[:, None] * channel[None, :], 1024).astype(jnp.float32)
    angle = full_turn * turns / 1024.0
    scale = 1.0 / math.sqrt(receivers)
    return (
        (jnp.cos(angle) * scale).astype(jnp.bfloat16),
        (-jnp.sin(angle) * scale).astype(jnp.bfloat16),
    )


def interp_matrices(codes, beam_count):
    shifted = codes // 4 - 1
    fraction = jnp.mod(codes, 4).astype(jnp.float32) / 4.0
    weights = (
        -fraction * (fraction - 1.0) * (fraction - 2.0) / 6.0,
        (fraction + 1.0) * (fraction - 1.0) * (fraction - 2.0) / 2.0,
        -(fraction + 1.0) * fraction * (fraction - 2.0) / 2.0,
        (fraction + 1.0) * fraction * (fraction - 1.0) / 6.0,
    )
    columns = jnp.arange(beam_count, dtype=jnp.int32)
    matrices = jnp.zeros(codes.shape + (beam_count,), jnp.float32)
    for tap_index in range(4):
        target = jnp.mod(columns + shifted + tap_index - 1, beam_count)
        matrices = matrices + weights[tap_index][..., None] * (target[..., None] == columns).astype(
            jnp.float32
        )
    return matrices


def phases(node_ids, positions, beam_angle, side):
    base = jnp.mod(beam_angle[:, None] * (positions[None, :] + 1), 1024)
    factor = 2 * node_ids + side + 1
    turns = jnp.mod(base[:, None, :] * factor[None, :, None], 1024).astype(jnp.float32)
    angle = full_turn * turns / 1024.0
    return (jnp.cos(angle), jnp.sin(angle))


def side_term(picture, matrices, cosine, sine):
    moved = jnp.einsum("gqa,cagr->cqgr", matrices, picture, precision=lax.Precision.HIGHEST)
    return (cosine * moved[0] - sine * moved[1], sine * moved[0] + cosine * moved[1])


def merge_pair(left_image, right_image, node_ids, positions, beam_angle, interp_table):
    matrices = interp_matrices(
        lax.dynamic_slice_in_dim(interp_table, node_ids[0], node_ids.shape[0]), left_image.shape[1]
    )
    left_cos, left_sin = phases(node_ids, positions, beam_angle, 0)
    right_cos, right_sin = phases(node_ids, positions, beam_angle, 1)
    left_re, left_im = side_term(left_image, matrices[:, 0], left_cos, left_sin)
    right_re, right_im = side_term(right_image, matrices[:, 1], right_cos, right_sin)
    return jnp.stack([(left_re + right_re) * half_root, (left_im + right_im) * half_root])


def toeplitz_blocks(taps_re, taps_im):
    tap_count = taps_re.shape[-1]
    leading = taps_re.shape[:-1]

    def lay_out(taps):
        padded = jnp.concatenate([taps, jnp.zeros(leading + (tap_count + 1,), taps.dtype)], axis=-1)
        tiled = jnp.tile(padded, (1,) * len(leading) + (tap_count,))
        banded = tiled[..., : 2 * tap_count * tap_count].reshape(
            leading + (tap_count, 2 * tap_count)
        )
        return jnp.swapaxes(banded, -1, -2)

    real_band = lay_out(taps_re)
    imag_band = lay_out(taps_im)
    upper = jnp.concatenate([real_band, imag_band], axis=-1)
    lower = jnp.concatenate([-imag_band, real_band], axis=-1)
    return jnp.concatenate([upper, lower], axis=-2)


def block_filter(extended, matrices, tap_count, per_channel):
    pulses, channels, length = extended.shape[1:]
    blocks = length // tap_count - 1
    pieces = extended.reshape(2, pulses, channels, blocks + 1, tap_count)
    windows = jnp.concatenate([pieces[:, :, :, :-1], pieces[:, :, :, 1:]], axis=4)
    windows = jnp.transpose(windows, (1, 2, 3, 0, 4)).reshape(
        pulses, channels, blocks, 4 * tap_count
    )
    if per_channel:
        output = jnp.einsum("pcnw,cwo->pcno", windows, matrices, preferred_element_type=jnp.float32)
    else:
        output = jnp.einsum("pcnw,wo->pcno", windows, matrices, preferred_element_type=jnp.float32)
    output = output.reshape(pulses, channels, blocks, 2, tap_count)
    return jnp.transpose(output, (3, 0, 1, 2, 4)).reshape(2, pulses, channels, blocks * tap_count)


def local(echoes, beam_angle, interp_table):
    rx_count = lax.axis_size("rx")
    pulse_count = lax.axis_size("pulse")
    rng_place = lax.axis_index("rng")
    rx_place = lax.axis_index("rx")
    pulse_place = lax.axis_index("pulse")
    pulses, channels, length = echoes.shape[1:]
    beam_count = beam_angle.shape[0]
    receivers = channels * rx_count
    channel_ids = rx_place * channels + jnp.arange(channels, dtype=jnp.int32)
    rx_re, rx_im = receiver_taps(channel_ids, RTAPS)
    rx_bands = toeplitz_blocks(rx_re, rx_im)
    chirp_re, chirp_im = chirp_taps(CTAPS)
    chirp_band = toeplitz_blocks(chirp_re, chirp_im)
    extended = extended_2(echoes, (("rng", 3),), RTAPS // 2)
    filtered = block_filter(extended, rx_bands, RTAPS, True).astype(jnp.bfloat16)
    filtered = extended_2(filtered, (("rng", 3),), CTAPS // 2)
    compressed = block_filter(filtered, chirp_band, CTAPS, False).astype(jnp.bfloat16)
    steering_real, steering_imaginary = steering(beam_angle, receivers)
    steer_matrix = jnp.concatenate(
        [
            jnp.concatenate([steering_real, -steering_imaginary], axis=1),
            jnp.concatenate([steering_imaginary, steering_real], axis=1),
        ],
        axis=0,
    )
    arrived = lax.all_to_all(compressed, "rx", split_axis=3, concat_axis=2, tiled=True)
    item_count, recv_count, owned_cols = arrived.shape[1:]
    stacked = jnp.transpose(arrived, (0, 2, 1, 3)).reshape(2 * recv_count, item_count * owned_cols)
    formed = jnp.dot(steer_matrix, stacked, preferred_element_type=jnp.float32)
    picture = formed.reshape(2, beam_count, item_count, owned_cols)
    owned_width = length // rx_count
    positions = (
        rng_place * length + rx_place * owned_width + jnp.arange(owned_width, dtype=jnp.int32)
    )
    for level in range(pulses.bit_length() - 1):
        groups_now = pulses >> level + 1
        node_ids = (pulse_count + pulse_place) * groups_now + jnp.arange(
            groups_now, dtype=jnp.int32
        )
        paired = picture.reshape(2, beam_count, groups_now, 2, owned_width)
        picture = merge_pair(
            paired[:, :, :, 0], paired[:, :, :, 1], node_ids, positions, beam_angle, interp_table
        )
    picture = picture[:, :, 0]
    cross_levels = pulse_count.bit_length() - 1
    piece_width = owned_width // pulse_count
    pieces = picture.reshape(2, beam_count, pulse_count, piece_width)
    spots = positions.reshape(pulse_count, piece_width)
    for level in range(cross_levels):
        parity = jnp.right_shift(pulse_place, level) & 1
        count_now = pieces.shape[2]
        paired = pieces.reshape(2, beam_count, count_now // 2, 2, piece_width)
        kept_half = lax.dynamic_index_in_dim(paired, parity, 3, keepdims=False)
        sent_half = lax.dynamic_index_in_dim(paired, 1 - parity, 3, keepdims=False)
        partner = swapped(sent_half, "pulse", level)
        spot_pairs = spots.reshape(count_now // 2, 2, piece_width)
        spots = lax.dynamic_index_in_dim(spot_pairs, parity, 1, keepdims=False)
        own_part = kept_half.reshape(2, beam_count, -1)
        other_part = partner.reshape(2, beam_count, -1)
        left_image = jnp.where(parity == 0, own_part, other_part)
        right_image = jnp.where(parity == 0, other_part, own_part)
        combine_node_ids = jnp.reshape(
            (pulse_count >> level + 1) + jnp.right_shift(pulse_place, level + 1), (1,)
        )
        merged = merge_pair(
            left_image[:, :, None],
            right_image[:, :, None],
            combine_node_ids,
            spots.reshape(-1),
            beam_angle,
            interp_table,
        )
        flat = merged[:, :, 0]
        pieces = flat.reshape(2, beam_count, count_now // 2, piece_width)
    picture = pieces.reshape(2, beam_count, piece_width)
    return picture


def receiver_bands(receivers):
    t = np.arange(RTAPS, dtype=np.float64)
    window = 0.5 - 0.5 * np.cos(full_turn * (t + 0.5) / RTAPS)
    window = window / np.sqrt(np.sum(window * window))
    angle = full_turn * np.arange(1, receivers + 1)[:, None] * (t - RTAPS // 2) / (4 * RTAPS)
    lane = np.arange(128)
    near = np.where(lane < 64, np.where(lane < 32, 256 + lane, 64 + lane), np.where(lane < 96, 192 + lane, lane))
    row = np.concatenate([128 + lane, near])
    lag = row[:, None] - np.arange(128)[None, :] - (128 - RTAPS // 2)
    pairs = banded(window * np.cos(angle), window * np.sin(angle), lag, RTAPS, 128)
    middle = ((lane >= 32) & (lane < 96))[None, :, None]
    edges = np.where(middle, pairs[:, 384:], pairs[:, 256:384])
    return np.concatenate([pairs[:, :256], edges], axis=1)


def chirp_bands():
    t = np.arange(CTAPS) - CTAPS // 2
    angle = math.pi * ((t * t) % (2 * CTAPS)) / CTAPS
    scale = 1.0 / math.sqrt(CTAPS)
    lag = np.arange(CTAPS + 128)[:, None] - np.arange(128)[None, :]
    return banded(np.cos(angle)[None] * scale, -np.sin(angle)[None] * scale, lag, CTAPS, 128)[0]


def banded(taps_re, taps_im, lag, count, group):
    inside = (lag >= 0) & (lag < count)
    spot = np.clip(lag, 0, count - 1)
    re = np.where(inside, taps_re[:, spot], 0.0)
    im = np.where(inside, taps_im[:, spot], 0.0)
    channels, rows, cols = re.shape
    upper = np.concatenate([re, im], axis=2).reshape(channels, rows // group, 1, group, 2 * cols)
    lower = np.concatenate([-im, re], axis=2).reshape(channels, rows // group, 1, group, 2 * cols)
    both = np.concatenate([upper, lower], axis=2)
    return both.reshape(channels, 2 * rows, 2 * cols).astype(np.float32).astype(ml_dtypes.bfloat16)


def turn(k, scale):
    shifted = k + 128
    quadrant = jnp.bitwise_and(jnp.right_shift(shifted, 8), 3)
    y = (jnp.bitwise_and(shifted, 255) - 128).astype(jnp.float32) * (full_turn / 1024.0)
    z = y * y
    sine = y * (1.0 + z * (-1 / 6 + z * (1 / 120 + z * (-1 / 5040 + z * (1 / 362880)))))
    cosine = 1.0 + z * (-0.5 + z * (1 / 24 + z * (-1 / 720 + z * (1 / 40320))))
    odd = jnp.bitwise_and(quadrant, 1) == 1
    c = jnp.where(odd, sine, cosine)
    s = jnp.where(odd, cosine, sine)
    c = jnp.where(jnp.bitwise_and(quadrant + 1, 2) == 2, -c, c)
    s = jnp.where(quadrant >= 2, -s, s)
    return c * scale, s * scale


def upright(row, size, folded):
    across = lax.broadcasted_iota(jnp.int32, (size, size), 1)
    down = lax.broadcasted_iota(jnp.int32, (size, size), 0)
    if folded:
        down = 8 * jnp.bitwise_and(down, 7) + jnp.right_shift(down, 3)
    spread = jnp.where(across == down, jnp.broadcast_to(row.astype(jnp.float32), (size, size)), 0.0)
    return jnp.sum(spread, axis=1, keepdims=True)


def refold(x):
    return jnp.swapaxes(x.reshape(8, 8, x.shape[1]), 0, 1).reshape(x.shape)


def shift_and_weights(codes):
    shift = jnp.right_shift(codes, 2) - 1
    f = jnp.bitwise_and(codes, 3).astype(jnp.float32) * 0.25
    weights = (
        -f * (f - 1.0) * (f - 2.0) * (1 / 6),
        (f + 1.0) * (f - 1.0) * (f - 2.0) * 0.5,
        -(f + 1.0) * f * (f - 2.0) * 0.5,
        (f + 1.0) * f * (f - 1.0) * (1 / 6),
    )
    return shift, weights


def tap_rows(codes):
    shift, weights = shift_and_weights(codes)
    spread = []
    for d in range(-2, 4):
        row = jnp.zeros(codes.shape, jnp.float32)
        for k in range(4):
            row = jnp.where(shift == d - k + 1, weights[k], row)
        spread.append(row)
    return spread


def interp_pair(codes, size):
    shift, weights = shift_and_weights(codes)
    wide = (size, 2 * size)
    first = lax.broadcasted_iota(jnp.int32, codes.shape, 1) + shift - 1
    gap = lax.broadcasted_iota(jnp.int32, wide, 0) - jnp.broadcast_to(first, wide)
    gap = jnp.bitwise_and(gap, size - 1)
    out = jnp.zeros(wide, jnp.float32)
    for k in range(4):
        out = jnp.where(gap == k, jnp.broadcast_to(weights[k], wide), out)
    turned = jnp.transpose(out)
    halves = [refold(turned[:size]), refold(turned[size:])]
    return jnp.concatenate(halves, axis=0).astype(jnp.bfloat16)


def times(a, b):
    return a[0] * b[0] - a[1] * b[1], a[0] * b[1] + a[1] * b[0]


def times_conj(a, b):
    return a[0] * b[0] + a[1] * b[1], a[1] * b[0] - a[0] * b[1]


def square(a):
    return (a[0] - a[1]) * (a[0] + a[1]), 2.0 * a[0] * a[1]


def choose(flag, a, b):
    return jnp.where(flag, a[0], b[0]), jnp.where(flag, a[1], b[1])


def powers(one, me):
    two = square(one)
    three = times(two, one)
    four = square(two)
    outer = choose(me < 2, three, four)
    more = choose(me < 2, choose(me == 0, one, two), choose(me == 2, three, four))
    inner = times(four, more)
    second = times_conj(square(inner), one)
    first = [times_conj(square(second), one)]
    first.append(times(first[0], two))
    leaf = [times_conj(square(first[0]), one)]
    for _ in range(3):
        leaf.append(times(leaf[-1], two))
    return [one] + leaf + first + [second, inner, outer]


def focus_kernel(
    pulse_count, ech, ang_hbm, tab_hbm, trx_hbm, chp_hbm, out,
    ang, tab, held, edge, wide, filt, trx, chp, phase, form, coef,
    offered, both, sent, got, final,
    near_ok, far_ok, near_sem, halo_sem, offer_send, offer_recv, piece_send, piece_recv,
):
    rx, rng, me = lax.axis_index("rx"), lax.axis_index("rng"), lax.axis_index("pulse")
    beams = ang.shape[1]
    rows, length = ech.shape[1:]
    channels = trx.shape[0]
    pulses = rows // channels
    owned = length // 2
    barrier = pltpu.get_barrier_semaphore()
    for step in range(1, pulse_count):
        far = {"pulse": lax.rem(me + step, pulse_count), "rng": 0}
        pl.semaphore_signal(barrier, inc=1, device_id=far, device_id_type=MESH)
    pl.semaphore_signal(barrier, inc=1, device_id={"rx": 1 - rx, "rng": 1}, device_id_type=MESH)

    @pl.when(rng == 0)
    def _():
        pl.semaphore_signal(barrier, inc=1, device_id={"rng": 1}, device_id_type=MESH)

    tables = [
        pltpu.make_async_copy(ang_hbm, ang, near_sem.at[0]),
        pltpu.make_async_copy(tab_hbm, tab, near_sem.at[1]),
    ]
    echo_in = pltpu.make_async_copy(ech, held, near_sem.at[2])
    chirp_in = pltpu.make_async_copy(chp_hbm, chp, near_sem.at[3])
    bands_in = [
        pltpu.make_async_copy(
            trx_hbm.at[pl.ds(rx * channels + 2 * i, 2)], trx.at[pl.ds(2 * i, 2)], near_sem.at[4 + i]
        )
        for i in range(channels // 2)
    ]
    for copy in tables + [echo_in] + bands_in + [chirp_in]:
        copy.start()

    @pl.when(rng == 0)
    def _():
        wide[:, 2] = jnp.zeros((2, rows, 128), wide.dtype)
        filt[:, :512] = jnp.zeros((rows, 512), filt.dtype)

    @pl.when(rng == 1)
    def _():
        wide[:, 3 + length // 128] = jnp.zeros((2, rows, 128), wide.dtype)
        filt[:, 512 + 2 * length :] = jnp.zeros((rows, 512), filt.dtype)

    for copy in tables:
        copy.wait()
    angle = upright(ang[...], beams, False).astype(jnp.int32)
    folded = upright(ang[...], beams, True).astype(jnp.int32)

    echo_in.wait()
    for part in range(2):
        for spot in range(length // 128):
            wide[part, 3 + spot] = held[part, :, 128 * spot : 128 * spot + 128].astype(jnp.float32)

    lane = lax.broadcasted_iota(jnp.int32, (pulses, 128), 1)
    low = lane < 64
    middle = jnp.logical_and(lane >= 32, lane < 96)

    def filter_pair(pair, start, blocks):
        results = []
        for c in (2 * pair, 2 * pair + 1):
            cells = [
                [
                    wide[part, start + j, pl.ds(c, pulses, stride=channels), :]
                    for j in range(blocks + 2)
                ]
                for part in range(2)
            ]
            left = jnp.concatenate(
                [
                    jnp.concatenate(
                        [
                            cells[0][j + 1],
                            cells[1][j + 1],
                            jnp.where(
                                middle,
                                pltpu.roll(jnp.where(low, cells[1][j + 2], cells[1][j]), 64, 1),
                                jnp.where(low, cells[0][j + 2], cells[0][j]),
                            ),
                        ],
                        axis=1,
                    )
                    for j in range(blocks)
                ],
                axis=0,
            ).astype(jnp.bfloat16)
            results.append(jnp.dot(left, trx[c], preferred_element_type=jnp.float32))
        for j in range(blocks):
            filt[2 * pair * pulses : 2 * (pair + 1) * pulses, pl.ds(pl.multiple_of(256 * (start + j), 256), 256)] = (
                jnp.concatenate([r[8 * j : 8 * j + 8] for r in results], axis=0).astype(jnp.bfloat16)
            )


    @pl.when(rng == 1)
    def _():
        pl.semaphore_wait(barrier, 3)
        pl.semaphore_signal(near_ok, inc=1, device_id={"rng": 0}, device_id_type=MESH)

    @pl.when(rng == 0)
    def _():
        pl.semaphore_wait(near_ok, 1)

    halo = pltpu.make_async_remote_copy(
        src_ref=ech.at[:, :, pl.ds(pl.multiple_of((1 - rng) * (length - EDGE), 128), EDGE)],
        dst_ref=edge,
        send_sem=halo_sem.at[0],
        recv_sem=halo_sem.at[1],
        device_id={"rng": 1 - rng},
        device_id_type=MESH,
    )
    halo.start()
    for pair in range(channels // 2):
        bands_in[pair].wait()
        filter_pair(pair, 2 + rng, length // 128 - 1)

    def turn_of(u):
        k = jnp.where(u < 2, 1, jnp.where(u > 5, 3, jnp.where((u - 3) * (u - 4) == 0, 2, 0)))
        h = jnp.where(u * (u - 4) * (u - 5) * (u - 7) == 0, 1, 0)
        return k, h

    def related(k):
        return jnp.where(
            k == 0,
            lax.rem(me + 2, 4),
            jnp.where(k == 1, 3 - me, jnp.where(k == 2, me + 1 - 2 * lax.rem(me, 2), me)),
        )

    def spot_of(u):
        k, h = turn_of(u)
        return 2 * related(k) + h

    late = (1 - jnp.abs(rx - rng)) * (1 - jnp.abs(lax.div(me, 2) - rng))

    def compress(half, units):
        left = jnp.concatenate(
            [
                filt[:, pl.ds(pl.multiple_of(2 * owned * half + 256 * spot_of(u), 256), 1280)]
                for u in units
            ],
            axis=0,
        )
        made = jnp.dot(left, chp[...], preferred_element_type=jnp.float32)
        made = [made[rows * n : rows * (n + 1)] for n in range(len(units))]
        return [
            jnp.concatenate([x[:, :128], x[:, 128:]], axis=0).astype(jnp.bfloat16) for x in made
        ]

    def offer(u):
        return pltpu.make_async_remote_copy(
            src_ref=offered.at[u],
            dst_ref=both.at[u, rx],
            send_sem=offer_send.at[u],
            recv_sem=offer_recv.at[u],
            device_id={"rx": 1 - rx},
            device_id_type=MESH,
        )

    def give(units):
        for u, block in zip(units, compress(1 - rx, units)):
            offered[u] = block
        for u in units:
            offer(u).start()

    chirp_in.wait()

    @pl.when(late == 0)
    def _():
        give([0, 1])


    halo.wait_recv()
    place = (1 - rng) * (length // 128 + 3)
    for part in range(2):
        for spot in range(3):
            wide[part, place + spot] = edge[part, :, 128 * spot : 128 * spot + 128].astype(jnp.float32)
    for pair in range(channels // 2):
        filter_pair(pair, (1 - rng) * (length // 128 + 1), 3)

    @pl.when(late == 1)
    def _():
        give([0, 1])

    give([2, 3])
    give([4, 5, 6, 7])

    node = [(pulse_count + me) * (pulses >> k + 1) for k in range(3)]
    nodes = [node[k] + i for k in range(3) for i in range(pulses >> k + 1)]
    codes = [tab[pl.ds(2 * n + side, 1), :] for n in nodes for side in range(2)]
    codes += [tab[pl.ds((pulse_count >> k) + jnp.right_shift(me, k), 1), :] for k in range(2)]
    mixers = [
        interp_pair(jnp.concatenate(codes[2 * i : 2 * i + 2], axis=1), beams) for i in range(4)
    ]
    spread = tap_rows(jnp.concatenate(codes[8:], axis=0))
    for m in range(8):
        for d in range(6):
            coef[6 * m + d] = jnp.broadcast_to(
                upright(spread[d][m : m + 1], beams, True), (beams, 128)
            )
    size = (beams, 2 * 2 * channels * pulses)
    column = lax.broadcasted_iota(jnp.int32, size, 1)
    local_channel = jnp.bitwise_and(jnp.right_shift(column, 3), channels - 1)
    receiver = local_channel + channels * jnp.right_shift(column, 7)
    cosine, sine = turn(jnp.bitwise_and(angle * receiver, 1023), 0.25)
    imag = jnp.bitwise_and(jnp.right_shift(column, 6), 1) == 1
    steer = jnp.where(imag, -sine, cosine).astype(jnp.bfloat16)
    lane_pulse = jnp.bitwise_and(column, pulses - 1)
    for i in range(pulses // 2):
        mixed = jnp.dot(mixers[i], steer, preferred_element_type=jnp.float32)
        for side in range(2):
            p = 2 * i + side
            form[p * beams : (p + 1) * beams, :] = jnp.where(
                lane_pulse == p, mixed[side * beams : (side + 1) * beams], 0.0
            ).astype(jnp.bfloat16)

    made = compress(rx, list(range(2 * pulse_count)))
    for u in range(2 * pulse_count):
        both[u, rx] = made[u]

    along = (rng * length + rx * owned) + 1 + lax.broadcasted_iota(jnp.int32, (beams, 128), 1)
    fields = powers(turn(jnp.bitwise_and(folded * along, 1023), 1.0), me)
    steps = powers(
        turn(jnp.bitwise_and(jnp.broadcast_to(folded, (beams, 128)) * 128, 1023), 1.0), me
    )
    for k in range(len(fields)):
        field = fields[k] if k == 0 else (fields[k][0] * half_root, fields[k][1] * half_root)
        for spot in range(2 * pulse_count):
            if spot:
                field = times(field, steps[k])
            phase[spot, k, 0], phase[spot, k, 1] = field

    def piece(u):
        k = 2 if u == 0 else turn_of(u)[0]
        return pltpu.make_async_remote_copy(
            src_ref=sent.at[u],
            dst_ref=got.at[u],
            send_sem=piece_send.at[u],
            recv_sem=piece_recv.at[u],
            device_id={"pulse": related(k)},
            device_id_type=MESH,
        )

    def unit(u, carry):
        spot = spot_of(u)
        offer(u).wait_recv()
        blocks_of = []
        for side in range(2):
            re, im = both[u, side, :rows], both[u, side, rows:]
            blocks_of.append(jnp.concatenate([re, im], axis=1))
            blocks_of.append(jnp.concatenate([-im, re], axis=1))
        right = jnp.concatenate(blocks_of, axis=0)

        def spun(field, x):
            return times((phase[spot, field, 0], phase[spot, field, 1]), x)

        def joined(field, left_x, right_x):
            moved = spun(0, right_x)
            return spun(field, (left_x[0] + moved[0], left_x[1] + moved[1]))

        def blended(m, x):
            results = []
            for part in range(2):
                rows_of = [x[part][8 * v : 8 * v + 8] for v in range(beams // 8)]
                lined = [pltpu.roll(v, 1, 0) for v in rows_of[-2:]] + rows_of
                lined += [pltpu.roll(v, 7, 0) for v in rows_of[:3]]
                sums = []
                for v in range(beams // 8):
                    terms = [coef[6 * m + d, 8 * v : 8 * v + 8] * lined[v + d] for d in range(6)]
                    sums.append(((terms[0] + terms[1]) + (terms[2] + terms[3])) + (terms[4] + terms[5]))
                results.append(jnp.concatenate(sums, axis=0))
            return results

        images = []
        for g in range(pulses // 2):
            x = jnp.dot(
                form[2 * g * beams : 2 * (g + 1) * beams, :], right, preferred_element_type=jnp.float32
            )
            left_x, right_x = (x[:beams, :128], x[:beams, 128:]), (x[beams:, :128], x[beams:, 128:])
            images.append(blended(g, joined(1 + g, left_x, right_x)))
        images = [joined(5 + g, images[2 * g], images[2 * g + 1]) for g in range(2)]
        picture = joined(7, blended(4, images[0]), blended(5, images[1]))
        picture = spun(8, blended(6, picture))
        re, im = spun(9, blended(7, picture))

        for n in range(6):

            @pl.when(u == n)
            def _():
                x = (re, im)
                if n == 5:
                    piece(0).wait_recv()
                    x = [x[part] + got[0, part].astype(jnp.float32) for part in range(2)]
                sent[n, 0] = x[0].astype(jnp.bfloat16)
                sent[n, 1] = x[1].astype(jnp.bfloat16)
                piece(n).start()

        @pl.when(u > 5)
        def _():
            final[u - 6, 0] = re
            final[u - 6, 1] = im

        return carry


    @pl.when(rng == 0)
    def _():
        pl.semaphore_wait(barrier, 2 * (pulse_count - 1))
        pl.semaphore_signal(far_ok, inc=1, device_id={"rng": 1}, device_id_type=MESH)

    @pl.when(rng == 1)
    def _():
        pl.semaphore_wait(far_ok, 1)

    lax.fori_loop(0, 2 * pulse_count, unit, 0)
    halo.wait_send()
    for u in range(2 * pulse_count):
        offer(u).wait_send()
    total = [[final[h, part] for part in range(2)] for h in range(2)]
    for u in (1, 3, 4, 2, 5):
        h = 1 if u > 3 else 0
        piece(u).wait_recv()
        for part in range(2):
            total[h][part] = total[h][part] + got[u, part].astype(jnp.float32)
    for part in range(2):
        out[part] = jnp.concatenate([refold(total[0][part]), refold(total[1][part])], axis=1)
    for u in range(6):
        piece(u).wait_send()


def fused(echoes, beam_angle, interp_table, pulse_count):
    pulses, channels, length = echoes.shape[1:]
    beams = beam_angle.shape[0]
    receivers = 2 * channels
    rows = pulses * channels
    bands = jnp.asarray(receiver_bands(receivers))
    chirps = jnp.asarray(chirp_bands())
    table = interp_table.reshape(-1, beams)
    bf16, f32 = jnp.bfloat16, jnp.float32
    away = pl.BlockSpec(memory_space=pltpu.HBM)
    operands = (echoes.reshape(2, rows, length), beam_angle.reshape(1, beams), table, bands, chirps)
    return pl.pallas_call(
        functools.partial(focus_kernel, pulse_count),
        out_shape=pltpu.VMEM((2, beams, SPAN), f32),
        in_specs=[away] * 5,
        out_specs=pl.BlockSpec(memory_space=pltpu.VMEM),
        scratch_shapes=[
            pltpu.VMEM((1, beams), jnp.int32),
            pltpu.VMEM(table.shape, jnp.int32),
            pltpu.VMEM((2, rows, length), bf16),
            pltpu.VMEM((2, rows, EDGE), bf16),
            pltpu.VMEM((2, length // 128 + 6, rows, 128), f32),
            pltpu.VMEM((rows, 2 * length + 1024), bf16),
            pltpu.VMEM((channels,) + bands.shape[1:], bf16),
            pltpu.VMEM(chirps.shape, bf16),
            pltpu.VMEM((2 * pulse_count, 10, 2, beams, 128), f32),
            pltpu.VMEM((pulses * beams, 2 * receivers * pulses), bf16),
            pltpu.VMEM((48, beams, 128), f32),
            pltpu.VMEM((2 * pulse_count, 2 * rows, 128), bf16),
            pltpu.VMEM((2 * pulse_count, 2, 2 * rows, 128), bf16),
            pltpu.VMEM((6, 2, beams, 128), bf16),
            pltpu.VMEM((6, 2, beams, 128), bf16),
            pltpu.VMEM((2, 2, beams, 128), f32),
            pltpu.SemaphoreType.REGULAR,
            pltpu.SemaphoreType.REGULAR,
            pltpu.SemaphoreType.DMA((8,)),
            pltpu.SemaphoreType.DMA((2,)),
            pltpu.SemaphoreType.DMA((2 * pulse_count,)),
            pltpu.SemaphoreType.DMA((2 * pulse_count,)),
            pltpu.SemaphoreType.DMA((2 * pulse_count - 2,)),
            pltpu.SemaphoreType.DMA((2 * pulse_count - 2,)),
        ],
        compiler_params=pltpu.CompilerParams(
            collective_id=0, has_side_effects=True, vmem_limit_bytes=50 << 20
        ),
    )(*[pltpu.with_memory_space_constraint(x, pltpu.HBM) for x in operands])


def route(echoes, beam_angle, interp_table):
    pulse_count = lax.axis_size("pulse")
    pulses, channels, length = echoes.shape[1:]
    fits = (
        lax.axis_size("rx") == 2
        and lax.axis_size("rng") == 2
        and pulse_count == 4
        and (pulses, channels, length) == (8, 8, 2 * SPAN * pulse_count)
        and beam_angle.shape[0] == 64
    )
    if fits:
        return fused(echoes, beam_angle, interp_table, pulse_count)
    return local(echoes, beam_angle, interp_table)


def solution(mesh):
    placed = (P(None, ("slab", "pulse"), "rx", "rng"), P(), P())
    return jax.shard_map(
        route,
        mesh=mesh,
        in_specs=placed,
        out_specs=P(None, "slab", ("rng", "rx", "pulse")),
        check_vma=False,
    )
```

```python
import functools
import math

import jax
import ml_dtypes
import jax.numpy as jnp
import numpy as np
from jax import lax
from jax.experimental import pallas as pl
from jax.experimental.pallas import tpu as pltpu
from jax.sharding import PartitionSpec as P

RTAPS = 64
CTAPS = 512


half_root = 0.7071067811865476
full_turn = 2.0 * math.pi
SPAN = 256
EDGE = 384
MESH = pl.DeviceIdType.MESH


def extended_2(block, sides, width):
    for axis, dim in sides:
        count = lax.axis_size(axis)
        forward = [(i, i + 1) for i in range(count - 1)]
        backward = [(target, source) for source, target in forward]
        low = lax.ppermute(
            lax.slice_in_dim(block, block.shape[dim] - width, None, axis=dim), axis, forward
        )
        high = lax.ppermute(lax.slice_in_dim(block, 0, width, axis=dim), axis, backward)
        block = jnp.concatenate([low, block, high], axis=dim)
    return block


def swapped(x, axis, distance):
    return lax.ppermute(x, axis, [(i, i ^ 1 << distance) for i in range(lax.axis_size(axis))])


def receiver_taps(channel_ids, tap_count):
    tap_index = jnp.arange(tap_count, dtype=jnp.float32)
    window = 0.5 - 0.5 * jnp.cos(full_turn * (tap_index + 0.5) / tap_count)
    window = window / jnp.sqrt(jnp.sum(window * window))
    channel = channel_ids.astype(jnp.float32)[:, None] + 1.0
    angle = full_turn * channel * (tap_index - tap_count // 2) / (4 * tap_count)
    return (
        (window * jnp.cos(angle)).astype(jnp.bfloat16),
        (window * jnp.sin(angle)).astype(jnp.bfloat16),
    )


def chirp_taps(tap_count):
    offset = jnp.arange(tap_count, dtype=jnp.int32) - tap_count // 2
    phase_step = jnp.mod(offset * offset, 2 * tap_count).astype(jnp.float32)
    angle = math.pi * phase_step / tap_count
    scale = 1.0 / math.sqrt(tap_count)
    return (
        (jnp.cos(angle) * scale).astype(jnp.bfloat16),
        (-jnp.sin(angle) * scale).astype(jnp.bfloat16),
    )


def steering(beam_angle, receivers):
    channel = jnp.arange(receivers, dtype=jnp.int32)
    turns = jnp.mod(beam_angle[:, None] * channel[None, :], 1024).astype(jnp.float32)
    angle = full_turn * turns / 1024.0
    scale = 1.0 / math.sqrt(receivers)
    return (
        (jnp.cos(angle) * scale).astype(jnp.bfloat16),
        (-jnp.sin(angle) * scale).astype(jnp.bfloat16),
    )


def interp_matrices(codes, beam_count):
    shifted = codes // 4 - 1
    fraction = jnp.mod(codes, 4).astype(jnp.float32) / 4.0
    weights = (
        -fraction * (fraction - 1.0) * (fraction - 2.0) / 6.0,
        (fraction + 1.0) * (fraction - 1.0) * (fraction - 2.0) / 2.0,
        -(fraction + 1.0) * fraction * (fraction - 2.0) / 2.0,
        (fraction + 1.0) * fraction * (fraction - 1.0) / 6.0,
    )
    columns = jnp.arange(beam_count, dtype=jnp.int32)
    matrices = jnp.zeros(codes.shape + (beam_count,), jnp.float32)
    for tap_index in range(4):
        target = jnp.mod(columns + shifted + tap_index - 1, beam_count)
        matrices = matrices + weights[tap_index][..., None] * (target[..., None] == columns).astype(
            jnp.float32
        )
    return matrices


def phases(node_ids, positions, beam_angle, side):
    base = jnp.mod(beam_angle[:, None] * (positions[None, :] + 1), 1024)
    factor = 2 * node_ids + side + 1
    turns = jnp.mod(base[:, None, :] * factor[None, :, None], 1024).astype(jnp.float32)
    angle = full_turn * turns / 1024.0
    return (jnp.cos(angle), jnp.sin(angle))


def side_term(picture, matrices, cosine, sine):
    moved = jnp.einsum("gqa,cagr->cqgr", matrices, picture, precision=lax.Precision.HIGHEST)
    return (cosine * moved[0] - sine * moved[1], sine * moved[0] + cosine * moved[1])


def merge_pair(left_image, right_image, node_ids, positions, beam_angle, interp_table):
    matrices = interp_matrices(
        lax.dynamic_slice_in_dim(interp_table, node_ids[0], node_ids.shape[0]), left_image.shape[1]
    )
    left_cos, left_sin = phases(node_ids, positions, beam_angle, 0)
    right_cos, right_sin = phases(node_ids, positions, beam_angle, 1)
    left_re, left_im = side_term(left_image, matrices[:, 0], left_cos, left_sin)
    right_re, right_im = side_term(right_image, matrices[:, 1], right_cos, right_sin)
    return jnp.stack([(left_re + right_re) * half_root, (left_im + right_im) * half_root])


def toeplitz_blocks(taps_re, taps_im):
    tap_count = taps_re.shape[-1]
    leading = taps_re.shape[:-1]

    def lay_out(taps):
        padded = jnp.concatenate([taps, jnp.zeros(leading + (tap_count + 1,), taps.dtype)], axis=-1)
        tiled = jnp.tile(padded, (1,) * len(leading) + (tap_count,))
        banded = tiled[..., : 2 * tap_count * tap_count].reshape(
            leading + (tap_count, 2 * tap_count)
        )
        return jnp.swapaxes(banded, -1, -2)

    real_band = lay_out(taps_re)
    imag_band = lay_out(taps_im)
    upper = jnp.concatenate([real_band, imag_band], axis=-1)
    lower = jnp.concatenate([-imag_band, real_band], axis=-1)
    return jnp.concatenate([upper, lower], axis=-2)


def block_filter(extended, matrices, tap_count, per_channel):
    pulses, channels, length = extended.shape[1:]
    blocks = length // tap_count - 1
    pieces = extended.reshape(2, pulses, channels, blocks + 1, tap_count)
    windows = jnp.concatenate([pieces[:, :, :, :-1], pieces[:, :, :, 1:]], axis=4)
    windows = jnp.transpose(windows, (1, 2, 3, 0, 4)).reshape(
        pulses, channels, blocks, 4 * tap_count
    )
    if per_channel:
        output = jnp.einsum("pcnw,cwo->pcno", windows, matrices, preferred_element_type=jnp.float32)
    else:
        output = jnp.einsum("pcnw,wo->pcno", windows, matrices, preferred_element_type=jnp.float32)
    output = output.reshape(pulses, channels, blocks, 2, tap_count)
    return jnp.transpose(output, (3, 0, 1, 2, 4)).reshape(2, pulses, channels, blocks * tap_count)


def local(echoes, beam_angle, interp_table):
    rx_count = lax.axis_size("rx")
    pulse_count = lax.axis_size("pulse")
    rng_place = lax.axis_index("rng")
    rx_place = lax.axis_index("rx")
    pulse_place = lax.axis_index("pulse")
    pulses, channels, length = echoes.shape[1:]
    beam_count = beam_angle.shape[0]
    receivers = channels * rx_count
    channel_ids = rx_place * channels + jnp.arange(channels, dtype=jnp.int32)
    rx_re, rx_im = receiver_taps(channel_ids, RTAPS)
    rx_bands = toeplitz_blocks(rx_re, rx_im)
    chirp_re, chirp_im = chirp_taps(CTAPS)
    chirp_band = toeplitz_blocks(chirp_re, chirp_im)
    extended = extended_2(echoes, (("rng", 3),), RTAPS // 2)
    filtered = block_filter(extended, rx_bands, RTAPS, True).astype(jnp.bfloat16)
    filtered = extended_2(filtered, (("rng", 3),), CTAPS // 2)
    compressed = block_filter(filtered, chirp_band, CTAPS, False).astype(jnp.bfloat16)
    steering_real, steering_imaginary = steering(beam_angle, receivers)
    steer_matrix = jnp.concatenate(
        [
            jnp.concatenate([steering_real, -steering_imaginary], axis=1),
            jnp.concatenate([steering_imaginary, steering_real], axis=1),
        ],
        axis=0,
    )
    arrived = lax.all_to_all(compressed, "rx", split_axis=3, concat_axis=2, tiled=True)
    item_count, recv_count, owned_cols = arrived.shape[1:]
    stacked = jnp.transpose(arrived, (0, 2, 1, 3)).reshape(2 * recv_count, item_count * owned_cols)
    formed = jnp.dot(steer_matrix, stacked, preferred_element_type=jnp.float32)
    picture = formed.reshape(2, beam_count, item_count, owned_cols)
    owned_width = length // rx_count
    positions = (
        rng_place * length + rx_place * owned_width + jnp.arange(owned_width, dtype=jnp.int32)
    )
    for level in range(pulses.bit_length() - 1):
        groups_now = pulses >> level + 1
        node_ids = (pulse_count + pulse_place) * groups_now + jnp.arange(
            groups_now, dtype=jnp.int32
        )
        paired = picture.reshape(2, beam_count, groups_now, 2, owned_width)
        picture = merge_pair(
            paired[:, :, :, 0], paired[:, :, :, 1], node_ids, positions, beam_angle, interp_table
        )
    picture = picture[:, :, 0]
    cross_levels = pulse_count.bit_length() - 1
    piece_width = owned_width // pulse_count
    pieces = picture.reshape(2, beam_count, pulse_count, piece_width)
    spots = positions.reshape(pulse_count, piece_width)
    for level in range(cross_levels):
        parity = jnp.right_shift(pulse_place, level) & 1
        count_now = pieces.shape[2]
        paired = pieces.reshape(2, beam_count, count_now // 2, 2, piece_width)
        kept_half = lax.dynamic_index_in_dim(paired, parity, 3, keepdims=False)
        sent_half = lax.dynamic_index_in_dim(paired, 1 - parity, 3, keepdims=False)
        partner = swapped(sent_half, "pulse", level)
        spot_pairs = spots.reshape(count_now // 2, 2, piece_width)
        spots = lax.dynamic_index_in_dim(spot_pairs, parity, 1, keepdims=False)
        own_part = kept_half.reshape(2, beam_count, -1)
        other_part = partner.reshape(2, beam_count, -1)
        left_image = jnp.where(parity == 0, own_part, other_part)
        right_image = jnp.where(parity == 0, other_part, own_part)
        combine_node_ids = jnp.reshape(
            (pulse_count >> level + 1) + jnp.right_shift(pulse_place, level + 1), (1,)
        )
        merged = merge_pair(
            left_image[:, :, None],
            right_image[:, :, None],
            combine_node_ids,
            spots.reshape(-1),
            beam_angle,
            interp_table,
        )
        flat = merged[:, :, 0]
        pieces = flat.reshape(2, beam_count, count_now // 2, piece_width)
    picture = pieces.reshape(2, beam_count, piece_width)
    return picture


def receiver_bands(receivers):
    t = np.arange(RTAPS, dtype=np.float64)
    window = 0.5 - 0.5 * np.cos(full_turn * (t + 0.5) / RTAPS)
    window = window / np.sqrt(np.sum(window * window))
    angle = full_turn * np.arange(1, receivers + 1)[:, None] * (t - RTAPS // 2) / (4 * RTAPS)
    lane = np.arange(128)
    near = np.where(lane < 64, np.where(lane < 32, 256 + lane, 64 + lane), np.where(lane < 96, 192 + lane, lane))
    row = np.concatenate([128 + lane, near])
    lag = row[:, None] - np.arange(128)[None, :] - (128 - RTAPS // 2)
    pairs = banded(window * np.cos(angle), window * np.sin(angle), lag, RTAPS, 128)
    middle = ((lane >= 32) & (lane < 96))[None, :, None]
    edges = np.where(middle, pairs[:, 384:], pairs[:, 256:384])
    return np.concatenate([pairs[:, :256], edges], axis=1)


def chirp_bands():
    t = np.arange(CTAPS) - CTAPS // 2
    angle = math.pi * ((t * t) % (2 * CTAPS)) / CTAPS
    scale = 1.0 / math.sqrt(CTAPS)
    lag = np.arange(CTAPS + 128)[:, None] - np.arange(128)[None, :]
    return banded(np.cos(angle)[None] * scale, -np.sin(angle)[None] * scale, lag, CTAPS, 128)[0]


def banded(taps_re, taps_im, lag, count, group):
    inside = (lag >= 0) & (lag < count)
    spot = np.clip(lag, 0, count - 1)
    re = np.where(inside, taps_re[:, spot], 0.0)
    im = np.where(inside, taps_im[:, spot], 0.0)
    channels, rows, cols = re.shape
    upper = np.concatenate([re, im], axis=2).reshape(channels, rows // group, 1, group, 2 * cols)
    lower = np.concatenate([-im, re], axis=2).reshape(channels, rows // group, 1, group, 2 * cols)
    both = np.concatenate([upper, lower], axis=2)
    return both.reshape(channels, 2 * rows, 2 * cols).astype(np.float32).astype(ml_dtypes.bfloat16)


def turn(k, scale):
    shifted = k + 128
    quadrant = jnp.bitwise_and(jnp.right_shift(shifted, 8), 3)
    y = (jnp.bitwise_and(shifted, 255) - 128).astype(jnp.float32) * (full_turn / 1024.0)
    z = y * y
    sine = y * (1.0 + z * (-1 / 6 + z * (1 / 120 + z * (-1 / 5040 + z * (1 / 362880)))))
    cosine = 1.0 + z * (-0.5 + z * (1 / 24 + z * (-1 / 720 + z * (1 / 40320))))
    odd = jnp.bitwise_and(quadrant, 1) == 1
    c = jnp.where(odd, sine, cosine)
    s = jnp.where(odd, cosine, sine)
    c = jnp.where(jnp.bitwise_and(quadrant + 1, 2) == 2, -c, c)
    s = jnp.where(quadrant >= 2, -s, s)
    return c * scale, s * scale


def upright(row, size, folded):
    across = lax.broadcasted_iota(jnp.int32, (size, size), 1)
    down = lax.broadcasted_iota(jnp.int32, (size, size), 0)
    if folded:
        down = 8 * jnp.bitwise_and(down, 7) + jnp.right_shift(down, 3)
    spread = jnp.where(across == down, jnp.broadcast_to(row.astype(jnp.float32), (size, size)), 0.0)
    return jnp.sum(spread, axis=1, keepdims=True)


def refold(x):
    return jnp.swapaxes(x.reshape(8, 8, x.shape[1]), 0, 1).reshape(x.shape)


def shift_and_weights(codes):
    shift = jnp.right_shift(codes, 2) - 1
    f = jnp.bitwise_and(codes, 3).astype(jnp.float32) * 0.25
    weights = (
        -f * (f - 1.0) * (f - 2.0) * (1 / 6),
        (f + 1.0) * (f - 1.0) * (f - 2.0) * 0.5,
        -(f + 1.0) * f * (f - 2.0) * 0.5,
        (f + 1.0) * f * (f - 1.0) * (1 / 6),
    )
    return shift, weights


def tap_rows(codes):
    shift, weights = shift_and_weights(codes)
    spread = []
    for d in range(-2, 4):
        row = jnp.zeros(codes.shape, jnp.float32)
        for k in range(4):
            row = jnp.where(shift == d - k + 1, weights[k], row)
        spread.append(row)
    return spread


def interp_pair(codes, size):
    shift, weights = shift_and_weights(codes)
    wide = (size, 2 * size)
    first = lax.broadcasted_iota(jnp.int32, codes.shape, 1) + shift - 1
    gap = lax.broadcasted_iota(jnp.int32, wide, 0) - jnp.broadcast_to(first, wide)
    gap = jnp.bitwise_and(gap, size - 1)
    out = jnp.zeros(wide, jnp.float32)
    for k in range(4):
        out = jnp.where(gap == k, jnp.broadcast_to(weights[k], wide), out)
    turned = jnp.transpose(out)
    halves = [refold(turned[:size]), refold(turned[size:])]
    return jnp.concatenate(halves, axis=0).astype(jnp.bfloat16)


def times(a, b):
    return a[0] * b[0] - a[1] * b[1], a[0] * b[1] + a[1] * b[0]


def times_conj(a, b):
    return a[0] * b[0] + a[1] * b[1], a[1] * b[0] - a[0] * b[1]


def square(a):
    return (a[0] - a[1]) * (a[0] + a[1]), 2.0 * a[0] * a[1]


def choose(flag, a, b):
    return jnp.where(flag, a[0], b[0]), jnp.where(flag, a[1], b[1])


def powers(one, me):
    two = square(one)
    three = times(two, one)
    four = square(two)
    outer = choose(me < 2, three, four)
    more = choose(me < 2, choose(me == 0, one, two), choose(me == 2, three, four))
    inner = times(four, more)
    second = times_conj(square(inner), one)
    first = [times_conj(square(second), one)]
    first.append(times(first[0], two))
    leaf = [times_conj(square(first[0]), one)]
    for _ in range(3):
        leaf.append(times(leaf[-1], two))
    return [one] + leaf + first + [second, inner, outer]


def focus_kernel(
    pulse_count, ech, ang_hbm, tab_hbm, trx_hbm, chp_hbm, out,
    ang, tab, held, edge, wide, filt, trx, chp, phase, form, coef,
    offered, both, sent, got, final,
    near_ok, far_ok, near_sem, halo_sem, offer_send, offer_recv, piece_send, piece_recv,
):
    rx, rng, me = lax.axis_index("rx"), lax.axis_index("rng"), lax.axis_index("pulse")
    beams = ang.shape[1]
    rows, length = ech.shape[1:]
    channels = trx.shape[0]
    pulses = rows // channels
    owned = length // 2
    barrier = pltpu.get_barrier_semaphore()
    for step in range(1, pulse_count):
        far = {"pulse": lax.rem(me + step, pulse_count), "rng": 0}
        pl.semaphore_signal(barrier, inc=1, device_id=far, device_id_type=MESH)
    pl.semaphore_signal(barrier, inc=1, device_id={"rx": 1 - rx, "rng": 1}, device_id_type=MESH)

    @pl.when(rng == 0)
    def _():
        pl.semaphore_signal(barrier, inc=1, device_id={"rng": 1}, device_id_type=MESH)

    tables = [
        pltpu.make_async_copy(ang_hbm, ang, near_sem.at[0]),
        pltpu.make_async_copy(tab_hbm, tab, near_sem.at[1]),
    ]
    echo_in = pltpu.make_async_copy(ech, held, near_sem.at[2])
    chirp_in = pltpu.make_async_copy(chp_hbm, chp, near_sem.at[3])
    bands_in = [
        pltpu.make_async_copy(
            trx_hbm.at[pl.ds(rx * channels + 2 * i, 2)], trx.at[pl.ds(2 * i, 2)], near_sem.at[4 + i]
        )
        for i in range(channels // 2)
    ]
    for copy in tables + [echo_in] + bands_in + [chirp_in]:
        copy.start()

    @pl.when(rng == 0)
    def _():
        wide[:, 2] = jnp.zeros((2, rows, 128), wide.dtype)
        filt[:, :512] = jnp.zeros((rows, 512), filt.dtype)

    @pl.when(rng == 1)
    def _():
        wide[:, 3 + length // 128] = jnp.zeros((2, rows, 128), wide.dtype)
        filt[:, 512 + 2 * length :] = jnp.zeros((rows, 512), filt.dtype)

    for copy in tables:
        copy.wait()
    angle = upright(ang[...], beams, False).astype(jnp.int32)
    folded = upright(ang[...], beams, True).astype(jnp.int32)

    echo_in.wait()
    for part in range(2):
        for spot in range(length // 128):
            wide[part, 3 + spot] = held[part, :, 128 * spot : 128 * spot + 128].astype(jnp.float32)

    lane = lax.broadcasted_iota(jnp.int32, (pulses, 128), 1)
    low = lane < 64
    middle = jnp.logical_and(lane >= 32, lane < 96)

    def filter_pair(pair, start, blocks):
        results = []
        for c in (2 * pair, 2 * pair + 1):
            cells = [
                [
                    wide[part, start + j, pl.ds(c, pulses, stride=channels), :]
                    for j in range(blocks + 2)
                ]
                for part in range(2)
            ]
            left = jnp.concatenate(
                [
                    jnp.concatenate(
                        [
                            cells[0][j + 1],
                            cells[1][j + 1],
                            jnp.where(
                                middle,
                                pltpu.roll(jnp.where(low, cells[1][j + 2], cells[1][j]), 64, 1),
                                jnp.where(low, cells[0][j + 2], cells[0][j]),
                            ),
                        ],
                        axis=1,
                    )
                    for j in range(blocks)
                ],
                axis=0,
            ).astype(jnp.bfloat16)
            results.append(jnp.dot(left, trx[c], preferred_element_type=jnp.float32))
        for j in range(blocks):
            filt[2 * pair * pulses : 2 * (pair + 1) * pulses, pl.ds(pl.multiple_of(256 * (start + j), 256), 256)] = (
                jnp.concatenate([r[8 * j : 8 * j + 8] for r in results], axis=0).astype(jnp.bfloat16)
            )


    @pl.when(rng == 1)
    def _():
        pl.semaphore_wait(barrier, 3)
        pl.semaphore_signal(near_ok, inc=1, device_id={"rng": 0}, device_id_type=MESH)

    @pl.when(rng == 0)
    def _():
        pl.semaphore_wait(near_ok, 1)

    halo = pltpu.make_async_remote_copy(
        src_ref=ech.at[:, :, pl.ds(pl.multiple_of((1 - rng) * (length - EDGE), 128), EDGE)],
        dst_ref=edge,
        send_sem=halo_sem.at[0],
        recv_sem=halo_sem.at[1],
        device_id={"rng": 1 - rng},
        device_id_type=MESH,
    )
    halo.start()
    for pair in range(channels // 2):
        bands_in[pair].wait()
        filter_pair(pair, 2 + rng, length // 128 - 1)

    def turn_of(u):
        k = jnp.where(u * (u - 2) == 0, 1, jnp.where(u > 5, 3, jnp.where((u - 3) * (u - 4) == 0, 2, 0)))
        h = jnp.where(u * (u - 4) * (u - 5) * (u - 7) == 0, 1, 0)
        return k, h

    def related(k):
        return jnp.where(
            k == 0,
            lax.rem(me + 2, 4),
            jnp.where(k == 1, 3 - me, jnp.where(k == 2, me + 1 - 2 * lax.rem(me, 2), me)),
        )

    def spot_of(u):
        k, h = turn_of(u)
        return 2 * related(k) + h

    late = (1 - jnp.abs(rx - rng)) * (1 - jnp.abs(lax.div(me, 2) - rng))

    def compress(half, units):
        left = jnp.concatenate(
            [
                filt[:, pl.ds(pl.multiple_of(2 * owned * half + 256 * spot_of(u), 256), 1280)]
                for u in units
            ],
            axis=0,
        )
        made = jnp.dot(left, chp[...], preferred_element_type=jnp.float32)
        made = [made[rows * n : rows * (n + 1)] for n in range(len(units))]
        return [
            jnp.concatenate([x[:, :128], x[:, 128:]], axis=0).astype(jnp.bfloat16) for x in made
        ]

    def offer(u):
        return pltpu.make_async_remote_copy(
            src_ref=offered.at[u],
            dst_ref=both.at[u, rx],
            send_sem=offer_send.at[u],
            recv_sem=offer_recv.at[u],
            device_id={"rx": 1 - rx},
            device_id_type=MESH,
        )

    def give(units):
        for u, block in zip(units, compress(1 - rx, units)):
            offered[u] = block
        for u in units:
            offer(u).start()

    chirp_in.wait()

    @pl.when(late == 0)
    def _():
        give([0, 1])


    halo.wait_recv()
    place = (1 - rng) * (length // 128 + 3)
    for part in range(2):
        for spot in range(3):
            wide[part, place + spot] = edge[part, :, 128 * spot : 128 * spot + 128].astype(jnp.float32)
    for pair in range(channels // 2):
        filter_pair(pair, (1 - rng) * (length // 128 + 1), 3)

    @pl.when(late == 1)
    def _():
        give([0, 1])

    give([2, 3])
    give([4, 5, 6, 7])

    node = [(pulse_count + me) * (pulses >> k + 1) for k in range(3)]
    nodes = [node[k] + i for k in range(3) for i in range(pulses >> k + 1)]
    codes = [tab[pl.ds(2 * n + side, 1), :] for n in nodes for side in range(2)]
    codes += [tab[pl.ds((pulse_count >> k) + jnp.right_shift(me, k), 1), :] for k in range(2)]
    mixers = [
        interp_pair(jnp.concatenate(codes[2 * i : 2 * i + 2], axis=1), beams) for i in range(4)
    ]
    spread = tap_rows(jnp.concatenate(codes[8:], axis=0))
    for m in range(8):
        for d in range(6):
            coef[6 * m + d] = jnp.broadcast_to(
                upright(spread[d][m : m + 1], beams, True), (beams, 128)
            )
    size = (beams, 2 * 2 * channels * pulses)
    column = lax.broadcasted_iota(jnp.int32, size, 1)
    local_channel = jnp.bitwise_and(jnp.right_shift(column, 3), channels - 1)
    receiver = local_channel + channels * jnp.right_shift(column, 7)
    cosine, sine = turn(jnp.bitwise_and(angle * receiver, 1023), 0.25)
    imag = jnp.bitwise_and(jnp.right_shift(column, 6), 1) == 1
    steer = jnp.where(imag, -sine, cosine).astype(jnp.bfloat16)
    lane_pulse = jnp.bitwise_and(column, pulses - 1)
    for i in range(pulses // 2):
        mixed = jnp.dot(mixers[i], steer, preferred_element_type=jnp.float32)
        for side in range(2):
            p = 2 * i + side
            form[p * beams : (p + 1) * beams, :] = jnp.where(
                lane_pulse == p, mixed[side * beams : (side + 1) * beams], 0.0
            ).astype(jnp.bfloat16)

    made = compress(rx, list(range(2 * pulse_count)))
    for u in range(2 * pulse_count):
        both[u, rx] = made[u]

    along = (rng * length + rx * owned) + 1 + lax.broadcasted_iota(jnp.int32, (beams, 128), 1)
    fields = powers(turn(jnp.bitwise_and(folded * along, 1023), 1.0), me)
    steps = powers(
        turn(jnp.bitwise_and(jnp.broadcast_to(folded, (beams, 128)) * 128, 1023), 1.0), me
    )
    for k in range(len(fields)):
        field = fields[k] if k == 0 else (fields[k][0] * half_root, fields[k][1] * half_root)
        for spot in range(2 * pulse_count):
            if spot:
                field = times(field, steps[k])
            phase[spot, k, 0], phase[spot, k, 1] = field

    def piece(u):
        k = jnp.where(u == 0, 2, turn_of(u)[0])
        return pltpu.make_async_remote_copy(
            src_ref=sent.at[u],
            dst_ref=got.at[u],
            send_sem=piece_send.at[u],
            recv_sem=piece_recv.at[u],
            device_id={"pulse": related(k)},
            device_id_type=MESH,
        )

    def unit(u, carry):
        spot = spot_of(u)
        offer(u).wait_recv()
        blocks_of = []
        for side in range(2):
            re, im = both[u, side, :rows], both[u, side, rows:]
            blocks_of.append(jnp.concatenate([re, im], axis=1))
            blocks_of.append(jnp.concatenate([-im, re], axis=1))
        right = jnp.concatenate(blocks_of, axis=0)

        def spun(field, x):
            return times((phase[spot, field, 0], phase[spot, field, 1]), x)

        def joined(field, left_x, right_x):
            moved = spun(0, right_x)
            return spun(field, (left_x[0] + moved[0], left_x[1] + moved[1]))

        def blended(m, x):
            results = []
            for part in range(2):
                rows_of = [x[part][8 * v : 8 * v + 8] for v in range(beams // 8)]
                lined = [pltpu.roll(v, 1, 0) for v in rows_of[-2:]] + rows_of
                lined += [pltpu.roll(v, 7, 0) for v in rows_of[:3]]
                sums = []
                for v in range(beams // 8):
                    terms = [coef[6 * m + d, 8 * v : 8 * v + 8] * lined[v + d] for d in range(6)]
                    sums.append(((terms[0] + terms[1]) + (terms[2] + terms[3])) + (terms[4] + terms[5]))
                results.append(jnp.concatenate(sums, axis=0))
            return results

        images = []
        for g in range(pulses // 2):
            x = jnp.dot(
                form[2 * g * beams : 2 * (g + 1) * beams, :], right, preferred_element_type=jnp.float32
            )
            left_x, right_x = (x[:beams, :128], x[:beams, 128:]), (x[beams:, :128], x[beams:, 128:])
            images.append(blended(g, joined(1 + g, left_x, right_x)))
        images = [joined(5 + g, images[2 * g], images[2 * g + 1]) for g in range(2)]
        picture = joined(7, blended(4, images[0]), blended(5, images[1]))
        picture = spun(8, blended(6, picture))
        re, im = spun(9, blended(7, picture))

        @pl.when(u < 5)
        def _():
            sent[u, 0] = re.astype(jnp.bfloat16)
            sent[u, 1] = im.astype(jnp.bfloat16)
            piece(u).start()

        @pl.when(u == 5)
        def _():
            piece(0).wait_recv()
            sent[5, 0] = (re + got[0, 0].astype(jnp.float32)).astype(jnp.bfloat16)
            sent[5, 1] = (im + got[0, 1].astype(jnp.float32)).astype(jnp.bfloat16)
            piece(5).start()

        @pl.when(u > 5)
        def _():
            final[u - 6, 0] = re
            final[u - 6, 1] = im

        return carry


    @pl.when(rng == 0)
    def _():
        pl.semaphore_wait(barrier, 2 * (pulse_count - 1))
        pl.semaphore_signal(far_ok, inc=1, device_id={"rng": 1}, device_id_type=MESH)

    @pl.when(rng == 1)
    def _():
        pl.semaphore_wait(far_ok, 1)

    lax.fori_loop(0, 2 * pulse_count, unit, 0)
    halo.wait_send()
    for u in range(2 * pulse_count):
        offer(u).wait_send()
    for u in range(5):
        piece(u).wait_send()
    for h, parts in enumerate(((2, 3, 1), (4, 5))):
        total = [final[h, part] for part in range(2)]
        for u in parts:
            piece(u).wait_recv()
            for part in range(2):
                total[part] = total[part] + got[u, part].astype(jnp.float32)
        for part in range(2):
            out[part, :, 128 * h : 128 * h + 128] = refold(total[part])
    piece(5).wait_send()


def fused(echoes, beam_angle, interp_table, pulse_count):
    pulses, channels, length = echoes.shape[1:]
    beams = beam_angle.shape[0]
    receivers = 2 * channels
    rows = pulses * channels
    bands = jnp.asarray(receiver_bands(receivers))
    chirps = jnp.asarray(chirp_bands())
    table = interp_table.reshape(-1, beams)
    bf16, f32 = jnp.bfloat16, jnp.float32
    away = pl.BlockSpec(memory_space=pltpu.HBM)
    operands = (echoes.reshape(2, rows, length), beam_angle.reshape(1, beams), table, bands, chirps)
    return pl.pallas_call(
        functools.partial(focus_kernel, pulse_count),
        out_shape=pltpu.VMEM((2, beams, SPAN), f32),
        in_specs=[away] * 5,
        out_specs=pl.BlockSpec(memory_space=pltpu.VMEM),
        scratch_shapes=[
            pltpu.VMEM((1, beams), jnp.int32),
            pltpu.VMEM(table.shape, jnp.int32),
            pltpu.VMEM((2, rows, length), bf16),
            pltpu.VMEM((2, rows, EDGE), bf16),
            pltpu.VMEM((2, length // 128 + 6, rows, 128), f32),
            pltpu.VMEM((rows, 2 * length + 1024), bf16),
            pltpu.VMEM((channels,) + bands.shape[1:], bf16),
            pltpu.VMEM(chirps.shape, bf16),
            pltpu.VMEM((2 * pulse_count, 10, 2, beams, 128), f32),
            pltpu.VMEM((pulses * beams, 2 * receivers * pulses), bf16),
            pltpu.VMEM((48, beams, 128), f32),
            pltpu.VMEM((2 * pulse_count, 2 * rows, 128), bf16),
            pltpu.VMEM((2 * pulse_count, 2, 2 * rows, 128), bf16),
            pltpu.VMEM((6, 2, beams, 128), bf16),
            pltpu.VMEM((6, 2, beams, 128), bf16),
            pltpu.VMEM((2, 2, beams, 128), f32),
            pltpu.SemaphoreType.REGULAR,
            pltpu.SemaphoreType.REGULAR,
            pltpu.SemaphoreType.DMA((8,)),
            pltpu.SemaphoreType.DMA((2,)),
            pltpu.SemaphoreType.DMA((2 * pulse_count,)),
            pltpu.SemaphoreType.DMA((2 * pulse_count,)),
            pltpu.SemaphoreType.DMA((2 * pulse_count - 2,)),
            pltpu.SemaphoreType.DMA((2 * pulse_count - 2,)),
        ],
        compiler_params=pltpu.CompilerParams(
            collective_id=0, has_side_effects=True, vmem_limit_bytes=50 << 20
        ),
    )(*[pltpu.with_memory_space_constraint(x, pltpu.HBM) for x in operands])


def route(echoes, beam_angle, interp_table):
    pulse_count = lax.axis_size("pulse")
    pulses, channels, length = echoes.shape[1:]
    fits = (
        lax.axis_size("rx") == 2
        and lax.axis_size("rng") == 2
        and pulse_count == 4
        and (pulses, channels, length) == (8, 8, 2 * SPAN * pulse_count)
        and beam_angle.shape[0] == 64
    )
    if fits:
        return fused(echoes, beam_angle, interp_table, pulse_count)
    return local(echoes, beam_angle, interp_table)


def solution(mesh):
    placed = (P(None, ("slab", "pulse"), "rx", "rng"), P(), P())
    return jax.shard_map(
        route,
        mesh=mesh,
        in_specs=placed,
        out_specs=P(None, "slab", ("rng", "rx", "pulse")),
        check_vma=False,
    )
```

```python
import functools
import math

import jax
import ml_dtypes
import jax.numpy as jnp
import numpy as np
from jax import lax
from jax.experimental import pallas as pl
from jax.experimental.pallas import tpu as pltpu
from jax.sharding import PartitionSpec as P

RTAPS = 64
CTAPS = 512


half_root = 0.7071067811865476
full_turn = 2.0 * math.pi
SPAN = 256
EDGE = 384
MESH = pl.DeviceIdType.MESH


def extended_2(block, sides, width):
    for axis, dim in sides:
        count = lax.axis_size(axis)
        forward = [(i, i + 1) for i in range(count - 1)]
        backward = [(target, source) for source, target in forward]
        low = lax.ppermute(
            lax.slice_in_dim(block, block.shape[dim] - width, None, axis=dim), axis, forward
        )
        high = lax.ppermute(lax.slice_in_dim(block, 0, width, axis=dim), axis, backward)
        block = jnp.concatenate([low, block, high], axis=dim)
    return block


def swapped(x, axis, distance):
    return lax.ppermute(x, axis, [(i, i ^ 1 << distance) for i in range(lax.axis_size(axis))])


def receiver_taps(channel_ids, tap_count):
    tap_index = jnp.arange(tap_count, dtype=jnp.float32)
    window = 0.5 - 0.5 * jnp.cos(full_turn * (tap_index + 0.5) / tap_count)
    window = window / jnp.sqrt(jnp.sum(window * window))
    channel = channel_ids.astype(jnp.float32)[:, None] + 1.0
    angle = full_turn * channel * (tap_index - tap_count // 2) / (4 * tap_count)
    return (
        (window * jnp.cos(angle)).astype(jnp.bfloat16),
        (window * jnp.sin(angle)).astype(jnp.bfloat16),
    )


def chirp_taps(tap_count):
    offset = jnp.arange(tap_count, dtype=jnp.int32) - tap_count // 2
    phase_step = jnp.mod(offset * offset, 2 * tap_count).astype(jnp.float32)
    angle = math.pi * phase_step / tap_count
    scale = 1.0 / math.sqrt(tap_count)
    return (
        (jnp.cos(angle) * scale).astype(jnp.bfloat16),
        (-jnp.sin(angle) * scale).astype(jnp.bfloat16),
    )


def steering(beam_angle, receivers):
    channel = jnp.arange(receivers, dtype=jnp.int32)
    turns = jnp.mod(beam_angle[:, None] * channel[None, :], 1024).astype(jnp.float32)
    angle = full_turn * turns / 1024.0
    scale = 1.0 / math.sqrt(receivers)
    return (
        (jnp.cos(angle) * scale).astype(jnp.bfloat16),
        (-jnp.sin(angle) * scale).astype(jnp.bfloat16),
    )


def interp_matrices(codes, beam_count):
    shifted = codes // 4 - 1
    fraction = jnp.mod(codes, 4).astype(jnp.float32) / 4.0
    weights = (
        -fraction * (fraction - 1.0) * (fraction - 2.0) / 6.0,
        (fraction + 1.0) * (fraction - 1.0) * (fraction - 2.0) / 2.0,
        -(fraction + 1.0) * fraction * (fraction - 2.0) / 2.0,
        (fraction + 1.0) * fraction * (fraction - 1.0) / 6.0,
    )
    columns = jnp.arange(beam_count, dtype=jnp.int32)
    matrices = jnp.zeros(codes.shape + (beam_count,), jnp.float32)
    for tap_index in range(4):
        target = jnp.mod(columns + shifted + tap_index - 1, beam_count)
        matrices = matrices + weights[tap_index][..., None] * (target[..., None] == columns).astype(
            jnp.float32
        )
    return matrices


def phases(node_ids, positions, beam_angle, side):
    base = jnp.mod(beam_angle[:, None] * (positions[None, :] + 1), 1024)
    factor = 2 * node_ids + side + 1
    turns = jnp.mod(base[:, None, :] * factor[None, :, None], 1024).astype(jnp.float32)
    angle = full_turn * turns / 1024.0
    return (jnp.cos(angle), jnp.sin(angle))


def side_term(picture, matrices, cosine, sine):
    moved = jnp.einsum("gqa,cagr->cqgr", matrices, picture, precision=lax.Precision.HIGHEST)
    return (cosine * moved[0] - sine * moved[1], sine * moved[0] + cosine * moved[1])


def merge_pair(left_image, right_image, node_ids, positions, beam_angle, interp_table):
    matrices = interp_matrices(
        lax.dynamic_slice_in_dim(interp_table, node_ids[0], node_ids.shape[0]), left_image.shape[1]
    )
    left_cos, left_sin = phases(node_ids, positions, beam_angle, 0)
    right_cos, right_sin = phases(node_ids, positions, beam_angle, 1)
    left_re, left_im = side_term(left_image, matrices[:, 0], left_cos, left_sin)
    right_re, right_im = side_term(right_image, matrices[:, 1], right_cos, right_sin)
    return jnp.stack([(left_re + right_re) * half_root, (left_im + right_im) * half_root])


def toeplitz_blocks(taps_re, taps_im):
    tap_count = taps_re.shape[-1]
    leading = taps_re.shape[:-1]

    def lay_out(taps):
        padded = jnp.concatenate([taps, jnp.zeros(leading + (tap_count + 1,), taps.dtype)], axis=-1)
        tiled = jnp.tile(padded, (1,) * len(leading) + (tap_count,))
        banded = tiled[..., : 2 * tap_count * tap_count].reshape(
            leading + (tap_count, 2 * tap_count)
        )
        return jnp.swapaxes(banded, -1, -2)

    real_band = lay_out(taps_re)
    imag_band = lay_out(taps_im)
    upper = jnp.concatenate([real_band, imag_band], axis=-1)
    lower = jnp.concatenate([-imag_band, real_band], axis=-1)
    return jnp.concatenate([upper, lower], axis=-2)


def block_filter(extended, matrices, tap_count, per_channel):
    pulses, channels, length = extended.shape[1:]
    blocks = length // tap_count - 1
    pieces = extended.reshape(2, pulses, channels, blocks + 1, tap_count)
    windows = jnp.concatenate([pieces[:, :, :, :-1], pieces[:, :, :, 1:]], axis=4)
    windows = jnp.transpose(windows, (1, 2, 3, 0, 4)).reshape(
        pulses, channels, blocks, 4 * tap_count
    )
    if per_channel:
        output = jnp.einsum("pcnw,cwo->pcno", windows, matrices, preferred_element_type=jnp.float32)
    else:
        output = jnp.einsum("pcnw,wo->pcno", windows, matrices, preferred_element_type=jnp.float32)
    output = output.reshape(pulses, channels, blocks, 2, tap_count)
    return jnp.transpose(output, (3, 0, 1, 2, 4)).reshape(2, pulses, channels, blocks * tap_count)


def local(echoes, beam_angle, interp_table):
    rx_count = lax.axis_size("rx")
    pulse_count = lax.axis_size("pulse")
    rng_place = lax.axis_index("rng")
    rx_place = lax.axis_index("rx")
    pulse_place = lax.axis_index("pulse")
    pulses, channels, length = echoes.shape[1:]
    beam_count = beam_angle.shape[0]
    receivers = channels * rx_count
    channel_ids = rx_place * channels + jnp.arange(channels, dtype=jnp.int32)
    rx_re, rx_im = receiver_taps(channel_ids, RTAPS)
    rx_bands = toeplitz_blocks(rx_re, rx_im)
    chirp_re, chirp_im = chirp_taps(CTAPS)
    chirp_band = toeplitz_blocks(chirp_re, chirp_im)
    extended = extended_2(echoes, (("rng", 3),), RTAPS // 2)
    filtered = block_filter(extended, rx_bands, RTAPS, True).astype(jnp.bfloat16)
    filtered = extended_2(filtered, (("rng", 3),), CTAPS // 2)
    compressed = block_filter(filtered, chirp_band, CTAPS, False).astype(jnp.bfloat16)
    steering_real, steering_imaginary = steering(beam_angle, receivers)
    steer_matrix = jnp.concatenate(
        [
            jnp.concatenate([steering_real, -steering_imaginary], axis=1),
            jnp.concatenate([steering_imaginary, steering_real], axis=1),
        ],
        axis=0,
    )
    arrived = lax.all_to_all(compressed, "rx", split_axis=3, concat_axis=2, tiled=True)
    item_count, recv_count, owned_cols = arrived.shape[1:]
    stacked = jnp.transpose(arrived, (0, 2, 1, 3)).reshape(2 * recv_count, item_count * owned_cols)
    formed = jnp.dot(steer_matrix, stacked, preferred_element_type=jnp.float32)
    picture = formed.reshape(2, beam_count, item_count, owned_cols)
    owned_width = length // rx_count
    positions = (
        rng_place * length + rx_place * owned_width + jnp.arange(owned_width, dtype=jnp.int32)
    )
    for level in range(pulses.bit_length() - 1):
        groups_now = pulses >> level + 1
        node_ids = (pulse_count + pulse_place) * groups_now + jnp.arange(
            groups_now, dtype=jnp.int32
        )
        paired = picture.reshape(2, beam_count, groups_now, 2, owned_width)
        picture = merge_pair(
            paired[:, :, :, 0], paired[:, :, :, 1], node_ids, positions, beam_angle, interp_table
        )
    picture = picture[:, :, 0]
    cross_levels = pulse_count.bit_length() - 1
    piece_width = owned_width // pulse_count
    pieces = picture.reshape(2, beam_count, pulse_count, piece_width)
    spots = positions.reshape(pulse_count, piece_width)
    for level in range(cross_levels):
        parity = jnp.right_shift(pulse_place, level) & 1
        count_now = pieces.shape[2]
        paired = pieces.reshape(2, beam_count, count_now // 2, 2, piece_width)
        kept_half = lax.dynamic_index_in_dim(paired, parity, 3, keepdims=False)
        sent_half = lax.dynamic_index_in_dim(paired, 1 - parity, 3, keepdims=False)
        partner = swapped(sent_half, "pulse", level)
        spot_pairs = spots.reshape(count_now // 2, 2, piece_width)
        spots = lax.dynamic_index_in_dim(spot_pairs, parity, 1, keepdims=False)
        own_part = kept_half.reshape(2, beam_count, -1)
        other_part = partner.reshape(2, beam_count, -1)
        left_image = jnp.where(parity == 0, own_part, other_part)
        right_image = jnp.where(parity == 0, other_part, own_part)
        combine_node_ids = jnp.reshape(
            (pulse_count >> level + 1) + jnp.right_shift(pulse_place, level + 1), (1,)
        )
        merged = merge_pair(
            left_image[:, :, None],
            right_image[:, :, None],
            combine_node_ids,
            spots.reshape(-1),
            beam_angle,
            interp_table,
        )
        flat = merged[:, :, 0]
        pieces = flat.reshape(2, beam_count, count_now // 2, piece_width)
    picture = pieces.reshape(2, beam_count, piece_width)
    return picture


def receiver_bands(receivers):
    t = np.arange(RTAPS, dtype=np.float64)
    window = 0.5 - 0.5 * np.cos(full_turn * (t + 0.5) / RTAPS)
    window = window / np.sqrt(np.sum(window * window))
    angle = full_turn * np.arange(1, receivers + 1)[:, None] * (t - RTAPS // 2) / (4 * RTAPS)
    lane = np.arange(128)
    near = np.where(lane < 64, np.where(lane < 32, 256 + lane, 64 + lane), np.where(lane < 96, 192 + lane, lane))
    row = np.concatenate([128 + lane, near])
    lag = row[:, None] - np.arange(128)[None, :] - (128 - RTAPS // 2)
    pairs = banded(window * np.cos(angle), window * np.sin(angle), lag, RTAPS, 128)
    middle = ((lane >= 32) & (lane < 96))[None, :, None]
    edges = np.where(middle, pairs[:, 384:], pairs[:, 256:384])
    return np.concatenate([pairs[:, :256], edges], axis=1)


def chirp_bands():
    t = np.arange(CTAPS) - CTAPS // 2
    angle = math.pi * ((t * t) % (2 * CTAPS)) / CTAPS
    scale = 1.0 / math.sqrt(CTAPS)
    lag = np.arange(CTAPS + 128)[:, None] - np.arange(128)[None, :]
    return banded(np.cos(angle)[None] * scale, -np.sin(angle)[None] * scale, lag, CTAPS, 128)[0]


def banded(taps_re, taps_im, lag, count, group):
    inside = (lag >= 0) & (lag < count)
    spot = np.clip(lag, 0, count - 1)
    re = np.where(inside, taps_re[:, spot], 0.0)
    im = np.where(inside, taps_im[:, spot], 0.0)
    channels, rows, cols = re.shape
    upper = np.concatenate([re, im], axis=2).reshape(channels, rows // group, 1, group, 2 * cols)
    lower = np.concatenate([-im, re], axis=2).reshape(channels, rows // group, 1, group, 2 * cols)
    both = np.concatenate([upper, lower], axis=2)
    return both.reshape(channels, 2 * rows, 2 * cols).astype(np.float32).astype(ml_dtypes.bfloat16)


def turn(k, scale):
    shifted = k + 128
    quadrant = jnp.bitwise_and(jnp.right_shift(shifted, 8), 3)
    y = (jnp.bitwise_and(shifted, 255) - 128).astype(jnp.float32) * (full_turn / 1024.0)
    z = y * y
    sine = y * (1.0 + z * (-1 / 6 + z * (1 / 120 + z * (-1 / 5040 + z * (1 / 362880)))))
    cosine = 1.0 + z * (-0.5 + z * (1 / 24 + z * (-1 / 720 + z * (1 / 40320))))
    odd = jnp.bitwise_and(quadrant, 1) == 1
    c = jnp.where(odd, sine, cosine)
    s = jnp.where(odd, cosine, sine)
    c = jnp.where(jnp.bitwise_and(quadrant + 1, 2) == 2, -c, c)
    s = jnp.where(quadrant >= 2, -s, s)
    return c * scale, s * scale


def upright(row, size, folded):
    across = lax.broadcasted_iota(jnp.int32, (size, size), 1)
    down = lax.broadcasted_iota(jnp.int32, (size, size), 0)
    if folded:
        down = 8 * jnp.bitwise_and(down, 7) + jnp.right_shift(down, 3)
    spread = jnp.where(across == down, jnp.broadcast_to(row.astype(jnp.float32), (size, size)), 0.0)
    return jnp.sum(spread, axis=1, keepdims=True)


def refold(x):
    return jnp.swapaxes(x.reshape(8, 8, x.shape[1]), 0, 1).reshape(x.shape)


def shift_and_weights(codes):
    shift = jnp.right_shift(codes, 2) - 1
    f = jnp.bitwise_and(codes, 3).astype(jnp.float32) * 0.25
    weights = (
        -f * (f - 1.0) * (f - 2.0) * (1 / 6),
        (f + 1.0) * (f - 1.0) * (f - 2.0) * 0.5,
        -(f + 1.0) * f * (f - 2.0) * 0.5,
        (f + 1.0) * f * (f - 1.0) * (1 / 6),
    )
    return shift, weights


def tap_rows(codes):
    shift, weights = shift_and_weights(codes)
    spread = []
    for d in range(-2, 4):
        row = jnp.zeros(codes.shape, jnp.float32)
        for k in range(4):
            row = jnp.where(shift == d - k + 1, weights[k], row)
        spread.append(row)
    return spread


def interp_pair(codes, size):
    shift, weights = shift_and_weights(codes)
    wide = (size, 2 * size)
    first = lax.broadcasted_iota(jnp.int32, codes.shape, 1) + shift - 1
    gap = lax.broadcasted_iota(jnp.int32, wide, 0) - jnp.broadcast_to(first, wide)
    gap = jnp.bitwise_and(gap, size - 1)
    out = jnp.zeros(wide, jnp.float32)
    for k in range(4):
        out = jnp.where(gap == k, jnp.broadcast_to(weights[k], wide), out)
    turned = jnp.transpose(out)
    halves = [refold(turned[:size]), refold(turned[size:])]
    return jnp.concatenate(halves, axis=0).astype(jnp.bfloat16)


def times(a, b):
    return a[0] * b[0] - a[1] * b[1], a[0] * b[1] + a[1] * b[0]


def times_conj(a, b):
    return a[0] * b[0] + a[1] * b[1], a[1] * b[0] - a[0] * b[1]


def square(a):
    return (a[0] - a[1]) * (a[0] + a[1]), 2.0 * a[0] * a[1]


def choose(flag, a, b):
    return jnp.where(flag, a[0], b[0]), jnp.where(flag, a[1], b[1])


def powers(one, me):
    two = square(one)
    three = times(two, one)
    four = square(two)
    outer = choose(me < 2, three, four)
    more = choose(me < 2, choose(me == 0, one, two), choose(me == 2, three, four))
    inner = times(four, more)
    second = times_conj(square(inner), one)
    first = [times_conj(square(second), one)]
    first.append(times(first[0], two))
    leaf = [times_conj(square(first[0]), one)]
    for _ in range(3):
        leaf.append(times(leaf[-1], two))
    return [one] + leaf + first + [second, inner, outer]


def focus_kernel(
    pulse_count, ech, ang_hbm, tab_hbm, trx_hbm, chp_hbm, out,
    ang, tab, held, edge, wide, filt, trx, chp, phase, form, coef,
    offered, both, sent, got, final,
    near_ok, far_ok, near_sem, halo_sem, offer_send, offer_recv, piece_send, piece_recv,
):
    rx, rng, me = lax.axis_index("rx"), lax.axis_index("rng"), lax.axis_index("pulse")
    beams = ang.shape[1]
    rows, length = ech.shape[1:]
    channels = trx.shape[0]
    pulses = rows // channels
    owned = length // 2
    barrier = pltpu.get_barrier_semaphore()
    pl.semaphore_signal(barrier, inc=1, device_id={"rx": 1 - rx, "rng": 1}, device_id_type=MESH)

    @pl.when(rng == 0)
    def _():
        pl.semaphore_signal(barrier, inc=1, device_id={"rng": 1}, device_id_type=MESH)

    tables = [
        pltpu.make_async_copy(ang_hbm, ang, near_sem.at[0]),
        pltpu.make_async_copy(tab_hbm, tab, near_sem.at[1]),
    ]
    echo_in = pltpu.make_async_copy(ech, held, near_sem.at[2])
    chirp_in = pltpu.make_async_copy(chp_hbm, chp, near_sem.at[3])
    bands_in = [
        pltpu.make_async_copy(
            trx_hbm.at[pl.ds(rx * channels + 2 * i, 2)], trx.at[pl.ds(2 * i, 2)], near_sem.at[4 + i]
        )
        for i in range(channels // 2)
    ]
    for copy in [echo_in] + tables + bands_in + [chirp_in]:
        copy.start()
    for step in range(1, pulse_count):
        far = {"pulse": lax.rem(me + step, pulse_count), "rng": 0}
        pl.semaphore_signal(barrier, inc=1, device_id=far, device_id_type=MESH)

    @pl.when(rng == 0)
    def _():
        wide[:, 2] = jnp.zeros((2, rows, 128), wide.dtype)
        filt[:, :512] = jnp.zeros((rows, 512), filt.dtype)

    @pl.when(rng == 1)
    def _():
        wide[:, 3 + length // 128] = jnp.zeros((2, rows, 128), wide.dtype)
        filt[:, 512 + 2 * length :] = jnp.zeros((rows, 512), filt.dtype)

    for copy in tables:
        copy.wait()
    angle = upright(ang[...], beams, False).astype(jnp.int32)
    folded = upright(ang[...], beams, True).astype(jnp.int32)

    echo_in.wait()
    for part in range(2):
        for spot in range(length // 128):
            wide[part, 3 + spot] = held[part, :, 128 * spot : 128 * spot + 128].astype(jnp.float32)

    lane = lax.broadcasted_iota(jnp.int32, (pulses, 128), 1)
    low = lane < 64
    middle = jnp.logical_and(lane >= 32, lane < 96)

    def filter_pair(pair, start, blocks):
        results = []
        for c in (2 * pair, 2 * pair + 1):
            cells = [
                [
                    wide[part, start + j, pl.ds(c, pulses, stride=channels), :]
                    for j in range(blocks + 2)
                ]
                for part in range(2)
            ]
            left = jnp.concatenate(
                [
                    jnp.concatenate(
                        [
                            cells[0][j + 1],
                            cells[1][j + 1],
                            jnp.where(
                                middle,
                                pltpu.roll(jnp.where(low, cells[1][j + 2], cells[1][j]), 64, 1),
                                jnp.where(low, cells[0][j + 2], cells[0][j]),
                            ),
                        ],
                        axis=1,
                    )
                    for j in range(blocks)
                ],
                axis=0,
            ).astype(jnp.bfloat16)
            results.append(jnp.dot(left, trx[c], preferred_element_type=jnp.float32))
        for j in range(blocks):
            filt[2 * pair * pulses : 2 * (pair + 1) * pulses, pl.ds(pl.multiple_of(256 * (start + j), 256), 256)] = (
                jnp.concatenate([r[8 * j : 8 * j + 8] for r in results], axis=0).astype(jnp.bfloat16)
            )


    @pl.when(rng == 1)
    def _():
        pl.semaphore_wait(barrier, 3)
        pl.semaphore_signal(near_ok, inc=1, device_id={"rng": 0}, device_id_type=MESH)

    @pl.when(rng == 0)
    def _():
        pl.semaphore_wait(near_ok, 1)

    halo = pltpu.make_async_remote_copy(
        src_ref=ech.at[:, :, pl.ds(pl.multiple_of((1 - rng) * (length - EDGE), 128), EDGE)],
        dst_ref=edge,
        send_sem=halo_sem.at[0],
        recv_sem=halo_sem.at[1],
        device_id={"rng": 1 - rng},
        device_id_type=MESH,
    )
    halo.start()
    for pair in range(channels // 2):
        bands_in[pair].wait()
        filter_pair(pair, 2 + rng, length // 128 - 1)

    def turn_of(u):
        k = jnp.where(u * (u - 2) == 0, 1, jnp.where(u > 5, 3, jnp.where((u - 3) * (u - 4) == 0, 2, 0)))
        h = jnp.where(u * (u - 4) * (u - 5) * (u - 7) == 0, 1, 0)
        return k, h

    def related(k):
        return jnp.where(
            k == 0,
            lax.rem(me + 2, 4),
            jnp.where(k == 1, 3 - me, jnp.where(k == 2, me + 1 - 2 * lax.rem(me, 2), me)),
        )

    def spot_of(u):
        k, h = turn_of(u)
        return 2 * related(k) + h

    late = (1 - jnp.abs(rx - rng)) * (1 - jnp.abs(lax.div(me, 2) - rng))

    def compress(half, units):
        left = jnp.concatenate(
            [
                filt[:, pl.ds(pl.multiple_of(2 * owned * half + 256 * spot_of(u), 256), 1280)]
                for u in units
            ],
            axis=0,
        )
        made = jnp.dot(left, chp[...], preferred_element_type=jnp.float32)
        made = [made[rows * n : rows * (n + 1)] for n in range(len(units))]
        return [
            jnp.concatenate([x[:, :128], x[:, 128:]], axis=0).astype(jnp.bfloat16) for x in made
        ]

    def offer(u):
        return pltpu.make_async_remote_copy(
            src_ref=offered.at[u],
            dst_ref=both.at[u, rx],
            send_sem=offer_send.at[u],
            recv_sem=offer_recv.at[u],
            device_id={"rx": 1 - rx},
            device_id_type=MESH,
        )

    def give(units):
        for u, block in zip(units, compress(1 - rx, units)):
            offered[u] = block
        for u in units:
            offer(u).start()

    chirp_in.wait()

    @pl.when(late == 0)
    def _():
        give([0, 1])


    halo.wait_recv()
    place = (1 - rng) * (length // 128 + 3)
    for part in range(2):
        for spot in range(3):
            wide[part, place + spot] = edge[part, :, 128 * spot : 128 * spot + 128].astype(jnp.float32)
    for pair in range(channels // 2):
        filter_pair(pair, (1 - rng) * (length // 128 + 1), 3)

    @pl.when(late == 1)
    def _():
        give([0, 1])

    give([2, 3])
    give([4, 5, 6, 7])

    node = [(pulse_count + me) * (pulses >> k + 1) for k in range(3)]
    nodes = [node[k] + i for k in range(3) for i in range(pulses >> k + 1)]
    codes = [tab[pl.ds(2 * n + side, 1), :] for n in nodes for side in range(2)]
    codes += [tab[pl.ds((pulse_count >> k) + jnp.right_shift(me, k), 1), :] for k in range(2)]
    mixers = [
        interp_pair(jnp.concatenate(codes[2 * i : 2 * i + 2], axis=1), beams) for i in range(4)
    ]
    spread = tap_rows(jnp.concatenate(codes[8:], axis=0))
    for m in range(8):
        for d in range(6):
            coef[6 * m + d] = jnp.broadcast_to(
                upright(spread[d][m : m + 1], beams, True), (beams, 128)
            )
    size = (beams, 2 * 2 * channels * pulses)
    column = lax.broadcasted_iota(jnp.int32, size, 1)
    local_channel = jnp.bitwise_and(jnp.right_shift(column, 3), channels - 1)
    receiver = local_channel + channels * jnp.right_shift(column, 7)
    cosine, sine = turn(jnp.bitwise_and(angle * receiver, 1023), 0.25)
    imag = jnp.bitwise_and(jnp.right_shift(column, 6), 1) == 1
    steer = jnp.where(imag, -sine, cosine).astype(jnp.bfloat16)
    lane_pulse = jnp.bitwise_and(column, pulses - 1)
    for i in range(pulses // 2):
        mixed = jnp.dot(mixers[i], steer, preferred_element_type=jnp.float32)
        for side in range(2):
            p = 2 * i + side
            form[p * beams : (p + 1) * beams, :] = jnp.where(
                lane_pulse == p, mixed[side * beams : (side + 1) * beams], 0.0
            ).astype(jnp.bfloat16)

    made = compress(rx, list(range(2 * pulse_count)))
    for u in range(2 * pulse_count):
        both[u, rx] = made[u]

    along = (rng * length + rx * owned) + 1 + lax.broadcasted_iota(jnp.int32, (beams, 128), 1)
    fields = powers(turn(jnp.bitwise_and(folded * along, 1023), 1.0), me)
    steps = powers(
        turn(jnp.bitwise_and(jnp.broadcast_to(folded, (beams, 128)) * 128, 1023), 1.0), me
    )
    for k in range(len(fields)):
        field = fields[k] if k == 0 else (fields[k][0] * half_root, fields[k][1] * half_root)
        for spot in range(2 * pulse_count):
            if spot:
                field = times(field, steps[k])
            phase[spot, k, 0], phase[spot, k, 1] = field

    def piece(u):
        k = jnp.where(u == 0, 2, turn_of(u)[0])
        return pltpu.make_async_remote_copy(
            src_ref=sent.at[u],
            dst_ref=got.at[u],
            send_sem=piece_send.at[u],
            recv_sem=piece_recv.at[u],
            device_id={"pulse": related(k)},
            device_id_type=MESH,
        )

    def unit(u, carry):
        spot = spot_of(u)
        offer(u).wait_recv()
        blocks_of = []
        for side in range(2):
            re, im = both[u, side, :rows], both[u, side, rows:]
            blocks_of.append(jnp.concatenate([re, im], axis=1))
            blocks_of.append(jnp.concatenate([-im, re], axis=1))
        right = jnp.concatenate(blocks_of, axis=0)

        def spun(field, x):
            return times((phase[spot, field, 0], phase[spot, field, 1]), x)

        def joined(field, left_x, right_x):
            moved = spun(0, right_x)
            return spun(field, (left_x[0] + moved[0], left_x[1] + moved[1]))

        def blended(m, x):
            results = []
            for part in range(2):
                rows_of = [x[part][8 * v : 8 * v + 8] for v in range(beams // 8)]
                lined = [pltpu.roll(v, 1, 0) for v in rows_of[-2:]] + rows_of
                lined += [pltpu.roll(v, 7, 0) for v in rows_of[:3]]
                sums = []
                for v in range(beams // 8):
                    terms = [coef[6 * m + d, 8 * v : 8 * v + 8] * lined[v + d] for d in range(6)]
                    sums.append(((terms[0] + terms[1]) + (terms[2] + terms[3])) + (terms[4] + terms[5]))
                results.append(jnp.concatenate(sums, axis=0))
            return results

        images = []
        for g in range(pulses // 2):
            x = jnp.dot(
                form[2 * g * beams : 2 * (g + 1) * beams, :], right, preferred_element_type=jnp.float32
            )
            left_x, right_x = (x[:beams, :128], x[:beams, 128:]), (x[beams:, :128], x[beams:, 128:])
            images.append(blended(g, joined(1 + g, left_x, right_x)))
        images = [joined(5 + g, images[2 * g], images[2 * g + 1]) for g in range(2)]
        picture = joined(7, blended(4, images[0]), blended(5, images[1]))
        picture = spun(8, blended(6, picture))
        re, im = spun(9, blended(7, picture))

        @pl.when(u < 5)
        def _():
            sent[u, 0] = re.astype(jnp.bfloat16)
            sent[u, 1] = im.astype(jnp.bfloat16)
            piece(u).start()

        @pl.when(u == 5)
        def _():
            piece(0).wait_recv()
            sent[5, 0] = (re + got[0, 0].astype(jnp.float32)).astype(jnp.bfloat16)
            sent[5, 1] = (im + got[0, 1].astype(jnp.float32)).astype(jnp.bfloat16)
            piece(5).start()

        @pl.when(u > 5)
        def _():
            final[u - 6, 0] = re
            final[u - 6, 1] = im

        return carry


    @pl.when(rng == 0)
    def _():
        pl.semaphore_wait(barrier, 2 * (pulse_count - 1))
        pl.semaphore_signal(far_ok, inc=1, device_id={"rng": 1}, device_id_type=MESH)

    @pl.when(rng == 1)
    def _():
        pl.semaphore_wait(far_ok, 1)

    lax.fori_loop(0, 2 * pulse_count, unit, 0)
    halo.wait_send()
    for u in range(2 * pulse_count):
        offer(u).wait_send()
    for u in range(5):
        piece(u).wait_send()
    for h, parts in enumerate(((2, 3, 1), (4, 5))):
        total = [final[h, part] for part in range(2)]
        for u in parts:
            piece(u).wait_recv()
            for part in range(2):
                total[part] = total[part] + got[u, part].astype(jnp.float32)
        for part in range(2):
            out[part, :, 128 * h : 128 * h + 128] = refold(total[part])
    piece(5).wait_send()


def fused(echoes, beam_angle, interp_table, pulse_count):
    pulses, channels, length = echoes.shape[1:]
    beams = beam_angle.shape[0]
    receivers = 2 * channels
    rows = pulses * channels
    bands = jnp.asarray(receiver_bands(receivers))
    chirps = jnp.asarray(chirp_bands())
    table = interp_table.reshape(-1, beams)
    bf16, f32 = jnp.bfloat16, jnp.float32
    away = pl.BlockSpec(memory_space=pltpu.HBM)
    operands = (echoes.reshape(2, rows, length), beam_angle.reshape(1, beams), table, bands, chirps)
    return pl.pallas_call(
        functools.partial(focus_kernel, pulse_count),
        out_shape=pltpu.VMEM((2, beams, SPAN), f32),
        in_specs=[away] * 5,
        out_specs=pl.BlockSpec(memory_space=pltpu.VMEM),
        scratch_shapes=[
            pltpu.VMEM((1, beams), jnp.int32),
            pltpu.VMEM(table.shape, jnp.int32),
            pltpu.VMEM((2, rows, length), bf16),
            pltpu.VMEM((2, rows, EDGE), bf16),
            pltpu.VMEM((2, length // 128 + 6, rows, 128), f32),
            pltpu.VMEM((rows, 2 * length + 1024), bf16),
            pltpu.VMEM((channels,) + bands.shape[1:], bf16),
            pltpu.VMEM(chirps.shape, bf16),
            pltpu.VMEM((2 * pulse_count, 10, 2, beams, 128), f32),
            pltpu.VMEM((pulses * beams, 2 * receivers * pulses), bf16),
            pltpu.VMEM((48, beams, 128), f32),
            pltpu.VMEM((2 * pulse_count, 2 * rows, 128), bf16),
            pltpu.VMEM((2 * pulse_count, 2, 2 * rows, 128), bf16),
            pltpu.VMEM((6, 2, beams, 128), bf16),
            pltpu.VMEM((6, 2, beams, 128), bf16),
            pltpu.VMEM((2, 2, beams, 128), f32),
            pltpu.SemaphoreType.REGULAR,
            pltpu.SemaphoreType.REGULAR,
            pltpu.SemaphoreType.DMA((8,)),
            pltpu.SemaphoreType.DMA((2,)),
            pltpu.SemaphoreType.DMA((2 * pulse_count,)),
            pltpu.SemaphoreType.DMA((2 * pulse_count,)),
            pltpu.SemaphoreType.DMA((2 * pulse_count - 2,)),
            pltpu.SemaphoreType.DMA((2 * pulse_count - 2,)),
        ],
        compiler_params=pltpu.CompilerParams(
            collective_id=0, has_side_effects=True, vmem_limit_bytes=50 << 20
        ),
    )(*[pltpu.with_memory_space_constraint(x, pltpu.HBM) for x in operands])


def route(echoes, beam_angle, interp_table):
    pulse_count = lax.axis_size("pulse")
    pulses, channels, length = echoes.shape[1:]
    fits = (
        lax.axis_size("rx") == 2
        and lax.axis_size("rng") == 2
        and pulse_count == 4
        and (pulses, channels, length) == (8, 8, 2 * SPAN * pulse_count)
        and beam_angle.shape[0] == 64
    )
    if fits:
        return fused(echoes, beam_angle, interp_table, pulse_count)
    return local(echoes, beam_angle, interp_table)


def solution(mesh):
    placed = (P(None, ("slab", "pulse"), "rx", "rng"), P(), P())
    return jax.shard_map(
        route,
        mesh=mesh,
        in_specs=placed,
        out_specs=P(None, "slab", ("rng", "rx", "pulse")),
        check_vma=False,
    )
```
